32 devices in a mesh: groups: 2 (over x), expert: 4 (over y, core), donor: 4 (over z).
Axes of the slice: x: 2, y: 2, z: 4, core: 2. Of those that a mesh axis runs over, the one named last changes fastest.
Arguments:
- hidden_in: bfloat16 [1024, 4096], P(('groups', 'expert')), parts along dimension 0, may hold values from -6 to 6
- queries: bfloat16 [1024, 4096], P(('groups', 'expert'), 'donor'), parts along dimension 0, may hold values from -39 to 39
- suffix_kv: bfloat16 [1024, 2, 256], P(('groups', 'expert')), parts along dimension 0, may hold values from -12 to 12
- kv_pool: bfloat16 [128, 2, 32, 256], P(('groups', 'expert', 'donor')), parts along dimension 0, may hold values from -12 to 12
- page_table: int32 [8, 16], P('groups'), parts along dimension 0, may hold values from 0 to 63, as said below
- prefix_len: int32 [8], P('groups'), parts along dimension 0, may hold values from 1 to 512, as said below
- out_weight: bfloat16 [4096, 4096], P('donor', 'expert'), may hold values from -0.09375 to 0.09375
- norm_gain: bfloat16 [4096], replicated, may hold values from 0.099609375 to 1.8984375
- expert_ids: int32 [1024, 4], P(('groups', 'expert')), parts along dimension 0, may hold values from 0 to 7, all different within a row; in each aligned block of 128 rows (0 to 127, 128 to 255, ...) at most 80 rows name the same one
- route_probs: float32 [1024, 4], P(('groups', 'expert')), parts along dimension 0, may hold values from 0.05 to 1
- w_gate_up: bfloat16 [16, 4096, 2, 768], P(('expert', 'donor')), may hold values from -0.09375 to 0.09375
- w_down: bfloat16 [16, 768, 4096], P(('expert', 'donor')), may hold values from -0.15625 to 0.15625
Outputs:
- layer_out: bfloat16 [1024, 4096], P(('groups', 'expert'), 'donor'), parts along dimension 0
- head_out: bfloat16 [1024, 4096], P(('groups', 'expert'), 'donor'), parts along dimension 0
The draws below stay inside these ranges and needn't reach their ends.
There are 2 independent parts, one for each index of `groups`. The reference program is written for one: setup_inputs(seed, part) draws one part's arguments, and reference() takes and returns one part's arrays. A program takes and returns all parts, laid end to end along the dimension named above; an argument that names none is the same for every part. Nothing has to cross between parts.
Inputs may be any that keep to these rules, and one draw needn't show every extreme that they name: For every sequence s the values page_table[s, j] // 4 over j are 0 to 15, each once; pages b * 4 to b * 4 + 3 hold one page of every sequence. `prefix_len`: in every draw one sequence has the longest prefix, 512 tokens. `expert_ids`: the 4 experts of a token differ. Among the 128 tokens of one sequence no expert is named by more than 80 tokens, and in some sequence of every draw some expert is named by exactly 80.
All inputs are finite; a program needn't handle non-finite values.
Results may differ from the reference program's by a relative error of at most 0.0056.
Values may be sent and summed in bfloat16 or wider, within the bound.
A program may use at most 128 MiB of HBM per device.

```python
import math
import jax
import jax.numpy as jnp
import numpy as np
from jax import lax

D = 4096
HD = 128
FFE = 1536
HEADS = 32
KVH = 2
PAGE = 32
SUF = 128
SEQS = 4
TOKENS = 512
MAXP = 16
POOL = 64
EXPERTS = 8
SHARES = 2
TOP = 4
CAPS = 80


def shared_draws(key):
    query_key = jax.random.fold_in(key, 101)
    cache_key = jax.random.fold_in(key, 102)
    queries = 0.5 * jnp.clip(jax.random.normal(query_key, (TOKENS, HEADS, HD), jnp.float32), -6.0, 6.0)
    suffix = 2.0 * jnp.clip(jax.random.normal(cache_key, (TOKENS, KVH, 2 * HD), jnp.float32), -6.0, 6.0)
    return (queries.reshape(TOKENS, HEADS * HD), suffix)


def draw_queries(key, part):
    return shared_draws(key)[0].astype(jnp.bfloat16)


def draw_suffix_kv(key, part):
    return shared_draws(key)[1].astype(jnp.bfloat16)


def permute_rows(base_key, rows_count, length):
    keys_all = jax.random.split(base_key, rows_count)
    return jax.vmap(lambda row_key: jax.random.permutation(row_key, length))(keys_all)


def draw_page_table(key, part):
    owners = permute_rows(jax.random.fold_in(key, 201), SEQS, MAXP)
    local_slots = permute_rows(jax.random.fold_in(key, 202), MAXP, SEQS)
    table = owners * SEQS + local_slots[owners, jnp.arange(SEQS)[:, None]]
    return table.astype(jnp.int32)


def draw_prefix_len(key, part):
    lengths = jax.random.randint(jax.random.fold_in(key, 301), (SEQS,), 1, MAXP * PAGE + 1)
    longest = jax.random.randint(jax.random.fold_in(key, 302), (), 0, SEQS)
    return jnp.where(jnp.arange(SEQS) == longest, MAXP * PAGE, lengths).astype(jnp.int32)


def steps_of(rng, dims, pieces, least, top_value):
    def one(dim, shards_of):
        heights = jax.random.uniform(jax.random.fold_in(jax.random.fold_in(rng, 6), dim), (shards_of,), jnp.float32, least / len(pieces), top_value / len(pieces))
        return jnp.repeat(jnp.exp(heights), dims[dim] // shards_of).reshape((-1,) + (1,) * (len(dims) - dim - 1))

    level = one(*pieces[0])
    for cut in pieces[1:]:
        level = level * one(*cut)
    return level


def assign_block(key, own, number, rows, number_of, top, bound, slope):
    sequence = jax.random.permutation(key, number_of)
    packed, common = portions_of(number_of, rows * top, bound, slope, True), portions_of(number_of, rows * top, bound, slope, False)
    places = jnp.arange(number_of)

    def named(sizes, turn):
        used = int((sizes > 0).sum())
        fixed = max(1, used // 4)
        passed = fixed + (places - fixed + turn * (used - fixed)) % max(1, number_of - fixed)
        return jnp.zeros((number_of,), jnp.int32).at[sequence[jnp.where(places < fixed, places, passed)]].set(jnp.asarray(sizes, jnp.int32))

    sizes = jnp.where(number % 4 == 0, named(packed, number // 4), named(common, number - number // 4 - 1))
    mixed = jax.random.permutation(jax.random.fold_in(own, 3), number_of)
    source_of, receiver = mixed[0:number_of // 2 * 2:2], mixed[1:number_of // 2 * 2:2]
    margin = jnp.minimum(sizes[source_of] - 1, bound - sizes[receiver]) // 2
    margin = jnp.where((source_of == sequence[0]) | (receiver == sequence[0]) | (sizes[receiver] == 0), 0, jnp.maximum(margin, 0))
    passed = jax.random.randint(jax.random.fold_in(own, 4), (number_of // 2,), 0, 1 << 20) % (margin + 1)
    sizes = sizes.at[source_of].add(-passed).at[receiver].add(passed)
    items = jnp.searchsorted(jnp.cumsum(sizes), jnp.arange(rows * top), side="right").astype(jnp.int32)
    listing = items.reshape(top, rows).T
    listing = listing[jax.random.permutation(jax.random.fold_in(own, 1), rows)]
    turn = jax.random.randint(jax.random.fold_in(own, 2), (rows, 1), 0, top)
    return jnp.take_along_axis(listing, (jnp.arange(top)[None, :] + turn) % top, axis=1)


def portions_of(count, total, reach, lean, full):
    loads = [(1 << 20) // math.isqrt(grade ** lean) + 1 for grade in range(1, count + 1)]
    largest = reach if full else min(reach, max(-(-total // count), total * loads[0] // sum(loads)))
    least = 1 if total - largest >= count - 1 else 0
    given, surplus = [largest] + [least] * (count - 1), total - largest - least * (count - 1)
    while surplus > 0:
        free = [i for i in range(1, count) if given[i] < largest] or [i for i in range(1, count) if given[i] < reach]
        whole, remaining = sum([loads[i] for i in free]), surplus
        for i in free:
            extra = min(reach - given[i], max(1, remaining * loads[i] // whole), surplus)
            given[i] = given[i] + extra
            surplus = surplus - extra
    return np.array(given)


def bell_draw(key, extent, scale, most, cuts=(), kind=jnp.bfloat16):
    values = scale * jax.random.normal(key, extent, jnp.float32)
    if cuts:
        values = values * steps_of(key, extent, cuts, -0.22, 0.18)
    return jnp.clip(values, -most, most).astype(kind)


def setup_inputs(seed: int = 0, part: int = 0) -> dict:
    splits = jax.random.split(jax.random.key(seed), 13)
    part_splits = jax.random.split(jax.random.fold_in(splits[12], part), 13)
    hidden_in = bell_draw(part_splits[0], (TOKENS, D), 1.0, 6.0, ((0, 4),))
    queries = draw_queries(jax.random.fold_in(jax.random.fold_in(splits[12], part), 71), part)
    suffix_kv = draw_suffix_kv(jax.random.fold_in(jax.random.fold_in(splits[12], part), 71), part)
    kv_pool = bell_draw(part_splits[3], (POOL, KVH, PAGE, 2 * HD), 2.0, 12.0, ((0, 16),))
    page_table = draw_page_table(jax.random.fold_in(jax.random.fold_in(splits[12], part), 71), part)
    prefix_len = draw_prefix_len(jax.random.fold_in(jax.random.fold_in(splits[12], part), 71), part)
    out_weight = bell_draw(splits[6], (HEADS * HD, D), (HEADS * HD) ** -0.5, 0.09375, ((0, 4), (1, 4)))
    norm_gain = jnp.clip(1.0 + 0.18 * jax.random.normal(splits[7], (D,), jnp.float32), 0.099609375, 1.8984375).astype(jnp.bfloat16)
    expert_ids_keys = jax.random.split(jax.random.fold_in(part_splits[8], 1), TOKENS // SUF)
    expert_ids_turns = jax.random.permutation(jax.random.fold_in(part_splits[8], 3), TOKENS // SUF)
    expert_ids = jax.vmap(lambda own, number: assign_block(jax.random.fold_in(part_splits[8], 2), own, number, SUF, EXPERTS, TOP, CAPS, 2))(expert_ids_keys, expert_ids_turns).reshape((TOKENS, TOP))
    route_probs = jnp.clip(jnp.exp(math.log(1.0) - 2.9957323 * jax.random.uniform(part_splits[9], (TOKENS, TOP), jnp.float32) ** steps_of(part_splits[9], (TOKENS, TOP), ((0, 4),), -0.2, 0.2)), 0.05, 1.0)
    w_gate_up = bell_draw(splits[10], (EXPERTS * SHARES, D, 2, FFE // SHARES), D ** -0.5, 0.09375, ((0, 16),))
    w_down = bell_draw(splits[11], (EXPERTS * SHARES, FFE // SHARES, D), FFE ** -0.5, 0.15625, ((0, 16),))
    return {"hidden_in": hidden_in, "queries": queries, "suffix_kv": suffix_kv, "kv_pool": kv_pool, "page_table": page_table, "prefix_len": prefix_len, "out_weight": out_weight, "norm_gain": norm_gain, "expert_ids": expert_ids, "route_probs": route_probs, "w_gate_up": w_gate_up, "w_down": w_down}


def reference(hidden_in, queries, suffix_kv, kv_pool, page_table, prefix_len, out_weight, norm_gain, expert_ids, route_probs, w_gate_up, w_down):
    group_size = HEADS // KVH
    score_scale = HD ** (-0.5)
    prefix_pos = jnp.arange(MAXP * PAGE, dtype=jnp.int32)
    causal = jnp.arange(SUF, dtype=jnp.int32)[:, None] >= jnp.arange(SUF, dtype=jnp.int32)[None, :]

    def attend(pair_index):
        seq_index = (pair_index // KVH).astype(jnp.int32)
        kv_index = (pair_index % KVH).astype(jnp.int32)
        query_rows = lax.dynamic_slice_in_dim(queries, seq_index * SUF, SUF, 0).reshape(SUF, HEADS, HD)
        query_rows = lax.dynamic_slice_in_dim(query_rows, kv_index * group_size, group_size, 1)
        page_rows = jnp.take(kv_pool, page_table[seq_index], axis=0)
        page_rows = lax.dynamic_index_in_dim(page_rows, kv_index, 1, keepdims=False).reshape(MAXP * PAGE, 2 * HD)
        fresh_pair = lax.dynamic_slice_in_dim(suffix_kv, seq_index * SUF, SUF, 0)
        fresh_pair = lax.dynamic_index_in_dim(fresh_pair, kv_index, 1, keepdims=False)
        keys_all = jnp.concatenate([page_rows[:, :HD], fresh_pair[:, :HD]], axis=0)
        vals_all = jnp.concatenate([page_rows[:, HD:], fresh_pair[:, HD:]], axis=0)
        prefix_seen = jnp.broadcast_to(prefix_pos[None, :] < prefix_len[seq_index], (SUF, MAXP * PAGE))
        visible = jnp.concatenate([prefix_seen, causal], axis=1)
        scores = jnp.einsum('thc,kc->thk', query_rows.astype(jnp.float32), keys_all.astype(jnp.float32)) * score_scale
        scores = jnp.where(visible[:, None, :], scores, -jnp.inf)
        row_top = lax.optimization_barrier(jnp.max(scores, axis=2, keepdims=True))
        exp_scores = jnp.where(visible[:, None, :], jnp.exp(scores - row_top), 0.0)
        row_total = lax.optimization_barrier(jnp.sum(exp_scores, axis=2, keepdims=True))
        weights = exp_scores.astype(jnp.bfloat16)
        mixed_heads = jnp.einsum('thk,kc->thc', weights.astype(jnp.float32), vals_all.astype(jnp.float32)) / row_total
        return mixed_heads.astype(jnp.bfloat16)
    per_pair = lax.map(attend, jnp.arange(SEQS * KVH, dtype=jnp.int32))
    head_out = per_pair.reshape(SEQS, KVH, SUF, group_size, HD).transpose(0, 2, 1, 3, 4).reshape(TOKENS, HEADS * HD)
    attn_proj = jnp.dot(head_out, out_weight, preferred_element_type=jnp.float32)
    resid = (hidden_in.astype(jnp.float32) + attn_proj).astype(jnp.bfloat16)
    resid_f = resid.astype(jnp.float32)
    normed = (resid_f * lax.rsqrt(lax.optimization_barrier(jnp.mean(resid_f * resid_f, axis=1, keepdims=True)) + 1e-06) * norm_gain.astype(jnp.float32)).astype(jnp.bfloat16)
    gates = route_probs / lax.optimization_barrier(jnp.sum(route_probs, axis=1, keepdims=True))
    ids_grid = expert_ids.reshape(SEQS, SUF, TOP)
    counts = lax.optimization_barrier(jnp.sum((ids_grid[..., None] == jnp.arange(EXPERTS, dtype=jnp.int32)).astype(jnp.int32), axis=2))
    before = jnp.cumsum(counts, axis=1) - counts
    slot_index = jnp.take_along_axis(before, ids_grid, axis=2)
    within = (ids_grid * CAPS + slot_index).astype(jnp.int32)
    token_rows = jnp.broadcast_to(jnp.arange(TOKENS, dtype=jnp.int32).reshape(SEQS, SUF, 1) + 1, (SEQS, SUF, TOP))
    seq_rows = jnp.broadcast_to(jnp.arange(SEQS, dtype=jnp.int32)[:, None, None], (SEQS, SUF, TOP))
    source = jnp.zeros((SEQS, EXPERTS * CAPS), jnp.int32).at[seq_rows, within].set(token_rows)
    gate_table = jnp.zeros((SEQS, EXPERTS * CAPS), jnp.float32).at[seq_rows, within].set(gates.reshape(SEQS, SUF, TOP))
    normed_pad = jnp.concatenate([jnp.zeros((1, D), jnp.bfloat16), normed], axis=0)
    block_units = FFE // SHARES

    def expert_step(moe_pad, expert_index):
        pick_rows = lax.dynamic_slice_in_dim(source, expert_index * CAPS, CAPS, 1).reshape(-1)
        slot_gates = lax.dynamic_slice_in_dim(gate_table, expert_index * CAPS, CAPS, 1).reshape(-1)
        rows_in = jnp.take(normed_pad, pick_rows, axis=0)
        up_blocks = lax.dynamic_slice_in_dim(w_gate_up, expert_index * SHARES, SHARES, 0)
        up_full = up_blocks.transpose(1, 2, 0, 3).reshape(D, 2 * FFE)
        down_full = lax.dynamic_slice_in_dim(w_down, expert_index * SHARES, SHARES, 0).reshape(SHARES * block_units, D)
        gate_up = jnp.dot(rows_in, up_full, preferred_element_type=jnp.float32)
        activated = (jax.nn.silu(gate_up[:, :FFE]) * gate_up[:, FFE:]).astype(jnp.bfloat16)
        result = jnp.dot(activated, down_full, preferred_element_type=jnp.float32).astype(jnp.bfloat16)
        moe_pad = moe_pad.at[pick_rows].add(result.astype(jnp.float32) * slot_gates[:, None])
        return (moe_pad, None)
    moe_pad, unused = lax.scan(expert_step, jnp.zeros((TOKENS + 1, D), jnp.float32), jnp.arange(EXPERTS, dtype=jnp.int32))
    layer_out = (resid_f + moe_pad[1:]).astype(jnp.bfloat16)
    return (layer_out, head_out)
```

```python
import functools
import math

import jax
import jax.numpy as jnp
from jax import lax
from jax.experimental import pallas as pl
from jax.experimental.pallas import tpu as pltpu
from jax.sharding import PartitionSpec as P

MESH = pl.DeviceIdType.MESH
VMEM_BYTES = 60 * 1024 * 1024
PIECE = 64


def place():
    expert = lax.axis_index("expert")
    return expert // 2, lax.rem(expert, 2), lax.axis_index("donor")


def send(src, dst, sends, recvs, slot, **where):
    return pltpu.make_async_remote_copy(
        src_ref=src,
        dst_ref=dst,
        send_sem=sends.at[slot],
        recv_sem=recvs.at[slot],
        device_id=where,
        device_id_type=MESH,
    )


def greet(chips, donors):
    row, core, donor = place()
    barrier = pltpu.get_barrier_semaphore()
    pl.semaphore_signal(
        barrier, inc=1, device_id={"expert": row * 2 + 1 - core}, device_id_type=MESH
    )
    for step in range(1, chips):
        other = lax.rem(row + step, chips) * 2 + core
        pl.semaphore_signal(barrier, inc=1, device_id={"expert": other}, device_id_type=MESH)
    for step in range(1, donors):
        other = lax.rem(donor + step, donors)
        pl.semaphore_signal(barrier, inc=1, device_id={"donor": other}, device_id_type=MESH)
    pl.semaphore_wait(barrier, chips + donors - 1)


def far_first(donors):
    return sorted(range(1, donors), key=lambda k: (-min(k, donors - k), k))


def gather_kernel(
    chips,
    donors,
    heads_ref,
    out_ref,
    hidden_ref,
    full_ref,
    terms_ref,
    terms_in,
    block_ref,
    own_sem,
    t_send,
    t_recv,
    z_send,
    z_recv,
    y_send,
    y_recv,
    c_send,
    c_recv,
):
    row, core, donor = place()
    rows, cols = block_ref.shape
    greet(chips, donors)
    strip = 16

    def project(step_z, slot):
        top = pl.multiple_of(lax.rem(donor + step_z, donors) * rows, rows)
        terms_ref[slot] = jnp.dot(
            heads_ref[pl.ds(top, rows), :], out_ref[...], preferred_element_type=jnp.float32
        ).astype(terms_ref.dtype)

    term_copies = {}
    for step in far_first(donors):
        project(step, step)
        copy = send(
            terms_ref.at[step],
            terms_in.at[step - 1],
            t_send,
            t_recv,
            step - 1,
            donor=lax.rem(donor + step, donors),
        )
        copy.start()
        term_copies[step] = copy
    project(0, 0)
    for step in far_first(donors):
        term_copies[step].wait_recv()

    def add(index, carry):
        at = pl.ds(pl.multiple_of(index * strip, strip), strip)
        value = terms_ref[0, at, :].astype(jnp.float32)
        for step in range(1, donors):
            value = value + terms_in[step - 1, at, :].astype(jnp.float32)
        value = value + hidden_ref[at, :].astype(jnp.float32)
        block_ref[at, :] = value.astype(block_ref.dtype)
        return carry

    lax.fori_loop(0, rows // strip, add, 0)

    def slot_of(donor_from, row_from, core_from):
        top = pl.multiple_of(donor_from * rows, rows)
        left = pl.multiple_of((row_from * 2 + core_from) * cols, cols)
        return full_ref.at[pl.ds(top, rows), pl.ds(left, cols)]

    own = pltpu.make_async_copy(block_ref, slot_of(donor, row, core), own_sem)
    own.start()
    started = []

    def along_y(src, step_z, donor_from):
        for step in range(1, chips):
            copy = send(
                src,
                slot_of(donor_from, row, core),
                y_send,
                y_recv,
                step_z * (chips - 1) + step - 1,
                expert=lax.rem(row + step, chips) * 2 + core,
            )
            copy.start()
            started.append(copy)

    def beside(src, step_z, step_y, donor_from, row_from):
        copy = send(
            src,
            slot_of(donor_from, row_from, core),
            c_send,
            c_recv,
            step_z * chips + step_y,
            expert=row * 2 + 1 - core,
        )
        copy.start()
        started.append(copy)

    along_y(block_ref, 0, donor)
    z_copies = {}
    near_first = far_first(donors)[::-1]
    for step in near_first:
        copy = send(
            block_ref,
            slot_of(donor, row, core),
            z_send,
            z_recv,
            step - 1,
            donor=lax.rem(donor + step, donors),
        )
        copy.start()
        z_copies[step] = copy
    beside(block_ref, 0, 0, donor, row)

    def take_y(step_z, donor_from):
        for step in range(1, chips):
            row_from = lax.rem(row + chips - step, chips)
            there = slot_of(donor_from, row_from, core)
            send(
                there,
                there,
                y_send,
                y_recv,
                step_z * (chips - 1) + step - 1,
                expert=row_from * 2 + core,
            ).wait_recv()
            beside(there, step_z, step, donor_from, row_from)

    for step in near_first:
        donor_from = lax.rem(donor + donors - step, donors)
        there = slot_of(donor_from, row, core)
        send(there, there, z_send, z_recv, step - 1, donor=donor_from).wait_recv()
        along_y(there, step, donor_from)
        beside(there, step, 0, donor_from, row)
    for step in [0] + near_first:
        take_y(step, lax.rem(donor + donors - step, donors))
    for step_z in range(donors):
        donor_from = lax.rem(donor + donors - step_z, donors)
        for step_y in range(chips):
            row_from = lax.rem(row + chips - step_y, chips)
            there = slot_of(donor_from, row_from, 1 - core)
            send(
                there, there, c_send, c_recv, step_z * chips + step_y, expert=row * 2 + 1 - core
            ).wait_recv()
    own.wait()
    for copy in list(term_copies.values()) + list(z_copies.values()) + started:
        copy.wait_send()


def gather_blocks(heads, out_weight, block, chips, donors):
    rows, cols = block.shape
    dma = pltpu.SemaphoreType.DMA
    return pl.pallas_call(
        functools.partial(gather_kernel, chips, donors),
        out_shape=jax.ShapeDtypeStruct((rows * donors, cols * chips * 2), block.dtype),
        in_specs=[pl.BlockSpec(memory_space=pltpu.VMEM)] * 3,
        out_specs=pl.BlockSpec(memory_space=pltpu.VMEM),
        scratch_shapes=[
            pltpu.VMEM((donors, rows, cols), block.dtype),
            pltpu.VMEM((donors - 1, rows, cols), block.dtype),
            pltpu.VMEM((rows, cols), block.dtype),
            dma,
            dma((donors - 1,)),
            dma((donors - 1,)),
            dma((donors - 1,)),
            dma((donors - 1,)),
            dma((donors * (chips - 1),)),
            dma((donors * (chips - 1),)),
            dma((donors * chips,)),
            dma((donors * chips,)),
        ],
        compiler_params=pltpu.CompilerParams(collective_id=1, has_side_effects=True),
        name="gather_blocks",
    )(heads, out_weight, block)


def reduce_kernel(
    chips,
    donors,
    act_ref,
    down_ref,
    total_ref,
    part_ref,
    c_in,
    y_out,
    y_in,
    z_out,
    z_in,
    c_send,
    c_recv,
    y_send,
    y_recv,
    z_send,
    z_recv,
):
    row, core, donor = place()
    rows, cols = total_ref.shape
    greet(chips, donors)
    order = far_first(donors) + [0]
    strip = 16

    def tile(row_to, core_to, step_z):
        top = pl.multiple_of((row_to * 2 + core_to) * rows, rows)
        left = pl.multiple_of(lax.rem(donor + step_z, donors) * cols, cols)
        return part_ref.at[pl.ds(top, rows), pl.ds(left, cols)]

    def add(out, *terms):
        def body(index, carry):
            at = pl.ds(pl.multiple_of(index * strip, strip), strip)
            value = terms[0][at, :].astype(jnp.float32)
            for term in terms[1:]:
                value = value + term[at, :].astype(jnp.float32)
            out[at, :] = value.astype(out.dtype)
            return carry

        lax.fori_loop(0, rows // strip, body, 0)

    started = []
    arrivals = {}

    def multiply(step_z):
        left = pl.multiple_of(lax.rem(donor + step_z, donors) * cols, cols)

        def body(index, carry):
            at = pl.ds(pl.multiple_of(index * rows, rows), rows)
            part_ref[at, pl.ds(left, cols)] = jnp.dot(
                act_ref[at, :],
                down_ref[:, pl.ds(left, cols)],
                preferred_element_type=jnp.float32,
            ).astype(part_ref.dtype)
            return carry

        lax.fori_loop(0, chips * 2, body, 0)

    def beside(step_z):
        for step_y in range(chips - 1, -1, -1):
            slot = step_z * chips + step_y
            copy = send(
                tile(lax.rem(row + step_y, chips), 1 - core, step_z),
                c_in.at[slot],
                c_send,
                c_recv,
                slot,
                expert=row * 2 + 1 - core,
            )
            copy.start()
            started.append(copy)

    def along_y(step_z):
        for step_y in range(chips - 1, 0, -1):
            row_to = lax.rem(row + step_y, chips)
            slot = step_z * chips + step_y
            send(
                c_in.at[slot], c_in.at[slot], c_send, c_recv, slot, expert=row * 2 + 1 - core
            ).wait_recv()
            hop = step_z * (chips - 1) + step_y - 1
            add(y_out.at[hop], tile(row_to, core, step_z), c_in.at[slot])
            copy = send(
                y_out.at[hop], y_in.at[hop], y_send, y_recv, hop, expert=row_to * 2 + core
            )
            copy.start()
            arrivals[hop] = copy
            started.append(copy)

    for index, step_z in enumerate(order):
        multiply(step_z)
        beside(step_z)
        if index:
            along_y(order[index - 1])
    along_y(order[-1])
    for step_z in order:
        slot = step_z * chips
        send(
            c_in.at[slot], c_in.at[slot], c_send, c_recv, slot, expert=row * 2 + 1 - core
        ).wait_recv()
        terms = [tile(row, core, step_z), c_in.at[slot]]
        for step_y in range(1, chips):
            hop = step_z * (chips - 1) + step_y - 1
            arrivals[hop].wait_recv()
            terms.append(y_in.at[hop])
        if step_z:
            add(z_out.at[step_z - 1], *terms)
            copy = send(
                z_out.at[step_z - 1],
                z_in.at[step_z - 1],
                z_send,
                z_recv,
                step_z - 1,
                donor=lax.rem(donor + step_z, donors),
            )
            copy.start()
            arrivals["z", step_z] = copy
            started.append(copy)
        else:
            for step in order[:-1]:
                arrivals["z", step].wait_recv()
                terms.append(z_in.at[step - 1])
            add(total_ref, *terms)
    for copy in started:
        copy.wait_send()


def reduce_blocks(activated, down, chips, donors):
    rows, cols = activated.shape[0] // (chips * 2), down.shape[1] // donors
    dma = pltpu.SemaphoreType.DMA
    held = lambda count: pltpu.VMEM((count, rows, cols), activated.dtype)
    return pl.pallas_call(
        functools.partial(reduce_kernel, chips, donors),
        out_shape=jax.ShapeDtypeStruct((rows, cols), jnp.float32),
        in_specs=[pl.BlockSpec(memory_space=pltpu.VMEM)] * 2,
        out_specs=pl.BlockSpec(memory_space=pltpu.VMEM),
        scratch_shapes=[
            pltpu.VMEM((activated.shape[0], down.shape[1]), activated.dtype),
            held(donors * chips),
            held(donors * (chips - 1)),
            held(donors * (chips - 1)),
            held(donors - 1),
            held(donors - 1),
            dma((donors * chips,)),
            dma((donors * chips,)),
            dma((donors * (chips - 1),)),
            dma((donors * (chips - 1),)),
            dma((donors - 1,)),
            dma((donors - 1,)),
        ],
        compiler_params=pltpu.CompilerParams(collective_id=2, has_side_effects=True),
        name="reduce_blocks",
    )(activated, down)


def mix_kernel(
    chips,
    donors,
    piece,
    heads_in,
    hidden_ref,
    gain_ref,
    gates_ref,
    outw_hbm,
    raw_hbm,
    down_hbm,
    out_ref,
    outw_ref,
    raw_ref,
    down_ref,
    heads_ref,
    p_ref,
    r_out,
    r_in,
    l_out,
    l_in,
    full_ref,
    w_ref,
    x_ref,
    acc_ref,
    ssq_ref,
    act_ref,
    part_ref,
    c_in,
    y_out,
    y_in,
    zr_out,
    zr_in,
    zl_out,
    zl_in,
    local_sem,
    raw_sem,
    hy_send,
    hy_recv,
    hc_send,
    hc_recv,
    r_send,
    r_recv,
    l_send,
    l_recv,
    y_send,
    y_recv,
    c_send,
    c_recv,
    cc_send,
    cc_recv,
    yy_send,
    yy_recv,
    zr_send,
    zr_recv,
    zl_send,
    zl_recv,
):
    row, core, donor = place()
    mine = row * 2 + core
    beside = row * 2 + 1 - core
    suffix, head_cols = heads_in.shape
    blocks, tokens, width = full_ref.shape
    model_width, ff_both = w_ref.shape
    ff_local = ff_both // 2
    seqs_each = hidden_ref.shape[0] // suffix
    per_seq = suffix // piece
    count = blocks * per_seq
    per_group = count // chips
    group_rows = 2 * suffix
    columns = out_ref.shape[1]
    last = donors - 1
    lag = 2
    first_mix = per_group + lag
    raw_steps, raw_slots, raw_rows = raw_sem.shape[0], raw_ref.shape[0], raw_ref.shape[1]
    relay = min(128, raw_rows)
    strip = 16

    own_copies = [
        pltpu.make_async_copy(outw_hbm, outw_ref, local_sem.at[0]),
        pltpu.make_async_copy(heads_in, heads_ref.at[pl.ds(mine * suffix, suffix)], local_sem.at[1]),
        pltpu.make_async_copy(down_hbm.at[0], down_ref, local_sem.at[2]),
    ]
    own_copies[0].start()
    own_copies[1].start()

    def raw_copy(index):
        at = pl.ds(pl.multiple_of(index * raw_rows, raw_rows), raw_rows)
        return pltpu.make_async_copy(
            raw_hbm.at[0, at], raw_ref.at[lax.rem(index, raw_slots)], raw_sem.at[index]
        )

    for index in range(raw_slots):
        raw_copy(index).start()
    own_copies[2].start()

    barrier = pltpu.get_barrier_semaphore()
    pl.semaphore_signal(barrier, inc=1, device_id={"expert": beside}, device_id_type=MESH)
    for step in range(1, chips):
        other = lax.rem(row + step, chips) * 2 + core
        pl.semaphore_signal(barrier, inc=1, device_id={"expert": other}, device_id_type=MESH)

    @pl.when(donor > 0)
    def _():
        pl.semaphore_signal(barrier, inc=1, device_id={"donor": donor - 1}, device_id_type=MESH)

    @pl.when(donor < last)
    def _():
        pl.semaphore_signal(barrier, inc=1, device_id={"donor": donor + 1}, device_id_type=MESH)

    acc_ref[...] = jnp.zeros_like(acc_ref)
    ssq_ref[...] = jnp.zeros_like(ssq_ref)
    pl.semaphore_wait(barrier, chips + jnp.minimum(donor, 1) + jnp.minimum(last - donor, 1))

    def heads_of(seq):
        return heads_ref.at[pl.ds(pl.multiple_of(seq * suffix, suffix), suffix)]

    def heads_y(step, seq, to):
        return send(heads_of(seq), heads_of(seq), hy_send, hy_recv, step - 1, expert=to)

    def heads_c(slot, seq):
        return send(heads_of(seq), heads_of(seq), hc_send, hc_recv, slot, expert=beside)

    own_copies[1].wait()
    heads_c(0, mine).start()
    for step in range(1, chips):
        heads_y(step, mine, lax.rem(row + step, chips) * 2 + core).start()
    own_copies[0].wait()

    def seq_at(from_row, from_core, index):
        return lax.rem(from_row + index // 2, chips) * 2 + lax.rem(from_core + lax.rem(index, 2), 2)

    def tile(from_row, from_core, chunk):
        seq = seq_at(from_row, from_core, chunk // per_seq)
        top = pl.multiple_of(seq * suffix + lax.rem(chunk, per_seq) * piece, piece)
        return full_ref.at[from_row * 2 + from_core, pl.ds(top, piece)]

    def right(chunk):
        return send(r_out.at[chunk], r_in.at[chunk], r_send, r_recv, chunk, donor=donor + 1)

    def left(chunk):
        return send(l_out.at[chunk], l_in.at[chunk], l_send, l_recv, chunk, donor=donor - 1)

    def across(step, chunk, from_row, to):
        there = tile(from_row, core, chunk)
        return send(there, there, y_send, y_recv, (step - 1) * count + chunk, expert=to)

    def over(step, chunk, from_row, from_core):
        there = tile(from_row, from_core, chunk)
        return send(there, there, c_send, c_recv, step * count + chunk, expert=beside)

    reach = jnp.maximum(donor, last - donor)

    def partial(index):
        seq = seq_at(row, core, index)
        step = index // 2

        @pl.when((index > 0) & (lax.rem(index, 2) == 0))
        def _():
            back = lax.rem(chips - step, chips)
            copy = send(
                heads_of(seq), heads_of(seq), hy_send, hy_recv, back - 1, expert=beside
            )
            copy.wait_recv()
            heads_c(back, seq).start()

        @pl.when(lax.rem(index, 2) == 1)
        def _():
            heads_c(lax.rem(chips - step, chips), seq).wait_recv()

        at = pl.ds(pl.multiple_of(index * suffix, suffix), suffix)
        p_ref[at, :] = jnp.dot(
            heads_ref[pl.ds(pl.multiple_of(seq * suffix, suffix), suffix), :],
            outw_ref[...],
            preferred_element_type=jnp.float32,
        )

        @pl.when(seq // seqs_each == donor)
        def _():
            top = pl.multiple_of(lax.rem(seq, seqs_each) * suffix, suffix)
            p_ref[at, :] = p_ref[at, :] + hidden_ref[pl.ds(top, suffix), :].astype(jnp.float32)

    def p_rows(chunk):
        return p_ref[pl.ds(pl.multiple_of(chunk * piece, piece), piece), :]

    def relay_weights(index):
        raw_copy(index).wait()
        half = lax.broadcasted_iota(jnp.int32, (relay, 2 * relay), 0)
        whole = lax.broadcasted_iota(jnp.int32, (relay, 2 * relay), 1)

        def body(part, carry):
            at = pl.ds(pl.multiple_of(index * raw_rows + part * relay, relay), relay)
            from_at = pl.ds(pl.multiple_of(part * relay, relay), relay)
            both = raw_ref[lax.rem(index, raw_slots), from_at].reshape(2 * relay, ff_local)
            for side in range(2):
                pick = (whole == 2 * half + side).astype(raw_ref.dtype)
                w_ref[at, side * ff_local : (side + 1) * ff_local] = jnp.dot(
                    pick, both, preferred_element_type=jnp.float32
                ).astype(w_ref.dtype)
            return carry

        lax.fori_loop(0, raw_rows // relay, body, 0)

        @pl.when(index + raw_slots < raw_steps)
        def _():
            raw_copy(index + raw_slots).start()

    cut = ff_both // 3

    def mix(turn, index):
        from_row = lax.rem(row + index // 2, chips)
        from_core = lax.rem(core + lax.rem(index, 2), 2)
        back = lax.rem(chips - index // 2, chips)

        @pl.when(lax.rem(index, 2) == 1)
        def _():
            def body(chunk, carry):
                over(back, turn * per_group + chunk, from_row, from_core).wait_recv()
                return carry

            lax.fori_loop(0, per_group, body, 0)

        block = from_row * 2 + from_core
        group = lax.rem(from_row + turn, chips)
        top = pl.multiple_of(group * group_rows, group_rows)
        left_at = pl.multiple_of(block * width, width)
        gain = gain_ref[:, pl.ds(left_at, width)].astype(jnp.float32)

        def scale(part, carry):
            here = pl.ds(pl.multiple_of(part * strip, strip), strip)
            at = pl.ds(pl.multiple_of(top + part * strip, strip), strip)
            value = full_ref[block, at, :].astype(jnp.float32)
            x_ref[here, :] = (value * gain).astype(x_ref.dtype)
            square = value * value
            total = square[:, :128]
            for start in range(128, width, 128):
                total = total + square[:, start : start + 128]
            ssq_ref[at, :] = ssq_ref[at, :] + total
            return carry

        lax.fori_loop(0, group_rows // strip, scale, 0)
        at = pl.ds(top, group_rows)

        def multiply(part, carry):
            wide = pl.ds(pl.multiple_of(part * cut, cut), cut)
            acc_ref[at, wide] = acc_ref[at, wide] + jnp.dot(
                x_ref[...], w_ref[pl.ds(left_at, width), wide], preferred_element_type=jnp.float32
            )
            return carry

        lax.fori_loop(0, ff_both // cut, multiply, 0)

    early = blocks * (chips - 1)

    def march(t, carry):
        @pl.when((t < count) & (lax.rem(t, per_seq) == 0))
        def _():
            partial(t // per_seq)

        here = t - donor

        @pl.when((here >= 0) & (here < count))
        def _():
            @pl.when(donor == 0)
            def _():
                r_out[here] = p_rows(here).astype(r_out.dtype)

            @pl.when(donor > 0)
            def _():
                right(here).wait_recv()

            @pl.when((donor > 0) & (donor < last))
            def _():
                r_out[here] = (p_rows(here) + r_in[here].astype(jnp.float32)).astype(r_out.dtype)

            @pl.when(donor < last)
            def _():
                right(here).start()

        there = t - (last - donor)

        @pl.when((there >= 0) & (there < count))
        def _():
            @pl.when(donor == last)
            def _():
                l_out[there] = p_rows(there).astype(l_out.dtype)

            @pl.when(donor < last)
            def _():
                left(there).wait_recv()

            @pl.when((donor > 0) & (donor < last))
            def _():
                l_out[there] = (p_rows(there) + l_in[there].astype(jnp.float32)).astype(l_out.dtype)

            @pl.when(donor > 0)
            def _():
                left(there).start()

        done = t - reach

        @pl.when((done >= 0) & (done < count))
        def _():
            goal = tile(row, core, done)

            @pl.when(donor == 0)
            def _():
                goal[...] = (p_rows(done) + l_in[done].astype(jnp.float32)).astype(goal.dtype)

            @pl.when(donor == last)
            def _():
                goal[...] = (p_rows(done) + r_in[done].astype(jnp.float32)).astype(goal.dtype)

            @pl.when((donor > 0) & (donor < last))
            def _():
                goal[...] = (
                    p_rows(done) + r_in[done].astype(jnp.float32) + l_in[done].astype(jnp.float32)
                ).astype(goal.dtype)

            for step in range(1, chips):
                across(step, done, row, lax.rem(row + step, chips) * 2 + core).start()
            over(0, done, row, core).start()

        came = t - reach - lag

        @pl.when((came >= 0) & (came < count))
        def _():
            for step in range(1, chips):
                from_row = lax.rem(row + chips - step, chips)
                across(step, came, from_row, from_row * 2 + core).wait_recv()
                over(step, came, from_row, core).start()

        @pl.when(t < raw_steps)
        def _():
            relay_weights(t)

        ready = t - reach - first_mix

        @pl.when((ready >= 0) & (ready < early))
        def _():
            mix(ready // blocks, lax.rem(ready, blocks))

        return carry

    steps = count + last + lag
    lax.fori_loop(0, steps, march, 0)

    def rest(index, carry):
        mix(index // blocks, lax.rem(index, blocks))
        return carry

    lax.fori_loop(jnp.minimum(steps - reach - first_mix, early), early, rest, 0)
    own_copies[2].wait()

    def activate(group):
        def body(part, carry):
            at = pl.ds(pl.multiple_of(group * group_rows + part * strip, strip), strip)
            mean = jnp.sum(ssq_ref[at, :], axis=1, keepdims=True) * (1.0 / model_width)
            inverse = lax.rsqrt(mean + 1e-06)
            gate = acc_ref[at, :ff_local] * inverse
            up = acc_ref[at, ff_local:] * inverse
            value = gate / (1.0 + jnp.exp(-gate)) * up * gates_ref[at, :]
            act_ref[at, :] = value.astype(act_ref.dtype)
            return carry

        lax.fori_loop(0, group_rows // strip, body, 0)

    def target(rank):
        low = jnp.minimum(donor, last - donor)
        single = reach - low
        rest_rank = rank - single
        gap = low - rest_rank // 2
        side = 1 - 2 * lax.rem(jnp.maximum(rest_rank, 0), 2)
        paired = donor + side * gap
        lone = jnp.where(donor < last - donor, last - rank, rank)
        return jnp.where(rank == last, donor, jnp.where(rank < single, lone, paired))

    def add(out, *terms):
        def body(part, carry):
            at = pl.ds(pl.multiple_of(part * strip, strip), strip)
            value = terms[0][at, :].astype(jnp.float32)
            for term in terms[1:]:
                value = value + term[at, :].astype(jnp.float32)
            out[at, :] = value.astype(out.dtype)
            return carry

        lax.fori_loop(0, suffix // strip, body, 0)

    order = list(range(1, chips)) + [0]

    def own_half(slot):
        return part_ref.at[slot, pl.ds(pl.multiple_of(core * suffix, suffix), suffix)]

    def swap(slot):
        away = part_ref.at[slot, pl.ds(pl.multiple_of((1 - core) * suffix, suffix), suffix)]
        return send(away, c_in.at[slot], cc_send, cc_recv, slot, expert=beside)

    def cross(hop, to):
        return send(y_out.at[hop], y_in.at[hop], yy_send, yy_recv, hop, expert=to)

    def produce(step, rank):
        slot = step * donors + rank
        top = pl.multiple_of(lax.rem(row + step, chips) * group_rows, group_rows)
        left_at = pl.multiple_of(target(rank) * columns, columns)
        part_ref[slot] = jnp.dot(
            act_ref[pl.ds(top, group_rows), :],
            down_ref[:, pl.ds(left_at, columns)],
            preferred_element_type=jnp.float32,
        ).astype(part_ref.dtype)
        swap(slot).start()

    def pass_on(step, rank):
        slot = step * donors + rank
        hop = (step - 1) * donors + rank
        swap(slot).wait_recv()
        add(y_out.at[hop], own_half(slot), c_in.at[slot])
        cross(hop, lax.rem(row + step, chips) * 2 + core).start()

    for step in order:
        for side in range(2):
            mix(chips - 1, 2 * ((step + 1) % chips) + side)
        activate(lax.rem(row + step, chips))
        if step:

            def body(rank, carry):
                produce(step, rank)

                @pl.when(rank > 0)
                def _():
                    pass_on(step, rank - 1)

                return carry

            lax.fori_loop(0, donors, body, 0)
            pass_on(step, donors - 1)
        else:

            def body(rank, carry):
                produce(0, rank)
                return carry

            lax.fori_loop(0, donors, body, 0)

    def shift_right(goal):
        return send(zr_out.at[goal], zr_in.at[goal], zr_send, zr_recv, goal, donor=donor + 1)

    def shift_left(goal):
        return send(zl_out.at[goal], zl_in.at[goal], zl_send, zl_recv, goal, donor=donor - 1)

    def finish(rank, carry):
        goal = target(rank)
        swap(rank).wait_recv()
        terms = [own_half(rank), c_in.at[rank]]
        for step in range(1, chips):
            hop = (step - 1) * donors + rank
            cross(hop, mine).wait_recv()
            terms.append(y_in.at[hop])

        @pl.when((goal >= donor) & (donor > 0))
        def _():
            shift_right(goal).wait_recv()

        @pl.when((goal <= donor) & (donor < last))
        def _():
            shift_left(goal).wait_recv()

        @pl.when(goal > donor)
        def _():
            @pl.when(donor == 0)
            def _():
                add(zr_out.at[goal], *terms)

            @pl.when(donor > 0)
            def _():
                add(zr_out.at[goal], zr_in.at[goal], *terms)

            shift_right(goal).start()

        @pl.when(goal < donor)
        def _():
            @pl.when(donor == last)
            def _():
                add(zl_out.at[goal], *terms)

            @pl.when(donor < last)
            def _():
                add(zl_out.at[goal], zl_in.at[goal], *terms)

            shift_left(goal).start()

        @pl.when(goal == donor)
        def _():
            def close(ends):
                for part in range(columns // width):
                    wide = slice(part * width, (part + 1) * width)

                    def body(index, carry):
                        at = pl.ds(pl.multiple_of(index * strip, strip), strip)
                        down = pl.ds(pl.multiple_of(mine * suffix + index * strip, strip), strip)
                        value = full_ref[donor * (columns // width) + part, down, :].astype(jnp.float32)
                        total = terms[0][at, wide].astype(jnp.float32)
                        for term in terms[1:] + ends:
                            total = total + term[at, wide].astype(jnp.float32)
                        out_ref[at, wide] = (value + total).astype(out_ref.dtype)
                        return carry

                    lax.fori_loop(0, suffix // strip, body, 0)

            @pl.when(donor == 0)
            def _():
                close([zl_in.at[donor]])

            @pl.when(donor == last)
            def _():
                close([zr_in.at[donor]])

            @pl.when((donor > 0) & (donor < last))
            def _():
                close([zl_in.at[donor], zr_in.at[donor]])

        return carry

    lax.fori_loop(0, donors, finish, 0)

    for step in range(1, chips):
        heads_y(step, mine, mine).wait_send()
    for step in range(chips):
        heads_c(step, mine).wait_send()

    def drain(chunk, carry):
        @pl.when(donor < last)
        def _():
            right(chunk).wait_send()

        @pl.when(donor > 0)
        def _():
            left(chunk).wait_send()

        for step in range(1, chips):
            across(step, chunk, row, mine).wait_send()
        for step in range(chips):
            over(step, chunk, row, core).wait_send()
        return carry

    lax.fori_loop(0, count, drain, 0)

    def drain_blocks(goal, carry):
        for step in range(chips):
            swap(step * donors + goal).wait_send()
        for step in range(1, chips):
            cross((step - 1) * donors + goal, mine).wait_send()

        @pl.when(goal > donor)
        def _():
            shift_right(goal).wait_send()

        @pl.when(goal < donor)
        def _():
            shift_left(goal).wait_send()

        return carry

    lax.fori_loop(0, donors, drain_blocks, 0)


def mix_scratch(heads, out_weight, w_gate_up, chips, donors, piece):
    suffix, head_cols = heads.shape
    blocks = 2 * chips
    width = out_weight.shape[1]
    model_width, ff_local = w_gate_up.shape[1], w_gate_up.shape[3]
    tokens = blocks * suffix
    columns = model_width // donors
    count = tokens // piece
    kind = heads.dtype
    vmem = lambda *shape: pltpu.VMEM(shape, kind)
    wide = lambda *shape: pltpu.VMEM(shape, jnp.float32)
    held = lambda number: pltpu.VMEM((number, suffix, columns), kind)
    return [
        vmem(head_cols, width),
        vmem(3, model_width // 8, 2, ff_local),
        vmem(ff_local, model_width),
        vmem(tokens, head_cols),
        wide(tokens, width),
        vmem(count, piece, width),
        vmem(count, piece, width),
        vmem(count, piece, width),
        vmem(count, piece, width),
        vmem(blocks, tokens, width),
        vmem(model_width, 2 * ff_local),
        vmem(2 * suffix, width),
        wide(tokens, 2 * ff_local),
        wide(tokens, 128),
        vmem(tokens, ff_local),
        vmem(chips * donors, 2 * suffix, columns),
        held(chips * donors),
        held((chips - 1) * donors),
        held((chips - 1) * donors),
        held(donors),
        held(donors),
        held(donors),
        held(donors),
    ]


def mix_blocks(heads, hidden, gain, gates, out_weight, w_gate_up, w_down, chips, donors, piece, scratch):
    suffix = heads.shape[0]
    columns = w_gate_up.shape[1] // donors
    count = 2 * chips * suffix // piece
    dma = pltpu.SemaphoreType.DMA
    pair = lambda number: [dma((number,)), dma((number,))]
    inside = pl.BlockSpec(memory_space=pltpu.VMEM)
    outside = pl.BlockSpec(memory_space=pl.ANY)
    return pl.pallas_call(
        functools.partial(mix_kernel, chips, donors, piece),
        out_shape=jax.ShapeDtypeStruct((suffix, columns), heads.dtype),
        in_specs=[inside] * 4 + [outside] * 3,
        out_specs=inside,
        scratch_shapes=scratch
        + [dma((3,)), dma((8,))]
        + pair(chips - 1)
        + pair(chips)
        + pair(count)
        + pair(count)
        + pair((chips - 1) * count)
        + pair(chips * count)
        + pair(chips * donors)
        + pair((chips - 1) * donors)
        + pair(donors)
        + pair(donors),
        compiler_params=pltpu.CompilerParams(
            collective_id=3, has_side_effects=True, vmem_limit_bytes=VMEM_BYTES
        ),
        name="mix_blocks",
    )(heads, hidden, gain, gates, out_weight, w_gate_up, w_down)


def shards(
    hidden_in,
    queries,
    suffix_kv,
    kv_pool,
    page_table,
    prefix_len,
    out_weight,
    norm_gain,
    expert_ids,
    route_probs,
    w_gate_up,
    w_down,
):
    n_expert = lax.axis_size("expert")
    n_donor = lax.axis_size("donor")
    expert_index = lax.axis_index("expert")
    donor_index = lax.axis_index("donor")
    share_count = n_donor // 2
    seq_count, page_count = page_table.shape
    suffix_len = queries.shape[0]
    kv_heads = suffix_kv.shape[1]
    head_dim = suffix_kv.shape[2] // 2
    page_len = kv_pool.shape[2]
    model_width = hidden_in.shape[1]
    columns = model_width // n_donor
    experts_all = 2 * n_expert
    ff_local = w_gate_up.shape[3]
    my_group = donor_index * kv_heads // n_donor
    owner_index = expert_index * n_donor + donor_index
    owner_of = page_table // seq_count
    held_slot = jnp.sum(jnp.where(owner_of == owner_index, page_table % seq_count, 0), axis=1)
    dest_group = jnp.arange(n_donor, dtype=jnp.int32) * kv_heads // n_donor
    wanted = (held_slot[:, None] * kv_heads + dest_group[None, :]).reshape(-1)
    outgoing = jnp.take(
        kv_pool.reshape(seq_count * kv_heads, page_len, 2 * head_dim), wanted, axis=0
    )
    arrived = lax.all_to_all(outgoing, ("expert", "donor"), split_axis=0, concat_axis=0, tiled=True)
    my_owners = lax.dynamic_index_in_dim(owner_of, expert_index, 0, keepdims=False)
    ordered = jnp.take(arrived, my_owners, axis=0).reshape(page_count * page_len, 2 * head_dim)
    prefix_keys = ordered[:, :head_dim]
    prefix_vals = ordered[:, head_dim:]
    score_scale = head_dim ** (-0.5)
    query_heads = queries.reshape(suffix_len, -1, head_dim)
    fresh_pair = lax.dynamic_index_in_dim(suffix_kv, my_group, 1, keepdims=False)
    causal = jnp.arange(suffix_len)[:, None] >= jnp.arange(suffix_len)[None, :]
    fresh_scores = (
        jnp.einsum(
            "thc,uc->thu", query_heads, fresh_pair[:, :head_dim], preferred_element_type=jnp.float32
        )
        * score_scale
    )
    fresh_scores = jnp.where(causal[:, None, :], fresh_scores, -jnp.inf)
    prefix_tokens = lax.dynamic_index_in_dim(prefix_len, expert_index, 0, keepdims=False)
    block_keys = min(1024, page_count * page_len)
    live_blocks = (prefix_tokens + block_keys - 1) // block_keys

    def block_scores(block_index):
        keys_block = lax.dynamic_slice_in_dim(prefix_keys, block_index * block_keys, block_keys, 0)
        raw_scores = (
            jnp.einsum("thc,kc->thk", query_heads, keys_block, preferred_element_type=jnp.float32)
            * score_scale
        )
        visible = block_index * block_keys + jnp.arange(block_keys) < prefix_tokens
        return jnp.where(visible[None, None, :], raw_scores, -jnp.inf)

    def raise_max(block_index, running):
        return jnp.maximum(running, jnp.max(block_scores(block_index), axis=2))

    row_max = lax.fori_loop(0, live_blocks, raise_max, jnp.max(fresh_scores, axis=2))

    def add_block(block_index, loop_state):
        row_total, weighted = loop_state
        exp_scores = jnp.exp(block_scores(block_index) - row_max[:, :, None])
        vals_block = lax.dynamic_slice_in_dim(prefix_vals, block_index * block_keys, block_keys, 0)
        weighted = weighted + jnp.einsum(
            "thk,kc->thc",
            exp_scores.astype(jnp.bfloat16),
            vals_block,
            preferred_element_type=jnp.float32,
        )
        return (row_total + jnp.sum(exp_scores, axis=2), weighted)

    fresh_exp = jnp.exp(fresh_scores - row_max[:, :, None])
    start_state = (
        jnp.sum(fresh_exp, axis=2),
        jnp.einsum(
            "thu,uc->thc",
            fresh_exp.astype(jnp.bfloat16),
            fresh_pair[:, head_dim:],
            preferred_element_type=jnp.float32,
        ),
    )
    row_total, weighted = lax.fori_loop(0, live_blocks, add_block, start_state)
    head_out = (weighted / row_total[:, :, None]).astype(jnp.bfloat16).reshape(suffix_len, -1)
    gate_weights = route_probs / jnp.sum(route_probs, axis=1, keepdims=True)
    chosen = expert_ids[:, :, None] == jnp.arange(experts_all, dtype=jnp.int32)
    gate_table = jnp.sum(jnp.where(chosen, gate_weights[:, :, None], 0.0), axis=1)
    gate_tables = [gate_table]
    for step in range(1, n_expert):
        pairs = [(source, (source + step) % n_expert) for source in range(n_expert)]
        gate_tables.append(lax.ppermute(gate_table, "expert", pairs))
    from_order = lax.rem(expert_index - jnp.arange(n_expert) + n_expert, n_expert)
    gate_all = jnp.stack(gate_tables)[from_order].reshape(n_expert * suffix_len, experts_all)
    my_expert = owner_index // share_count
    my_gates = lax.dynamic_slice_in_dim(gate_all, my_expert, 1, 1)

    seqs_each = n_expert // n_donor
    width = model_width // n_expert
    hidden_parts = []
    for shift in range(seqs_each):
        pairs = []
        for source in range(n_expert * n_donor):
            seq, part = source // n_donor, source % n_donor
            target = part * seqs_each + (seq + shift) % seqs_each
            pairs.append((source, target * n_donor + seq // seqs_each))
        target = donor_index * seqs_each + lax.rem(expert_index + shift, seqs_each)
        sent = lax.dynamic_slice_in_dim(hidden_in, target * width, width, 1)
        hidden_parts.append(lax.ppermute(sent, ("expert", "donor"), pairs))
    turned = lax.rem(expert_index - jnp.arange(seqs_each) + seqs_each * n_expert, seqs_each)
    hidden_block = jnp.stack(hidden_parts)[turned].reshape(seqs_each * suffix_len, width)

    chips = n_expert // 2
    scratch = mix_scratch(head_out, out_weight, w_gate_up, chips, n_donor, PIECE)
    held_bytes = sum(math.prod(item.shape) * item.dtype.itemsize for item in scratch)
    if held_bytes <= VMEM_BYTES - 4 * 1024 * 1024:
        layer_out = mix_blocks(
            head_out,
            hidden_block,
            norm_gain.reshape(1, model_width),
            my_gates,
            out_weight,
            w_gate_up,
            w_down,
            chips,
            n_donor,
            PIECE,
            scratch,
        )
        return (layer_out, head_out)

    heads_all = lax.all_gather(head_out, "expert", axis=0, tiled=True)
    w_in, heads_all = lax.optimization_barrier(
        (w_gate_up[0].reshape(model_width, 2 * ff_local), heads_all)
    )
    resid = gather_blocks(heads_all, out_weight, hidden_block, n_expert // 2, n_donor)
    resid_f = resid.astype(jnp.float32)
    inverse = lax.rsqrt(jnp.mean(resid_f * resid_f, axis=1, keepdims=True) + 1e-06)
    normed = (resid_f * inverse * norm_gain.astype(jnp.float32)).astype(jnp.bfloat16)
    gate_up = jnp.dot(
        normed,
        w_in,
        preferred_element_type=jnp.float32,
    )
    activated = (
        jax.nn.silu(gate_up[:, :ff_local]) * gate_up[:, ff_local:] * my_gates
    ).astype(jnp.bfloat16)
    expert_mix = reduce_blocks(activated, w_down[0], n_expert // 2, n_donor)
    resid_mine = lax.dynamic_slice(
        resid,
        (expert_index * suffix_len, donor_index * columns),
        (suffix_len, columns),
    )
    layer_out = (resid_mine.astype(jnp.float32) + expert_mix).astype(
        jnp.bfloat16
    )
    return (layer_out, head_out)


def solution(mesh):
    in_specs = (
        P(("groups", "expert"), None),
        P(("groups", "expert"), "donor"),
        P(("groups", "expert"), None, None),
        P(("groups", "expert", "donor"), None, None, None),
        P("groups", None),
        P("groups"),
        P("donor", "expert"),
        P(),
        P(("groups", "expert"), None),
        P(("groups", "expert"), None),
        P(("expert", "donor"), None, None, None),
        P(("expert", "donor"), None, None),
    )
    out_specs = (P(("groups", "expert"), "donor"), P(("groups", "expert"), "donor"))
    return jax.shard_map(shards, mesh=mesh, in_specs=in_specs, out_specs=out_specs, check_vma=False)
```

```python
import functools
import math

import jax
import jax.numpy as jnp
from jax import lax
from jax.experimental import pallas as pl
from jax.experimental.pallas import tpu as pltpu
from jax.sharding import PartitionSpec as P

MESH = pl.DeviceIdType.MESH
VMEM_BYTES = 60 * 1024 * 1024
PIECE = 32
HOP = 3
LAG = 3


def place():
    expert = lax.axis_index("expert")
    return expert // 2, lax.rem(expert, 2), lax.axis_index("donor")


def send(src, dst, sends, recvs, slot, **where):
    return pltpu.make_async_remote_copy(
        src_ref=src,
        dst_ref=dst,
        send_sem=sends.at[slot],
        recv_sem=recvs.at[slot],
        device_id=where,
        device_id_type=MESH,
    )


def greet(chips, donors):
    row, core, donor = place()
    barrier = pltpu.get_barrier_semaphore()
    pl.semaphore_signal(
        barrier, inc=1, device_id={"expert": row * 2 + 1 - core}, device_id_type=MESH
    )
    for step in range(1, chips):
        other = lax.rem(row + step, chips) * 2 + core
        pl.semaphore_signal(barrier, inc=1, device_id={"expert": other}, device_id_type=MESH)
    for step in range(1, donors):
        other = lax.rem(donor + step, donors)
        pl.semaphore_signal(barrier, inc=1, device_id={"donor": other}, device_id_type=MESH)
    pl.semaphore_wait(barrier, chips + donors - 1)


def far_first(donors):
    return sorted(range(1, donors), key=lambda k: (-min(k, donors - k), k))


def gather_kernel(
    chips,
    donors,
    heads_ref,
    out_ref,
    hidden_ref,
    full_ref,
    terms_ref,
    terms_in,
    block_ref,
    own_sem,
    t_send,
    t_recv,
    z_send,
    z_recv,
    y_send,
    y_recv,
    c_send,
    c_recv,
):
    row, core, donor = place()
    rows, cols = block_ref.shape
    greet(chips, donors)
    strip = 16

    def project(step_z, slot):
        top = pl.multiple_of(lax.rem(donor + step_z, donors) * rows, rows)
        terms_ref[slot] = jnp.dot(
            heads_ref[pl.ds(top, rows), :], out_ref[...], preferred_element_type=jnp.float32
        ).astype(terms_ref.dtype)

    term_copies = {}
    for step in far_first(donors):
        project(step, step)
        copy = send(
            terms_ref.at[step],
            terms_in.at[step - 1],
            t_send,
            t_recv,
            step - 1,
            donor=lax.rem(donor + step, donors),
        )
        copy.start()
        term_copies[step] = copy
    project(0, 0)
    for step in far_first(donors):
        term_copies[step].wait_recv()

    def add(index, carry):
        at = pl.ds(pl.multiple_of(index * strip, strip), strip)
        value = terms_ref[0, at, :].astype(jnp.float32)
        for step in range(1, donors):
            value = value + terms_in[step - 1, at, :].astype(jnp.float32)
        value = value + hidden_ref[at, :].astype(jnp.float32)
        block_ref[at, :] = value.astype(block_ref.dtype)
        return carry

    lax.fori_loop(0, rows // strip, add, 0)

    def slot_of(donor_from, row_from, core_from):
        top = pl.multiple_of(donor_from * rows, rows)
        left = pl.multiple_of((row_from * 2 + core_from) * cols, cols)
        return full_ref.at[pl.ds(top, rows), pl.ds(left, cols)]

    own = pltpu.make_async_copy(block_ref, slot_of(donor, row, core), own_sem)
    own.start()
    started = []

    def along_y(src, step_z, donor_from):
        for step in range(1, chips):
            copy = send(
                src,
                slot_of(donor_from, row, core),
                y_send,
                y_recv,
                step_z * (chips - 1) + step - 1,
                expert=lax.rem(row + step, chips) * 2 + core,
            )
            copy.start()
            started.append(copy)

    def beside(src, step_z, step_y, donor_from, row_from):
        copy = send(
            src,
            slot_of(donor_from, row_from, core),
            c_send,
            c_recv,
            step_z * chips + step_y,
            expert=row * 2 + 1 - core,
        )
        copy.start()
        started.append(copy)

    along_y(block_ref, 0, donor)
    z_copies = {}
    near_first = far_first(donors)[::-1]
    for step in near_first:
        copy = send(
            block_ref,
            slot_of(donor, row, core),
            z_send,
            z_recv,
            step - 1,
            donor=lax.rem(donor + step, donors),
        )
        copy.start()
        z_copies[step] = copy
    beside(block_ref, 0, 0, donor, row)

    def take_y(step_z, donor_from):
        for step in range(1, chips):
            row_from = lax.rem(row + chips - step, chips)
            there = slot_of(donor_from, row_from, core)
            send(
                there,
                there,
                y_send,
                y_recv,
                step_z * (chips - 1) + step - 1,
                expert=row_from * 2 + core,
            ).wait_recv()
            beside(there, step_z, step, donor_from, row_from)

    for step in near_first:
        donor_from = lax.rem(donor + donors - step, donors)
        there = slot_of(donor_from, row, core)
        send(there, there, z_send, z_recv, step - 1, donor=donor_from).wait_recv()
        along_y(there, step, donor_from)
        beside(there, step, 0, donor_from, row)
    for step in [0] + near_first:
        take_y(step, lax.rem(donor + donors - step, donors))
    for step_z in range(donors):
        donor_from = lax.rem(donor + donors - step_z, donors)
        for step_y in range(chips):
            row_from = lax.rem(row + chips - step_y, chips)
            there = slot_of(donor_from, row_from, 1 - core)
            send(
                there, there, c_send, c_recv, step_z * chips + step_y, expert=row * 2 + 1 - core
            ).wait_recv()
    own.wait()
    for copy in list(term_copies.values()) + list(z_copies.values()) + started:
        copy.wait_send()


def gather_blocks(heads, out_weight, block, chips, donors):
    rows, cols = block.shape
    dma = pltpu.SemaphoreType.DMA
    return pl.pallas_call(
        functools.partial(gather_kernel, chips, donors),
        out_shape=jax.ShapeDtypeStruct((rows * donors, cols * chips * 2), block.dtype),
        in_specs=[pl.BlockSpec(memory_space=pltpu.VMEM)] * 3,
        out_specs=pl.BlockSpec(memory_space=pltpu.VMEM),
        scratch_shapes=[
            pltpu.VMEM((donors, rows, cols), block.dtype),
            pltpu.VMEM((donors - 1, rows, cols), block.dtype),
            pltpu.VMEM((rows, cols), block.dtype),
            dma,
            dma((donors - 1,)),
            dma((donors - 1,)),
            dma((donors - 1,)),
            dma((donors - 1,)),
            dma((donors * (chips - 1),)),
            dma((donors * (chips - 1),)),
            dma((donors * chips,)),
            dma((donors * chips,)),
        ],
        compiler_params=pltpu.CompilerParams(collective_id=1, has_side_effects=True),
        name="gather_blocks",
    )(heads, out_weight, block)


def reduce_kernel(
    chips,
    donors,
    act_ref,
    down_ref,
    total_ref,
    part_ref,
    c_in,
    y_out,
    y_in,
    z_out,
    z_in,
    c_send,
    c_recv,
    y_send,
    y_recv,
    z_send,
    z_recv,
):
    row, core, donor = place()
    rows, cols = total_ref.shape
    greet(chips, donors)
    order = far_first(donors) + [0]
    strip = 16

    def tile(row_to, core_to, step_z):
        top = pl.multiple_of((row_to * 2 + core_to) * rows, rows)
        left = pl.multiple_of(lax.rem(donor + step_z, donors) * cols, cols)
        return part_ref.at[pl.ds(top, rows), pl.ds(left, cols)]

    def add(out, *terms):
        def body(index, carry):
            at = pl.ds(pl.multiple_of(index * strip, strip), strip)
            value = terms[0][at, :].astype(jnp.float32)
            for term in terms[1:]:
                value = value + term[at, :].astype(jnp.float32)
            out[at, :] = value.astype(out.dtype)
            return carry

        lax.fori_loop(0, rows // strip, body, 0)

    started = []
    arrivals = {}

    def multiply(step_z):
        left = pl.multiple_of(lax.rem(donor + step_z, donors) * cols, cols)

        def body(index, carry):
            at = pl.ds(pl.multiple_of(index * rows, rows), rows)
            part_ref[at, pl.ds(left, cols)] = jnp.dot(
                act_ref[at, :],
                down_ref[:, pl.ds(left, cols)],
                preferred_element_type=jnp.float32,
            ).astype(part_ref.dtype)
            return carry

        lax.fori_loop(0, chips * 2, body, 0)

    def beside(step_z):
        for step_y in range(chips - 1, -1, -1):
            slot = step_z * chips + step_y
            copy = send(
                tile(lax.rem(row + step_y, chips), 1 - core, step_z),
                c_in.at[slot],
                c_send,
                c_recv,
                slot,
                expert=row * 2 + 1 - core,
            )
            copy.start()
            started.append(copy)

    def along_y(step_z):
        for step_y in range(chips - 1, 0, -1):
            row_to = lax.rem(row + step_y, chips)
            slot = step_z * chips + step_y
            send(
                c_in.at[slot], c_in.at[slot], c_send, c_recv, slot, expert=row * 2 + 1 - core
            ).wait_recv()
            hop = step_z * (chips - 1) + step_y - 1
            add(y_out.at[hop], tile(row_to, core, step_z), c_in.at[slot])
            copy = send(
                y_out.at[hop], y_in.at[hop], y_send, y_recv, hop, expert=row_to * 2 + core
            )
            copy.start()
            arrivals[hop] = copy
            started.append(copy)

    for index, step_z in enumerate(order):
        multiply(step_z)
        beside(step_z)
        if index:
            along_y(order[index - 1])
    along_y(order[-1])
    for step_z in order:
        slot = step_z * chips
        send(
            c_in.at[slot], c_in.at[slot], c_send, c_recv, slot, expert=row * 2 + 1 - core
        ).wait_recv()
        terms = [tile(row, core, step_z), c_in.at[slot]]
        for step_y in range(1, chips):
            hop = step_z * (chips - 1) + step_y - 1
            arrivals[hop].wait_recv()
            terms.append(y_in.at[hop])
        if step_z:
            add(z_out.at[step_z - 1], *terms)
            copy = send(
                z_out.at[step_z - 1],
                z_in.at[step_z - 1],
                z_send,
                z_recv,
                step_z - 1,
                donor=lax.rem(donor + step_z, donors),
            )
            copy.start()
            arrivals["z", step_z] = copy
            started.append(copy)
        else:
            for step in order[:-1]:
                arrivals["z", step].wait_recv()
                terms.append(z_in.at[step - 1])
            add(total_ref, *terms)
    for copy in started:
        copy.wait_send()


def reduce_blocks(activated, down, chips, donors):
    rows, cols = activated.shape[0] // (chips * 2), down.shape[1] // donors
    dma = pltpu.SemaphoreType.DMA
    held = lambda count: pltpu.VMEM((count, rows, cols), activated.dtype)
    return pl.pallas_call(
        functools.partial(reduce_kernel, chips, donors),
        out_shape=jax.ShapeDtypeStruct((rows, cols), jnp.float32),
        in_specs=[pl.BlockSpec(memory_space=pltpu.VMEM)] * 2,
        out_specs=pl.BlockSpec(memory_space=pltpu.VMEM),
        scratch_shapes=[
            pltpu.VMEM((activated.shape[0], down.shape[1]), activated.dtype),
            held(donors * chips),
            held(donors * (chips - 1)),
            held(donors * (chips - 1)),
            held(donors - 1),
            held(donors - 1),
            dma((donors * chips,)),
            dma((donors * chips,)),
            dma((donors * (chips - 1),)),
            dma((donors * (chips - 1),)),
            dma((donors - 1,)),
            dma((donors - 1,)),
        ],
        compiler_params=pltpu.CompilerParams(collective_id=2, has_side_effects=True),
        name="reduce_blocks",
    )(activated, down)


def mix_kernel(
    chips,
    donors,
    piece,
    heads_in,
    gain_ref,
    probs_ref,
    ids_ref,
    hidden_hbm,
    outw_hbm,
    raw_hbm,
    down_hbm,
    out_ref,
    hidden_ref,
    gates_out,
    gates_in,
    outw_ref,
    raw_ref,
    down_ref,
    heads_ref,
    p_ref,
    r_out,
    r_in,
    l_out,
    l_in,
    full_ref,
    w_ref,
    x_ref,
    acc_ref,
    ssq_ref,
    act_ref,
    gates_ref,
    part_ref,
    c_in,
    y_out,
    y_in,
    zr_out,
    zr_in,
    zl_out,
    zl_in,
    local_sem,
    raw_sem,
    g_send,
    g_recv,
    h_send,
    h_recv,
    hy_send,
    hy_recv,
    hc_send,
    hc_recv,
    r_send,
    r_recv,
    l_send,
    l_recv,
    y_send,
    y_recv,
    c_send,
    c_recv,
    cc_send,
    cc_recv,
    yy_send,
    yy_recv,
    zr_send,
    zr_recv,
    zl_send,
    zl_recv,
):
    row, core, donor = place()
    mine = row * 2 + core
    beside = row * 2 + 1 - core
    suffix, head_cols = heads_in.shape
    blocks, tokens, width = full_ref.shape
    model_width, ff_both = w_ref.shape
    ff_local = ff_both // 2
    seqs_each = hidden_ref.shape[0]
    per_seq = suffix // piece
    count = blocks * per_seq
    per_group = count // chips
    group_rows = 2 * suffix
    columns = out_ref.shape[1]
    last = donors - 1
    lag = LAG
    first_mix = per_group + lag
    raw_steps, raw_slots, raw_rows = raw_sem.shape[0], raw_ref.shape[0], raw_ref.shape[1]
    relay = min(128, raw_rows)
    strip = 16

    own_copies = [
        pltpu.make_async_copy(outw_hbm, outw_ref, local_sem.at[0]),
        pltpu.make_async_copy(heads_in, heads_ref.at[pl.ds(mine * suffix, suffix)], local_sem.at[1]),
        pltpu.make_async_copy(down_hbm.at[0], down_ref, local_sem.at[2]),
    ]
    own_copies[0].start()
    own_copies[1].start()

    def raw_copy(index):
        at = pl.ds(pl.multiple_of(index * raw_rows, raw_rows), raw_rows)
        return pltpu.make_async_copy(
            raw_hbm.at[0, at], raw_ref.at[lax.rem(index, raw_slots)], raw_sem.at[index]
        )

    for index in range(raw_slots):
        raw_copy(index).start()
    own_copies[2].start()

    barrier = pltpu.get_barrier_semaphore()
    for step in range(1, blocks):
        other = lax.rem(mine + step, blocks)
        pl.semaphore_signal(barrier, inc=1, device_id={"expert": other}, device_id_type=MESH)

    @pl.when(donor > 0)
    def _():
        pl.semaphore_signal(barrier, inc=1, device_id={"donor": donor - 1}, device_id_type=MESH)

    @pl.when(donor < last)
    def _():
        pl.semaphore_signal(barrier, inc=1, device_id={"donor": donor + 1}, device_id_type=MESH)

    acc_ref[...] = jnp.zeros_like(acc_ref)
    ssq_ref[...] = jnp.zeros_like(ssq_ref)
    pl.semaphore_wait(barrier, blocks - 1 + jnp.minimum(donor, 1) + jnp.minimum(last - donor, 1))

    def heads_of(seq):
        return heads_ref.at[pl.ds(pl.multiple_of(seq * suffix, suffix), suffix)]

    def heads_y(step, seq, to):
        return send(heads_of(seq), heads_of(seq), hy_send, hy_recv, step - 1, expert=to)

    def heads_c(slot, seq):
        return send(heads_of(seq), heads_of(seq), hc_send, hc_recv, slot, expert=beside)

    def gates_to(step):
        return send(
            gates_out.at[step],
            gates_in.at[mine],
            g_send,
            g_recv,
            step - 1,
            expert=lax.rem(mine + step, blocks),
        )

    def partner(index):
        return lax.rem(donor - lax.rem(mine, donors) + donors, donors) + donors * index

    def hidden_to(index):
        at = pl.ds(pl.multiple_of(partner(index) * width, width), width)
        slot = mine // donors
        return pltpu.make_async_remote_copy(
            src_ref=hidden_hbm.at[:, at],
            dst_ref=hidden_ref.at[slot],
            send_sem=h_send.at[index],
            recv_sem=h_recv.at[slot],
            device_id={"expert": partner(index)},
            device_id_type=MESH,
        )

    def hidden_own(index):
        at = pl.ds(pl.multiple_of(mine * width, width), width)
        return pltpu.make_async_copy(hidden_hbm.at[:, at], hidden_ref.at[index], h_recv.at[index])

    own_copies[1].wait()
    heads_c(0, mine).start()
    for step in range(1, chips):
        heads_y(step, mine, lax.rem(row + step, chips) * 2 + core).start()
    for index in range(seqs_each):

        @pl.when(partner(index) != mine)
        def _():
            hidden_to(index).start()

        @pl.when(partner(index) == mine)
        def _():
            hidden_own(index).start()

    square = (suffix, suffix)
    eye = lax.broadcasted_iota(jnp.int32, square, 0) == lax.broadcasted_iota(jnp.int32, square, 1)
    parts_of = donors // 2
    share = probs_ref[...] / jnp.sum(probs_ref[...], axis=1, keepdims=True)
    for step in range(blocks):
        named = (lax.rem(mine + step, blocks) * donors + donor) // parts_of
        column = jnp.sum(jnp.where(ids_ref[...] == named, share, 0.0), axis=1, keepdims=True)
        line = jnp.sum(jnp.where(eye, column, 0.0), axis=0, keepdims=True)
        if step:
            gates_out[step] = jnp.broadcast_to(line, gates_out.shape[1:])
            gates_to(step).start()
        else:
            gates_in[mine] = jnp.broadcast_to(line, gates_out.shape[1:])
    own_copies[0].wait()

    def seq_at(from_row, from_core, index):
        return lax.rem(from_row + index // 2, chips) * 2 + lax.rem(from_core + lax.rem(index, 2), 2)

    def tile(from_row, from_core, chunk):
        seq = seq_at(from_row, from_core, chunk // per_seq)
        top = pl.multiple_of(seq * suffix + lax.rem(chunk, per_seq) * piece, piece)
        return full_ref.at[from_row * 2 + from_core, pl.ds(top, piece)]

    def right(chunk):
        return send(r_out.at[chunk], r_in.at[chunk], r_send, r_recv, chunk, donor=donor + 1)

    def left(chunk):
        return send(l_out.at[chunk], l_in.at[chunk], l_send, l_recv, chunk, donor=donor - 1)

    def across(step, chunk, from_row, to):
        there = tile(from_row, core, chunk)
        return send(there, there, y_send, y_recv, (step - 1) * count + chunk, expert=to)

    def over(step, chunk, from_row, from_core):
        there = tile(from_row, from_core, chunk)
        return send(there, there, c_send, c_recv, step * count + chunk, expert=beside)

    reach = jnp.maximum(donor, last - donor) * HOP

    def partial(index):
        seq = seq_at(row, core, index)
        step = index // 2

        @pl.when((index > 0) & (lax.rem(index, 2) == 0))
        def _():
            back = lax.rem(chips - step, chips)
            copy = send(
                heads_of(seq), heads_of(seq), hy_send, hy_recv, back - 1, expert=beside
            )
            copy.wait_recv()
            heads_c(back, seq).start()

        @pl.when(lax.rem(index, 2) == 1)
        def _():
            heads_c(lax.rem(chips - step, chips), seq).wait_recv()

        at = pl.ds(pl.multiple_of(index * suffix, suffix), suffix)
        p_ref[at, :] = jnp.dot(
            heads_ref[pl.ds(pl.multiple_of(seq * suffix, suffix), suffix), :],
            outw_ref[...],
            preferred_element_type=jnp.float32,
        )

        for index in range(seqs_each):

            @pl.when(partner(index) == seq)
            def _():
                hidden_own(index).wait()
                p_ref[at, :] = p_ref[at, :] + hidden_ref[index].astype(jnp.float32)

    def p_rows(chunk):
        return p_ref[pl.ds(pl.multiple_of(chunk * piece, piece), piece), :]

    def relay_weights(index):
        raw_copy(index).wait()
        half = lax.broadcasted_iota(jnp.int32, (relay, 2 * relay), 0)
        whole = lax.broadcasted_iota(jnp.int32, (relay, 2 * relay), 1)

        def body(part, carry):
            at = pl.ds(pl.multiple_of(index * raw_rows + part * relay, relay), relay)
            from_at = pl.ds(pl.multiple_of(part * relay, relay), relay)
            both = raw_ref[lax.rem(index, raw_slots), from_at].reshape(2 * relay, ff_local)
            for side in range(2):
                pick = (whole == 2 * half + side).astype(raw_ref.dtype)
                w_ref[at, side * ff_local : (side + 1) * ff_local] = jnp.dot(
                    pick, both, preferred_element_type=jnp.float32
                ).astype(w_ref.dtype)
            return carry

        lax.fori_loop(0, raw_rows // relay, body, 0)

        @pl.when(index + raw_slots < raw_steps)
        def _():
            raw_copy(index + raw_slots).start()

    cut = ff_both // 3

    def mix(turn, index):
        from_row = lax.rem(row + index // 2, chips)
        from_core = lax.rem(core + lax.rem(index, 2), 2)
        back = lax.rem(chips - index // 2, chips)

        @pl.when(lax.rem(index, 2) == 1)
        def _():
            def body(chunk, carry):
                over(back, turn * per_group + chunk, from_row, from_core).wait_recv()
                return carry

            lax.fori_loop(0, per_group, body, 0)

        block = from_row * 2 + from_core
        group = lax.rem(from_row + turn, chips)
        top = pl.multiple_of(group * group_rows, group_rows)
        left_at = pl.multiple_of(block * width, width)
        gain = gain_ref[:, pl.ds(left_at, width)].astype(jnp.float32)

        def scale(part, carry):
            here = pl.ds(pl.multiple_of(part * strip, strip), strip)
            at = pl.ds(pl.multiple_of(top + part * strip, strip), strip)
            value = full_ref[block, at, :].astype(jnp.float32)
            x_ref[here, :] = (value * gain).astype(x_ref.dtype)
            square = value * value
            total = square[:, :128]
            for start in range(128, width, 128):
                total = total + square[:, start : start + 128]
            ssq_ref[at, :] = ssq_ref[at, :] + total
            return carry

        lax.fori_loop(0, group_rows // strip, scale, 0)
        at = pl.ds(top, group_rows)

        def multiply(part, carry):
            wide = pl.ds(pl.multiple_of(part * cut, cut), cut)
            acc_ref[at, wide] = acc_ref[at, wide] + jnp.dot(
                x_ref[...], w_ref[pl.ds(left_at, width), wide], preferred_element_type=jnp.float32
            )
            return carry

        lax.fori_loop(0, ff_both // cut, multiply, 0)

    early = blocks * (chips - 1)

    def march(t, carry):
        @pl.when((t < count) & (lax.rem(t, per_seq) == 0))
        def _():
            partial(t // per_seq)

        here = t - donor * HOP

        @pl.when((here >= 0) & (here < count))
        def _():
            @pl.when(donor == 0)
            def _():
                r_out[here] = p_rows(here).astype(r_out.dtype)

            @pl.when(donor > 0)
            def _():
                right(here).wait_recv()

            @pl.when((donor > 0) & (donor < last))
            def _():
                r_out[here] = (p_rows(here) + r_in[here].astype(jnp.float32)).astype(r_out.dtype)

            @pl.when(donor < last)
            def _():
                right(here).start()

        there = t - (last - donor) * HOP

        @pl.when((there >= 0) & (there < count))
        def _():
            @pl.when(donor == last)
            def _():
                l_out[there] = p_rows(there).astype(l_out.dtype)

            @pl.when(donor < last)
            def _():
                left(there).wait_recv()

            @pl.when((donor > 0) & (donor < last))
            def _():
                l_out[there] = (p_rows(there) + l_in[there].astype(jnp.float32)).astype(l_out.dtype)

            @pl.when(donor > 0)
            def _():
                left(there).start()

        done = t - reach

        @pl.when((done >= 0) & (done < count))
        def _():
            goal = tile(row, core, done)

            @pl.when(donor == 0)
            def _():
                goal[...] = (p_rows(done) + l_in[done].astype(jnp.float32)).astype(goal.dtype)

            @pl.when(donor == last)
            def _():
                goal[...] = (p_rows(done) + r_in[done].astype(jnp.float32)).astype(goal.dtype)

            @pl.when((donor > 0) & (donor < last))
            def _():
                goal[...] = (
                    p_rows(done) + r_in[done].astype(jnp.float32) + l_in[done].astype(jnp.float32)
                ).astype(goal.dtype)

            for step in range(1, chips):
                across(step, done, row, lax.rem(row + step, chips) * 2 + core).start()
            over(0, done, row, core).start()

        came = t - reach - lag

        @pl.when((came >= 0) & (came < count))
        def _():
            for step in range(1, chips):
                from_row = lax.rem(row + chips - step, chips)
                across(step, came, from_row, from_row * 2 + core).wait_recv()
                over(step, came, from_row, core).start()

        @pl.when(t < raw_steps)
        def _():
            relay_weights(t)

        ready = t - reach - first_mix

        @pl.when((ready >= 0) & (ready < early))
        def _():
            mix(ready // blocks, lax.rem(ready, blocks))

        return carry

    steps = count + last * HOP + lag
    lax.fori_loop(0, steps, march, 0)

    def rest(index, carry):
        mix(index // blocks, lax.rem(index, blocks))
        return carry

    lax.fori_loop(jnp.minimum(steps - reach - first_mix, early), early, rest, 0)
    own_copies[2].wait()

    for step in range(1, blocks):
        back = lax.rem(mine + blocks - step, blocks)
        send(
            gates_out.at[step], gates_in.at[back], g_send, g_recv, step - 1, expert=back
        ).wait_recv()

    def activate(group):
        for side in range(2):
            seq = group * 2 + side
            gates_ref[side * suffix : (side + 1) * suffix, :] = jnp.sum(
                jnp.where(eye, gates_in[seq][:1, :], 0.0), axis=1, keepdims=True
            )

        def body(part, carry):
            at = pl.ds(pl.multiple_of(group * group_rows + part * strip, strip), strip)
            here = pl.ds(pl.multiple_of(part * strip, strip), strip)
            mean = jnp.sum(ssq_ref[at, :], axis=1, keepdims=True) * (1.0 / model_width)
            inverse = lax.rsqrt(mean + 1e-06)
            gate = acc_ref[at, :ff_local] * inverse
            up = acc_ref[at, ff_local:] * inverse
            value = gate / (1.0 + jnp.exp(-gate)) * up * gates_ref[here, :]
            act_ref[at, :] = value.astype(act_ref.dtype)
            return carry

        lax.fori_loop(0, group_rows // strip, body, 0)

    def target(rank):
        low = jnp.minimum(donor, last - donor)
        single = jnp.maximum(donor, last - donor) - low
        rest_rank = rank - single
        gap = low - rest_rank // 2
        side = 1 - 2 * lax.rem(jnp.maximum(rest_rank, 0), 2)
        paired = donor + side * gap
        lone = jnp.where(donor < last - donor, last - rank, rank)
        return jnp.where(rank == last, donor, jnp.where(rank < single, lone, paired))

    def add(out, *terms):
        def body(part, carry):
            at = pl.ds(pl.multiple_of(part * strip, strip), strip)
            value = terms[0][at, :].astype(jnp.float32)
            for term in terms[1:]:
                value = value + term[at, :].astype(jnp.float32)
            out[at, :] = value.astype(out.dtype)
            return carry

        lax.fori_loop(0, suffix // strip, body, 0)

    order = list(range(1, chips)) + [0]

    def own_half(slot):
        return part_ref.at[slot, pl.ds(pl.multiple_of(core * suffix, suffix), suffix)]

    def swap(slot):
        away = part_ref.at[slot, pl.ds(pl.multiple_of((1 - core) * suffix, suffix), suffix)]
        return send(away, c_in.at[slot], cc_send, cc_recv, slot, expert=beside)

    def cross(hop, to):
        return send(y_out.at[hop], y_in.at[hop], yy_send, yy_recv, hop, expert=to)

    def produce(step, rank):
        slot = step * donors + rank
        top = pl.multiple_of(lax.rem(row + step, chips) * group_rows, group_rows)
        left_at = pl.multiple_of(target(rank) * columns, columns)
        part_ref[slot] = jnp.dot(
            act_ref[pl.ds(top, group_rows), :],
            down_ref[:, pl.ds(left_at, columns)],
            preferred_element_type=jnp.float32,
        ).astype(part_ref.dtype)
        swap(slot).start()

    def pass_on(step, rank):
        slot = step * donors + rank
        hop = (step - 1) * donors + rank
        swap(slot).wait_recv()
        add(y_out.at[hop], own_half(slot), c_in.at[slot])
        cross(hop, lax.rem(row + step, chips) * 2 + core).start()

    for step in order:
        for side in range(2):
            mix(chips - 1, 2 * ((step + 1) % chips) + side)
        activate(lax.rem(row + step, chips))
        if step:

            def body(rank, carry):
                produce(step, rank)

                @pl.when(rank > 0)
                def _():
                    pass_on(step, rank - 1)

                return carry

            lax.fori_loop(0, donors, body, 0)
            pass_on(step, donors - 1)
        else:

            def body(rank, carry):
                produce(0, rank)
                return carry

            lax.fori_loop(0, donors, body, 0)

    def shift_right(goal):
        return send(zr_out.at[goal], zr_in.at[goal], zr_send, zr_recv, goal, donor=donor + 1)

    def shift_left(goal):
        return send(zl_out.at[goal], zl_in.at[goal], zl_send, zl_recv, goal, donor=donor - 1)

    def finish(rank, carry):
        goal = target(rank)
        swap(rank).wait_recv()
        terms = [own_half(rank), c_in.at[rank]]
        for step in range(1, chips):
            hop = (step - 1) * donors + rank
            cross(hop, mine).wait_recv()
            terms.append(y_in.at[hop])

        @pl.when((goal >= donor) & (donor > 0))
        def _():
            shift_right(goal).wait_recv()

        @pl.when((goal <= donor) & (donor < last))
        def _():
            shift_left(goal).wait_recv()

        @pl.when(goal > donor)
        def _():
            @pl.when(donor == 0)
            def _():
                add(zr_out.at[goal], *terms)

            @pl.when(donor > 0)
            def _():
                add(zr_out.at[goal], zr_in.at[goal], *terms)

            shift_right(goal).start()

        @pl.when(goal < donor)
        def _():
            @pl.when(donor == last)
            def _():
                add(zl_out.at[goal], *terms)

            @pl.when(donor < last)
            def _():
                add(zl_out.at[goal], zl_in.at[goal], *terms)

            shift_left(goal).start()

        @pl.when(goal == donor)
        def _():
            def close(ends):
                for part in range(columns // width):
                    wide = slice(part * width, (part + 1) * width)

                    def body(index, carry):
                        at = pl.ds(pl.multiple_of(index * strip, strip), strip)
                        down = pl.ds(pl.multiple_of(mine * suffix + index * strip, strip), strip)
                        value = full_ref[donor * (columns // width) + part, down, :].astype(jnp.float32)
                        total = terms[0][at, wide].astype(jnp.float32)
                        for term in terms[1:] + ends:
                            total = total + term[at, wide].astype(jnp.float32)
                        out_ref[at, wide] = (value + total).astype(out_ref.dtype)
                        return carry

                    lax.fori_loop(0, suffix // strip, body, 0)

            @pl.when(donor == 0)
            def _():
                close([zl_in.at[donor]])

            @pl.when(donor == last)
            def _():
                close([zr_in.at[donor]])

            @pl.when((donor > 0) & (donor < last))
            def _():
                close([zl_in.at[donor], zr_in.at[donor]])

        return carry

    lax.fori_loop(0, donors, finish, 0)

    for step in range(1, blocks):
        gates_to(step).wait_send()
    for index in range(seqs_each):

        @pl.when(partner(index) != mine)
        def _():
            hidden_to(index).wait_send()

    for step in range(1, chips):
        heads_y(step, mine, mine).wait_send()
    for step in range(chips):
        heads_c(step, mine).wait_send()

    def drain(chunk, carry):
        @pl.when(donor < last)
        def _():
            right(chunk).wait_send()

        @pl.when(donor > 0)
        def _():
            left(chunk).wait_send()

        for step in range(1, chips):
            across(step, chunk, row, mine).wait_send()
        for step in range(chips):
            over(step, chunk, row, core).wait_send()
        return carry

    lax.fori_loop(0, count, drain, 0)

    def drain_blocks(goal, carry):
        for step in range(chips):
            swap(step * donors + goal).wait_send()
        for step in range(1, chips):
            cross((step - 1) * donors + goal, mine).wait_send()

        @pl.when(goal > donor)
        def _():
            shift_right(goal).wait_send()

        @pl.when(goal < donor)
        def _():
            shift_left(goal).wait_send()

        return carry

    lax.fori_loop(0, donors, drain_blocks, 0)


def page_kernel(
    experts,
    donors,
    pool_ref,
    held_ref,
    bias_ref,
    query_ref,
    fresh_ref,
    head_ref,
    out_buf,
    pages_in,
    sends,
    recvs,
):
    expert, donor = lax.axis_index("expert"), lax.axis_index("donor")
    seqs, kv_heads = out_buf.shape[0], out_buf.shape[1]
    suffix, columns = head_ref.shape
    head_dim = fresh_ref.shape[1] // 2
    order = [
        (step_e, step_z)
        for step_z in [*far_first(donors), 0]
        for step_e in range(experts)
        if step_e or step_z
    ]
    barrier = pltpu.get_barrier_semaphore()

    def ahead(step_e, step_z):
        return lax.rem(expert + step_e, experts), lax.rem(donor + step_z, donors)

    for step_e, step_z in order:
        to_e, to_z = ahead(step_e, step_z)
        pl.semaphore_signal(
            barrier, inc=1, device_id={"expert": to_e, "donor": to_z}, device_id_type=MESH
        )
    for seq in range(seqs):
        for group in range(kv_heads):
            out_buf[seq, group] = pool_ref[held_ref[seq], group]
    pl.semaphore_wait(barrier, experts * donors - 1)
    mine = expert * donors + donor

    def page(step_e, step_z):
        to_e, to_z = ahead(step_e, step_z)
        return send(
            out_buf.at[to_e, to_z * kv_heads // donors],
            pages_in.at[mine],
            sends,
            recvs,
            step_e * donors + step_z,
            expert=to_e,
            donor=to_z,
        )

    for step_e, step_z in order:
        page(step_e, step_z).start()
    pages_in[mine] = out_buf[expert, donor * kv_heads // donors]
    for step_e, step_z in order:
        from_e, from_z = ahead(experts - step_e, donors - step_z)
        send(
            out_buf.at[expert, donor * kv_heads // donors],
            pages_in.at[from_e * donors + from_z],
            sends,
            recvs,
            step_e * donors + step_z,
            expert=from_e,
            donor=from_z,
        ).wait_recv()
    keys_count = pages_in.shape[0] * pages_in.shape[1]
    causal = lax.broadcasted_iota(jnp.int32, (suffix, suffix), 0) >= lax.broadcasted_iota(
        jnp.int32, (suffix, suffix), 1
    )
    scale = head_dim ** (-0.5)
    both = (((1,), (1,)), ((), ()))
    for left in range(0, columns, head_dim):
        query = query_ref[:, left : left + head_dim]
        old_keys = pages_in[:, :, :head_dim].reshape(keys_count, head_dim)
        old = lax.dot_general(query, old_keys, both, preferred_element_type=jnp.float32)
        new = lax.dot_general(
            query, fresh_ref[:, :head_dim], both, preferred_element_type=jnp.float32
        )
        old = old * scale + bias_ref[...]
        new = jnp.where(causal, new * scale, -jnp.inf)
        top = jnp.maximum(
            jnp.max(old, axis=1, keepdims=True), jnp.max(new, axis=1, keepdims=True)
        )
        old = jnp.exp(old - top)
        new = jnp.exp(new - top)
        total = jnp.sum(old, axis=1, keepdims=True) + jnp.sum(new, axis=1, keepdims=True)
        old_vals = pages_in[:, :, head_dim:].reshape(keys_count, head_dim)
        mixed = jnp.dot(old.astype(query.dtype), old_vals, preferred_element_type=jnp.float32)
        mixed = mixed + jnp.dot(
            new.astype(query.dtype), fresh_ref[:, head_dim:], preferred_element_type=jnp.float32
        )
        head_ref[:, left : left + head_dim] = (mixed / total).astype(head_ref.dtype)
    for step_e, step_z in order:
        page(step_e, step_z).wait_send()


def page_heads(pool, held, bias, queries, fresh, experts, donors):
    seqs, kv_heads, page_len, both = pool.shape
    dma = pltpu.SemaphoreType.DMA
    inside = pl.BlockSpec(memory_space=pltpu.VMEM)
    return pl.pallas_call(
        functools.partial(page_kernel, experts, donors),
        out_shape=jax.ShapeDtypeStruct(queries.shape, queries.dtype),
        in_specs=[inside, pl.BlockSpec(memory_space=pltpu.SMEM)] + [inside] * 3,
        out_specs=inside,
        scratch_shapes=[
            pltpu.VMEM((seqs, kv_heads, page_len, both), pool.dtype),
            pltpu.VMEM((experts * donors, page_len, both), pool.dtype),
            dma((experts * donors,)),
            dma((experts * donors,)),
        ],
        compiler_params=pltpu.CompilerParams(collective_id=4, has_side_effects=True),
        name="page_heads",
    )(pool, held, bias, queries, fresh)


def mix_scratch(heads, out_weight, w_gate_up, chips, donors, piece):
    suffix, head_cols = heads.shape
    blocks = 2 * chips
    width = out_weight.shape[1]
    model_width, ff_local = w_gate_up.shape[1], w_gate_up.shape[3]
    tokens = blocks * suffix
    columns = model_width // donors
    count = tokens // piece
    kind = heads.dtype
    vmem = lambda *shape: pltpu.VMEM(shape, kind)
    wide = lambda *shape: pltpu.VMEM(shape, jnp.float32)
    held = lambda number: pltpu.VMEM((number, suffix, columns), kind)
    return [
        vmem(blocks // donors, suffix, width),
        wide(blocks, 8, suffix),
        wide(blocks, 8, suffix),
        vmem(head_cols, width),
        vmem(3, model_width // 8, 2, ff_local),
        vmem(ff_local, model_width),
        vmem(tokens, head_cols),
        wide(tokens, width),
        vmem(count, piece, width),
        vmem(count, piece, width),
        vmem(count, piece, width),
        vmem(count, piece, width),
        vmem(blocks, tokens, width),
        vmem(model_width, 2 * ff_local),
        vmem(2 * suffix, width),
        wide(tokens, 2 * ff_local),
        wide(tokens, 128),
        vmem(tokens, ff_local),
        wide(2 * suffix, 1),
        vmem(chips * donors, 2 * suffix, columns),
        held(chips * donors),
        held((chips - 1) * donors),
        held((chips - 1) * donors),
        held(donors),
        held(donors),
        held(donors),
        held(donors),
    ]


def mix_blocks(
    heads, gain, probs, ids, hidden, out_weight, w_gate_up, w_down, chips, donors, piece, scratch
):
    suffix = heads.shape[0]
    columns = w_gate_up.shape[1] // donors
    count = 2 * chips * suffix // piece
    dma = pltpu.SemaphoreType.DMA
    pair = lambda number: [dma((number,)), dma((number,))]
    inside = pl.BlockSpec(memory_space=pltpu.VMEM)
    outside = pl.BlockSpec(memory_space=pl.ANY)
    return pl.pallas_call(
        functools.partial(mix_kernel, chips, donors, piece),
        out_shape=jax.ShapeDtypeStruct((suffix, columns), heads.dtype),
        in_specs=[inside] * 4 + [outside] * 4,
        out_specs=inside,
        scratch_shapes=scratch
        + [dma((3,)), dma((8,))]
        + pair(2 * chips - 1)
        + pair(2 * chips // donors)
        + pair(chips - 1)
        + pair(chips)
        + pair(count)
        + pair(count)
        + pair((chips - 1) * count)
        + pair(chips * count)
        + pair(chips * donors)
        + pair((chips - 1) * donors)
        + pair(donors)
        + pair(donors),
        compiler_params=pltpu.CompilerParams(
            collective_id=3, has_side_effects=True, vmem_limit_bytes=VMEM_BYTES
        ),
        name="mix_blocks",
    )(heads, gain, probs, ids, hidden, out_weight, w_gate_up, w_down)


def shards(
    hidden_in,
    queries,
    suffix_kv,
    kv_pool,
    page_table,
    prefix_len,
    out_weight,
    norm_gain,
    expert_ids,
    route_probs,
    w_gate_up,
    w_down,
):
    n_expert = lax.axis_size("expert")
    n_donor = lax.axis_size("donor")
    expert_index = lax.axis_index("expert")
    donor_index = lax.axis_index("donor")
    share_count = n_donor // 2
    seq_count, page_count = page_table.shape
    suffix_len = queries.shape[0]
    kv_heads = suffix_kv.shape[1]
    head_dim = suffix_kv.shape[2] // 2
    page_len = kv_pool.shape[2]
    model_width = hidden_in.shape[1]
    columns = model_width // n_donor
    experts_all = 2 * n_expert
    ff_local = w_gate_up.shape[3]
    my_group = donor_index * kv_heads // n_donor
    owner_index = expert_index * n_donor + donor_index
    owner_of = page_table // seq_count
    held_slot = jnp.sum(jnp.where(owner_of == owner_index, page_table % seq_count, 0), axis=1)
    chips = n_expert // 2
    my_pair = lax.dynamic_index_in_dim(suffix_kv, my_group, 1, keepdims=False)
    scratch = mix_scratch(queries, out_weight, w_gate_up, chips, n_donor, PIECE)
    held_bytes = sum(math.prod(item.shape) * item.dtype.itemsize for item in scratch)
    if held_bytes <= VMEM_BYTES - 4 * 1024 * 1024:
        is_mine = (jnp.arange(seq_count) == expert_index)[:, None]
        owned = owner_of[:, :, None] == jnp.arange(n_expert * n_donor)
        place_of = jnp.arange(page_count)[None, :, None]
        first = page_len * jnp.sum(jnp.where(owned & is_mine[:, :, None], place_of, 0), axis=(0, 1))
        length = jnp.sum(jnp.where(is_mine[:, 0], prefix_len, 0))
        seen = first[:, None] + jnp.arange(page_len) < length
        bias = jnp.where(seen, 0.0, -jnp.inf).astype(jnp.float32).reshape(1, -1)
        head_out = page_heads(kv_pool, held_slot, bias, queries, my_pair, n_expert, n_donor)
        layer_out = mix_blocks(
            head_out,
            norm_gain.reshape(1, model_width),
            route_probs,
            expert_ids,
            hidden_in,
            out_weight,
            w_gate_up,
            w_down,
            chips,
            n_donor,
            PIECE,
            scratch,
        )
        return (layer_out, head_out)

    dest_group = jnp.arange(n_donor, dtype=jnp.int32) * kv_heads // n_donor
    wanted = (held_slot[:, None] * kv_heads + dest_group[None, :]).reshape(-1)
    outgoing = jnp.take(
        kv_pool.reshape(seq_count * kv_heads, page_len, 2 * head_dim), wanted, axis=0
    )
    arrived = lax.all_to_all(outgoing, ("expert", "donor"), split_axis=0, concat_axis=0, tiled=True)
    my_owners = lax.dynamic_index_in_dim(owner_of, expert_index, 0, keepdims=False)
    ordered = jnp.take(arrived, my_owners, axis=0).reshape(page_count * page_len, 2 * head_dim)
    prefix_keys = ordered[:, :head_dim]
    prefix_vals = ordered[:, head_dim:]
    score_scale = head_dim ** (-0.5)
    query_heads = queries.reshape(suffix_len, -1, head_dim)
    fresh_pair = lax.dynamic_index_in_dim(suffix_kv, my_group, 1, keepdims=False)
    causal = jnp.arange(suffix_len)[:, None] >= jnp.arange(suffix_len)[None, :]
    fresh_scores = (
        jnp.einsum(
            "thc,uc->thu", query_heads, fresh_pair[:, :head_dim], preferred_element_type=jnp.float32
        )
        * score_scale
    )
    fresh_scores = jnp.where(causal[:, None, :], fresh_scores, -jnp.inf)
    prefix_tokens = lax.dynamic_index_in_dim(prefix_len, expert_index, 0, keepdims=False)
    block_keys = min(1024, page_count * page_len)
    live_blocks = (prefix_tokens + block_keys - 1) // block_keys

    def block_scores(block_index):
        keys_block = lax.dynamic_slice_in_dim(prefix_keys, block_index * block_keys, block_keys, 0)
        raw_scores = (
            jnp.einsum("thc,kc->thk", query_heads, keys_block, preferred_element_type=jnp.float32)
            * score_scale
        )
        visible = block_index * block_keys + jnp.arange(block_keys) < prefix_tokens
        return jnp.where(visible[None, None, :], raw_scores, -jnp.inf)

    def raise_max(block_index, running):
        return jnp.maximum(running, jnp.max(block_scores(block_index), axis=2))

    row_max = lax.fori_loop(0, live_blocks, raise_max, jnp.max(fresh_scores, axis=2))

    def add_block(block_index, loop_state):
        row_total, weighted = loop_state
        exp_scores = jnp.exp(block_scores(block_index) - row_max[:, :, None])
        vals_block = lax.dynamic_slice_in_dim(prefix_vals, block_index * block_keys, block_keys, 0)
        weighted = weighted + jnp.einsum(
            "thk,kc->thc",
            exp_scores.astype(jnp.bfloat16),
            vals_block,
            preferred_element_type=jnp.float32,
        )
        return (row_total + jnp.sum(exp_scores, axis=2), weighted)

    fresh_exp = jnp.exp(fresh_scores - row_max[:, :, None])
    start_state = (
        jnp.sum(fresh_exp, axis=2),
        jnp.einsum(
            "thu,uc->thc",
            fresh_exp.astype(jnp.bfloat16),
            fresh_pair[:, head_dim:],
            preferred_element_type=jnp.float32,
        ),
    )
    row_total, weighted = lax.fori_loop(0, live_blocks, add_block, start_state)
    head_out = (weighted / row_total[:, :, None]).astype(jnp.bfloat16).reshape(suffix_len, -1)
    gate_weights = route_probs / jnp.sum(route_probs, axis=1, keepdims=True)
    chosen = expert_ids[:, :, None] == jnp.arange(experts_all, dtype=jnp.int32)
    gate_table = jnp.sum(jnp.where(chosen, gate_weights[:, :, None], 0.0), axis=1)
    gate_tables = [gate_table]
    for step in range(1, n_expert):
        pairs = [(source, (source + step) % n_expert) for source in range(n_expert)]
        gate_tables.append(lax.ppermute(gate_table, "expert", pairs))
    from_order = lax.rem(expert_index - jnp.arange(n_expert) + n_expert, n_expert)
    gate_all = jnp.stack(gate_tables)[from_order].reshape(n_expert * suffix_len, experts_all)
    my_expert = owner_index // share_count
    my_gates = lax.dynamic_slice_in_dim(gate_all, my_expert, 1, 1)

    seqs_each = n_expert // n_donor
    width = model_width // n_expert
    hidden_parts = []
    for shift in range(seqs_each):
        pairs = []
        for source in range(n_expert * n_donor):
            seq, part = source // n_donor, source % n_donor
            target = part * seqs_each + (seq + shift) % seqs_each
            pairs.append((source, target * n_donor + seq // seqs_each))
        target = donor_index * seqs_each + lax.rem(expert_index + shift, seqs_each)
        sent = lax.dynamic_slice_in_dim(hidden_in, target * width, width, 1)
        hidden_parts.append(lax.ppermute(sent, ("expert", "donor"), pairs))
    turned = lax.rem(expert_index - jnp.arange(seqs_each) + seqs_each * n_expert, seqs_each)
    hidden_block = jnp.stack(hidden_parts)[turned].reshape(seqs_each * suffix_len, width)

    heads_all = lax.all_gather(head_out, "expert", axis=0, tiled=True)
    w_in, heads_all = lax.optimization_barrier(
        (w_gate_up[0].reshape(model_width, 2 * ff_local), heads_all)
    )
    resid = gather_blocks(heads_all, out_weight, hidden_block, n_expert // 2, n_donor)
    resid_f = resid.astype(jnp.float32)
    inverse = lax.rsqrt(jnp.mean(resid_f * resid_f, axis=1, keepdims=True) + 1e-06)
    normed = (resid_f * inverse * norm_gain.astype(jnp.float32)).astype(jnp.bfloat16)
    gate_up = jnp.dot(
        normed,
        w_in,
        preferred_element_type=jnp.float32,
    )
    activated = (
        jax.nn.silu(gate_up[:, :ff_local]) * gate_up[:, ff_local:] * my_gates
    ).astype(jnp.bfloat16)
    expert_mix = reduce_blocks(activated, w_down[0], n_expert // 2, n_donor)
    resid_mine = lax.dynamic_slice(
        resid,
        (expert_index * suffix_len, donor_index * columns),
        (suffix_len, columns),
    )
    layer_out = (resid_mine.astype(jnp.float32) + expert_mix).astype(
        jnp.bfloat16
    )
    return (layer_out, head_out)


def solution(mesh):
    in_specs = (
        P(("groups", "expert"), None),
        P(("groups", "expert"), "donor"),
        P(("groups", "expert"), None, None),
        P(("groups", "expert", "donor"), None, None, None),
        P("groups", None),
        P("groups"),
        P("donor", "expert"),
        P(),
        P(("groups", "expert"), None),
        P(("groups", "expert"), None),
        P(("expert", "donor"), None, None, None),
        P(("expert", "donor"), None, None),
    )
    out_specs = (P(("groups", "expert"), "donor"), P(("groups", "expert"), "donor"))
    return jax.shard_map(shards, mesh=mesh, in_specs=in_specs, out_specs=out_specs, check_vma=False)
```

```python
import functools
import math

import jax
import jax.numpy as jnp
from jax import lax
from jax.experimental import pallas as pl
from jax.experimental.pallas import tpu as pltpu
from jax.sharding import PartitionSpec as P

MESH = pl.DeviceIdType.MESH
VMEM_BYTES = 60 * 1024 * 1024
PIECE = 32
HOP = 3
LAG = 3


def place():
    expert = lax.axis_index("expert")
    return expert // 2, lax.rem(expert, 2), lax.axis_index("donor")


def send(src, dst, sends, recvs, slot, **where):
    return pltpu.make_async_remote_copy(
        src_ref=src,
        dst_ref=dst,
        send_sem=sends.at[slot],
        recv_sem=recvs.at[slot],
        device_id=where,
        device_id_type=MESH,
    )


def greet(chips, donors):
    row, core, donor = place()
    barrier = pltpu.get_barrier_semaphore()
    pl.semaphore_signal(
        barrier, inc=1, device_id={"expert": row * 2 + 1 - core}, device_id_type=MESH
    )
    for step in range(1, chips):
        other = lax.rem(row + step, chips) * 2 + core
        pl.semaphore_signal(barrier, inc=1, device_id={"expert": other}, device_id_type=MESH)
    for step in range(1, donors):
        other = lax.rem(donor + step, donors)
        pl.semaphore_signal(barrier, inc=1, device_id={"donor": other}, device_id_type=MESH)
    pl.semaphore_wait(barrier, chips + donors - 1)


def far_first(donors):
    return sorted(range(1, donors), key=lambda k: (-min(k, donors - k), k))


def gather_kernel(
    chips,
    donors,
    heads_ref,
    out_ref,
    hidden_ref,
    full_ref,
    terms_ref,
    terms_in,
    block_ref,
    own_sem,
    t_send,
    t_recv,
    z_send,
    z_recv,
    y_send,
    y_recv,
    c_send,
    c_recv,
):
    row, core, donor = place()
    rows, cols = block_ref.shape
    greet(chips, donors)
    strip = 16

    def project(step_z, slot):
        top = pl.multiple_of(lax.rem(donor + step_z, donors) * rows, rows)
        terms_ref[slot] = jnp.dot(
            heads_ref[pl.ds(top, rows), :], out_ref[...], preferred_element_type=jnp.float32
        ).astype(terms_ref.dtype)

    term_copies = {}
    for step in far_first(donors):
        project(step, step)
        copy = send(
            terms_ref.at[step],
            terms_in.at[step - 1],
            t_send,
            t_recv,
            step - 1,
            donor=lax.rem(donor + step, donors),
        )
        copy.start()
        term_copies[step] = copy
    project(0, 0)
    for step in far_first(donors):
        term_copies[step].wait_recv()

    def add(index, carry):
        at = pl.ds(pl.multiple_of(index * strip, strip), strip)
        value = terms_ref[0, at, :].astype(jnp.float32)
        for step in range(1, donors):
            value = value + terms_in[step - 1, at, :].astype(jnp.float32)
        value = value + hidden_ref[at, :].astype(jnp.float32)
        block_ref[at, :] = value.astype(block_ref.dtype)
        return carry

    lax.fori_loop(0, rows // strip, add, 0)

    def slot_of(donor_from, row_from, core_from):
        top = pl.multiple_of(donor_from * rows, rows)
        left = pl.multiple_of((row_from * 2 + core_from) * cols, cols)
        return full_ref.at[pl.ds(top, rows), pl.ds(left, cols)]

    own = pltpu.make_async_copy(block_ref, slot_of(donor, row, core), own_sem)
    own.start()
    started = []

    def along_y(src, step_z, donor_from):
        for step in range(1, chips):
            copy = send(
                src,
                slot_of(donor_from, row, core),
                y_send,
                y_recv,
                step_z * (chips - 1) + step - 1,
                expert=lax.rem(row + step, chips) * 2 + core,
            )
            copy.start()
            started.append(copy)

    def beside(src, step_z, step_y, donor_from, row_from):
        copy = send(
            src,
            slot_of(donor_from, row_from, core),
            c_send,
            c_recv,
            step_z * chips + step_y,
            expert=row * 2 + 1 - core,
        )
        copy.start()
        started.append(copy)

    along_y(block_ref, 0, donor)
    z_copies = {}
    near_first = far_first(donors)[::-1]
    for step in near_first:
        copy = send(
            block_ref,
            slot_of(donor, row, core),
            z_send,
            z_recv,
            step - 1,
            donor=lax.rem(donor + step, donors),
        )
        copy.start()
        z_copies[step] = copy
    beside(block_ref, 0, 0, donor, row)

    def take_y(step_z, donor_from):
        for step in range(1, chips):
            row_from = lax.rem(row + chips - step, chips)
            there = slot_of(donor_from, row_from, core)
            send(
                there,
                there,
                y_send,
                y_recv,
                step_z * (chips - 1) + step - 1,
                expert=row_from * 2 + core,
            ).wait_recv()
            beside(there, step_z, step, donor_from, row_from)

    for step in near_first:
        donor_from = lax.rem(donor + donors - step, donors)
        there = slot_of(donor_from, row, core)
        send(there, there, z_send, z_recv, step - 1, donor=donor_from).wait_recv()
        along_y(there, step, donor_from)
        beside(there, step, 0, donor_from, row)
    for step in [0] + near_first:
        take_y(step, lax.rem(donor + donors - step, donors))
    for step_z in range(donors):
        donor_from = lax.rem(donor + donors - step_z, donors)
        for step_y in range(chips):
            row_from = lax.rem(row + chips - step_y, chips)
            there = slot_of(donor_from, row_from, 1 - core)
            send(
                there, there, c_send, c_recv, step_z * chips + step_y, expert=row * 2 + 1 - core
            ).wait_recv()
    own.wait()
    for copy in list(term_copies.values()) + list(z_copies.values()) + started:
        copy.wait_send()


def gather_blocks(heads, out_weight, block, chips, donors):
    rows, cols = block.shape
    dma = pltpu.SemaphoreType.DMA
    return pl.pallas_call(
        functools.partial(gather_kernel, chips, donors),
        out_shape=jax.ShapeDtypeStruct((rows * donors, cols * chips * 2), block.dtype),
        in_specs=[pl.BlockSpec(memory_space=pltpu.VMEM)] * 3,
        out_specs=pl.BlockSpec(memory_space=pltpu.VMEM),
        scratch_shapes=[
            pltpu.VMEM((donors, rows, cols), block.dtype),
            pltpu.VMEM((donors - 1, rows, cols), block.dtype),
            pltpu.VMEM((rows, cols), block.dtype),
            dma,
            dma((donors - 1,)),
            dma((donors - 1,)),
            dma((donors - 1,)),
            dma((donors - 1,)),
            dma((donors * (chips - 1),)),
            dma((donors * (chips - 1),)),
            dma((donors * chips,)),
            dma((donors * chips,)),
        ],
        compiler_params=pltpu.CompilerParams(collective_id=1, has_side_effects=True),
        name="gather_blocks",
    )(heads, out_weight, block)


def reduce_kernel(
    chips,
    donors,
    act_ref,
    down_ref,
    total_ref,
    part_ref,
    c_in,
    y_out,
    y_in,
    z_out,
    z_in,
    c_send,
    c_recv,
    y_send,
    y_recv,
    z_send,
    z_recv,
):
    row, core, donor = place()
    rows, cols = total_ref.shape
    greet(chips, donors)
    order = far_first(donors) + [0]
    strip = 16

    def tile(row_to, core_to, step_z):
        top = pl.multiple_of((row_to * 2 + core_to) * rows, rows)
        left = pl.multiple_of(lax.rem(donor + step_z, donors) * cols, cols)
        return part_ref.at[pl.ds(top, rows), pl.ds(left, cols)]

    def add(out, *terms):
        def body(index, carry):
            at = pl.ds(pl.multiple_of(index * strip, strip), strip)
            value = terms[0][at, :].astype(jnp.float32)
            for term in terms[1:]:
                value = value + term[at, :].astype(jnp.float32)
            out[at, :] = value.astype(out.dtype)
            return carry

        lax.fori_loop(0, rows // strip, body, 0)

    started = []
    arrivals = {}

    def multiply(step_z):
        left = pl.multiple_of(lax.rem(donor + step_z, donors) * cols, cols)

        def body(index, carry):
            at = pl.ds(pl.multiple_of(index * rows, rows), rows)
            part_ref[at, pl.ds(left, cols)] = jnp.dot(
                act_ref[at, :],
                down_ref[:, pl.ds(left, cols)],
                preferred_element_type=jnp.float32,
            ).astype(part_ref.dtype)
            return carry

        lax.fori_loop(0, chips * 2, body, 0)

    def beside(step_z):
        for step_y in range(chips - 1, -1, -1):
            slot = step_z * chips + step_y
            copy = send(
                tile(lax.rem(row + step_y, chips), 1 - core, step_z),
                c_in.at[slot],
                c_send,
                c_recv,
                slot,
                expert=row * 2 + 1 - core,
            )
            copy.start()
            started.append(copy)

    def along_y(step_z):
        for step_y in range(chips - 1, 0, -1):
            row_to = lax.rem(row + step_y, chips)
            slot = step_z * chips + step_y
            send(
                c_in.at[slot], c_in.at[slot], c_send, c_recv, slot, expert=row * 2 + 1 - core
            ).wait_recv()
            hop = step_z * (chips - 1) + step_y - 1
            add(y_out.at[hop], tile(row_to, core, step_z), c_in.at[slot])
            copy = send(
                y_out.at[hop], y_in.at[hop], y_send, y_recv, hop, expert=row_to * 2 + core
            )
            copy.start()
            arrivals[hop] = copy
            started.append(copy)

    for index, step_z in enumerate(order):
        multiply(step_z)
        beside(step_z)
        if index:
            along_y(order[index - 1])
    along_y(order[-1])
    for step_z in order:
        slot = step_z * chips
        send(
            c_in.at[slot], c_in.at[slot], c_send, c_recv, slot, expert=row * 2 + 1 - core
        ).wait_recv()
        terms = [tile(row, core, step_z), c_in.at[slot]]
        for step_y in range(1, chips):
            hop = step_z * (chips - 1) + step_y - 1
            arrivals[hop].wait_recv()
            terms.append(y_in.at[hop])
        if step_z:
            add(z_out.at[step_z - 1], *terms)
            copy = send(
                z_out.at[step_z - 1],
                z_in.at[step_z - 1],
                z_send,
                z_recv,
                step_z - 1,
                donor=lax.rem(donor + step_z, donors),
            )
            copy.start()
            arrivals["z", step_z] = copy
            started.append(copy)
        else:
            for step in order[:-1]:
                arrivals["z", step].wait_recv()
                terms.append(z_in.at[step - 1])
            add(total_ref, *terms)
    for copy in started:
        copy.wait_send()


def reduce_blocks(activated, down, chips, donors):
    rows, cols = activated.shape[0] // (chips * 2), down.shape[1] // donors
    dma = pltpu.SemaphoreType.DMA
    held = lambda count: pltpu.VMEM((count, rows, cols), activated.dtype)
    return pl.pallas_call(
        functools.partial(reduce_kernel, chips, donors),
        out_shape=jax.ShapeDtypeStruct((rows, cols), jnp.float32),
        in_specs=[pl.BlockSpec(memory_space=pltpu.VMEM)] * 2,
        out_specs=pl.BlockSpec(memory_space=pltpu.VMEM),
        scratch_shapes=[
            pltpu.VMEM((activated.shape[0], down.shape[1]), activated.dtype),
            held(donors * chips),
            held(donors * (chips - 1)),
            held(donors * (chips - 1)),
            held(donors - 1),
            held(donors - 1),
            dma((donors * chips,)),
            dma((donors * chips,)),
            dma((donors * (chips - 1),)),
            dma((donors * (chips - 1),)),
            dma((donors - 1,)),
            dma((donors - 1,)),
        ],
        compiler_params=pltpu.CompilerParams(collective_id=2, has_side_effects=True),
        name="reduce_blocks",
    )(activated, down)


def mix_kernel(
    chips,
    donors,
    piece,
    heads_in,
    gain_ref,
    probs_ref,
    ids_ref,
    hidden_hbm,
    outw_hbm,
    raw_hbm,
    down_hbm,
    out_ref,
    hidden_ref,
    gates_out,
    gates_in,
    gain_wide,
    outw_ref,
    raw_ref,
    down_ref,
    heads_ref,
    p_ref,
    r_out,
    r_in,
    l_out,
    l_in,
    full_ref,
    w_ref,
    x_ref,
    acc_ref,
    ssq_ref,
    act_ref,
    gates_ref,
    part_ref,
    c_in,
    y_out,
    y_in,
    zr_out,
    zr_in,
    zl_out,
    zl_in,
    local_sem,
    raw_sem,
    g_send,
    g_recv,
    h_send,
    h_recv,
    hy_send,
    hy_recv,
    hc_send,
    hc_recv,
    r_send,
    r_recv,
    l_send,
    l_recv,
    y_send,
    y_recv,
    c_send,
    c_recv,
    cc_send,
    cc_recv,
    yy_send,
    yy_recv,
    zr_send,
    zr_recv,
    zl_send,
    zl_recv,
):
    row, core, donor = place()
    mine = row * 2 + core
    beside = row * 2 + 1 - core
    suffix, head_cols = heads_in.shape
    blocks, tokens, width = full_ref.shape
    model_width, ff_both = w_ref.shape
    ff_local = ff_both // 2
    seqs_each = hidden_ref.shape[0]
    per_seq = suffix // piece
    count = blocks * per_seq
    per_group = count // chips
    group_rows = 2 * suffix
    columns = out_ref.shape[1]
    last = donors - 1
    lag = LAG
    first_mix = per_group + lag
    raw_steps, raw_slots, raw_rows = raw_sem.shape[0], raw_ref.shape[0], raw_ref.shape[1]
    relay = min(128, raw_rows)
    strip = 16

    own_copies = [
        pltpu.make_async_copy(outw_hbm, outw_ref, local_sem.at[0]),
        pltpu.make_async_copy(heads_in, heads_ref.at[pl.ds(mine * suffix, suffix)], local_sem.at[1]),
        pltpu.make_async_copy(down_hbm.at[0], down_ref, local_sem.at[2]),
    ]
    own_copies[0].start()
    own_copies[1].start()

    def raw_copy(index):
        at = pl.ds(pl.multiple_of(index * raw_rows, raw_rows), raw_rows)
        return pltpu.make_async_copy(
            raw_hbm.at[0, at], raw_ref.at[lax.rem(index, raw_slots)], raw_sem.at[index]
        )

    for index in range(raw_slots):
        raw_copy(index).start()
    own_copies[2].start()

    barrier = pltpu.get_barrier_semaphore()
    for step in range(1, blocks):
        other = lax.rem(mine + step, blocks)
        pl.semaphore_signal(barrier, inc=1, device_id={"expert": other}, device_id_type=MESH)

    @pl.when(donor > 0)
    def _():
        pl.semaphore_signal(barrier, inc=1, device_id={"donor": donor - 1}, device_id_type=MESH)

    @pl.when(donor < last)
    def _():
        pl.semaphore_signal(barrier, inc=1, device_id={"donor": donor + 1}, device_id_type=MESH)

    gain_wide[...] = gain_ref[...].astype(jnp.float32)
    acc_ref[...] = jnp.zeros_like(acc_ref)
    ssq_ref[...] = jnp.zeros_like(ssq_ref)
    pl.semaphore_wait(barrier, blocks - 1 + jnp.minimum(donor, 1) + jnp.minimum(last - donor, 1))

    def heads_of(seq):
        return heads_ref.at[pl.ds(pl.multiple_of(seq * suffix, suffix), suffix)]

    def heads_y(step, seq, to):
        return send(heads_of(seq), heads_of(seq), hy_send, hy_recv, step - 1, expert=to)

    def heads_c(slot, seq):
        return send(heads_of(seq), heads_of(seq), hc_send, hc_recv, slot, expert=beside)

    def gates_to(step):
        return send(
            gates_out.at[step],
            gates_in.at[mine],
            g_send,
            g_recv,
            step - 1,
            expert=lax.rem(mine + step, blocks),
        )

    def partner(index):
        return lax.rem(donor - lax.rem(mine, donors) + donors, donors) + donors * index

    def hidden_to(index):
        at = pl.ds(pl.multiple_of(partner(index) * width, width), width)
        slot = mine // donors
        return pltpu.make_async_remote_copy(
            src_ref=hidden_hbm.at[:, at],
            dst_ref=hidden_ref.at[slot],
            send_sem=h_send.at[index],
            recv_sem=h_recv.at[slot],
            device_id={"expert": partner(index)},
            device_id_type=MESH,
        )

    def hidden_own(index):
        at = pl.ds(pl.multiple_of(mine * width, width), width)
        return pltpu.make_async_copy(hidden_hbm.at[:, at], hidden_ref.at[index], h_recv.at[index])

    own_copies[1].wait()
    heads_c(0, mine).start()
    for step in range(1, chips):
        heads_y(step, mine, lax.rem(row + step, chips) * 2 + core).start()
    for index in range(seqs_each):

        @pl.when(partner(index) != mine)
        def _():
            hidden_to(index).start()

        @pl.when(partner(index) == mine)
        def _():
            hidden_own(index).start()

    square = (suffix, suffix)
    eye = lax.broadcasted_iota(jnp.int32, square, 0) == lax.broadcasted_iota(jnp.int32, square, 1)
    parts_of = donors // 2
    share = probs_ref[...] / jnp.sum(probs_ref[...], axis=0, keepdims=True)
    for step in range(blocks):
        named = (lax.rem(mine + step, blocks) * donors + donor) // parts_of
        line = jnp.sum(jnp.where(ids_ref[...] == named, share, 0.0), axis=0, keepdims=True)
        if step:
            gates_out[step] = jnp.broadcast_to(line, gates_out.shape[1:])
            gates_to(step).start()
        else:
            gates_in[mine] = jnp.broadcast_to(line, gates_out.shape[1:])
    own_copies[0].wait()

    def seq_at(from_row, from_core, index):
        return lax.rem(from_row + index // 2, chips) * 2 + lax.rem(from_core + lax.rem(index, 2), 2)

    def tile(from_row, from_core, chunk):
        seq = seq_at(from_row, from_core, chunk // per_seq)
        top = pl.multiple_of(seq * suffix + lax.rem(chunk, per_seq) * piece, piece)
        return full_ref.at[from_row * 2 + from_core, pl.ds(top, piece)]

    def right(chunk):
        return send(r_out.at[chunk], r_in.at[chunk], r_send, r_recv, chunk, donor=donor + 1)

    def left(chunk):
        return send(l_out.at[chunk], l_in.at[chunk], l_send, l_recv, chunk, donor=donor - 1)

    def across(step, chunk, from_row, to):
        there = tile(from_row, core, chunk)
        return send(there, there, y_send, y_recv, (step - 1) * count + chunk, expert=to)

    def over(step, chunk, from_row, from_core):
        there = tile(from_row, from_core, chunk)
        return send(there, there, c_send, c_recv, step * count + chunk, expert=beside)

    reach = jnp.maximum(donor, last - donor) * HOP

    def partial(index):
        seq = seq_at(row, core, index)
        step = index // 2

        @pl.when((index > 0) & (lax.rem(index, 2) == 0))
        def _():
            back = lax.rem(chips - step, chips)
            copy = send(
                heads_of(seq), heads_of(seq), hy_send, hy_recv, back - 1, expert=beside
            )
            copy.wait_recv()
            heads_c(back, seq).start()

        @pl.when(lax.rem(index, 2) == 1)
        def _():
            heads_c(lax.rem(chips - step, chips), seq).wait_recv()

        at = pl.ds(pl.multiple_of(index * suffix, suffix), suffix)
        p_ref[at, :] = jnp.dot(
            heads_ref[pl.ds(pl.multiple_of(seq * suffix, suffix), suffix), :],
            outw_ref[...],
            preferred_element_type=jnp.float32,
        )

        for index in range(seqs_each):

            @pl.when(partner(index) == seq)
            def _():
                hidden_own(index).wait()
                p_ref[at, :] = p_ref[at, :] + hidden_ref[index].astype(jnp.float32)

    def p_rows(chunk):
        return p_ref[pl.ds(pl.multiple_of(chunk * piece, piece), piece), :]

    def relay_weights(index):
        raw_copy(index).wait()
        half = lax.broadcasted_iota(jnp.int32, (relay, 2 * relay), 0)
        whole = lax.broadcasted_iota(jnp.int32, (relay, 2 * relay), 1)

        def body(part, carry):
            at = pl.ds(pl.multiple_of(index * raw_rows + part * relay, relay), relay)
            from_at = pl.ds(pl.multiple_of(part * relay, relay), relay)
            both = raw_ref[lax.rem(index, raw_slots), from_at].reshape(2 * relay, ff_local)
            for side in range(2):
                pick = (whole == 2 * half + side).astype(raw_ref.dtype)
                w_ref[at, side * ff_local : (side + 1) * ff_local] = jnp.dot(
                    pick, both, preferred_element_type=jnp.float32
                ).astype(w_ref.dtype)
            return carry

        lax.fori_loop(0, raw_rows // relay, body, 0)

        @pl.when(index + raw_slots < raw_steps)
        def _():
            raw_copy(index + raw_slots).start()

    cut = ff_both // 3

    def mix(turn, index):
        from_row = lax.rem(row + index // 2, chips)
        from_core = lax.rem(core + lax.rem(index, 2), 2)
        back = lax.rem(chips - index // 2, chips)

        @pl.when(lax.rem(index, 2) == 1)
        def _():
            def body(chunk, carry):
                over(back, turn * per_group + chunk, from_row, from_core).wait_recv()
                return carry

            lax.fori_loop(0, per_group, body, 0)

        block = from_row * 2 + from_core
        group = lax.rem(from_row + turn, chips)
        top = pl.multiple_of(group * group_rows, group_rows)
        left_at = pl.multiple_of(block * width, width)
        lanes = gain_wide.shape[1]
        tiles = width // lanes
        gain = gain_wide[pl.ds(pl.multiple_of(block * tiles, tiles), tiles), :]

        def scale(part, carry):
            here = pl.ds(pl.multiple_of(part * strip, strip), strip)
            at = pl.ds(pl.multiple_of(top + part * strip, strip), strip)
            total = ssq_ref[at, :]
            for part_at in range(tiles):
                wide = slice(part_at * lanes, (part_at + 1) * lanes)
                value = full_ref[block, at, wide].astype(jnp.float32)
                x_ref[here, wide] = (value * gain[part_at : part_at + 1, :]).astype(x_ref.dtype)
                total = total + value * value
            ssq_ref[at, :] = total
            return carry

        lax.fori_loop(0, group_rows // strip, scale, 0)
        at = pl.ds(top, group_rows)

        def multiply(part, carry):
            wide = pl.ds(pl.multiple_of(part * cut, cut), cut)
            acc_ref[at, wide] = acc_ref[at, wide] + jnp.dot(
                x_ref[...], w_ref[pl.ds(left_at, width), wide], preferred_element_type=jnp.float32
            )
            return carry

        lax.fori_loop(0, ff_both // cut, multiply, 0)

    early = blocks * (chips - 1)

    def march(t, carry):
        @pl.when((t < count) & (lax.rem(t, per_seq) == 0))
        def _():
            partial(t // per_seq)

        here = t - donor * HOP

        @pl.when((here >= 0) & (here < count))
        def _():
            @pl.when(donor == 0)
            def _():
                r_out[here] = p_rows(here).astype(r_out.dtype)

            @pl.when(donor > 0)
            def _():
                right(here).wait_recv()

            @pl.when((donor > 0) & (donor < last))
            def _():
                r_out[here] = (p_rows(here) + r_in[here].astype(jnp.float32)).astype(r_out.dtype)

            @pl.when(donor < last)
            def _():
                right(here).start()

        there = t - (last - donor) * HOP

        @pl.when((there >= 0) & (there < count))
        def _():
            @pl.when(donor == last)
            def _():
                l_out[there] = p_rows(there).astype(l_out.dtype)

            @pl.when(donor < last)
            def _():
                left(there).wait_recv()

            @pl.when((donor > 0) & (donor < last))
            def _():
                l_out[there] = (p_rows(there) + l_in[there].astype(jnp.float32)).astype(l_out.dtype)

            @pl.when(donor > 0)
            def _():
                left(there).start()

        done = t - reach

        @pl.when((done >= 0) & (done < count))
        def _():
            goal = tile(row, core, done)

            @pl.when(donor == 0)
            def _():
                goal[...] = (p_rows(done) + l_in[done].astype(jnp.float32)).astype(goal.dtype)

            @pl.when(donor == last)
            def _():
                goal[...] = (p_rows(done) + r_in[done].astype(jnp.float32)).astype(goal.dtype)

            @pl.when((donor > 0) & (donor < last))
            def _():
                goal[...] = (
                    p_rows(done) + r_in[done].astype(jnp.float32) + l_in[done].astype(jnp.float32)
                ).astype(goal.dtype)

            for step in range(1, chips):
                across(step, done, row, lax.rem(row + step, chips) * 2 + core).start()
            over(0, done, row, core).start()

        came = t - reach - lag

        @pl.when((came >= 0) & (came < count))
        def _():
            for step in range(1, chips):
                from_row = lax.rem(row + chips - step, chips)
                across(step, came, from_row, from_row * 2 + core).wait_recv()
                over(step, came, from_row, core).start()

        @pl.when(t < raw_steps)
        def _():
            relay_weights(t)

        ready = t - reach - first_mix

        @pl.when((ready >= 0) & (ready < early))
        def _():
            mix(ready // blocks, lax.rem(ready, blocks))

        return carry

    steps = count + last * HOP + lag
    lax.fori_loop(0, steps, march, 0)

    def rest(index, carry):
        mix(index // blocks, lax.rem(index, blocks))
        return carry

    lax.fori_loop(jnp.minimum(steps - reach - first_mix, early), early, rest, 0)
    own_copies[2].wait()

    for step in range(1, blocks):
        back = lax.rem(mine + blocks - step, blocks)
        send(
            gates_out.at[step], gates_in.at[back], g_send, g_recv, step - 1, expert=back
        ).wait_recv()

    def activate(group):
        for side in range(2):
            seq = group * 2 + side
            gates_ref[side * suffix : (side + 1) * suffix, :] = jnp.sum(
                jnp.where(eye, gates_in[seq][:1, :], 0.0), axis=1, keepdims=True
            )

        def body(part, carry):
            at = pl.ds(pl.multiple_of(group * group_rows + part * strip, strip), strip)
            here = pl.ds(pl.multiple_of(part * strip, strip), strip)
            mean = jnp.sum(ssq_ref[at, :], axis=1, keepdims=True) * (1.0 / model_width)
            inverse = lax.rsqrt(mean + 1e-06)
            gate = acc_ref[at, :ff_local] * inverse
            up = acc_ref[at, ff_local:] * inverse
            value = gate / (1.0 + jnp.exp(-gate)) * up * gates_ref[here, :]
            act_ref[at, :] = value.astype(act_ref.dtype)
            return carry

        lax.fori_loop(0, group_rows // strip, body, 0)

    def target(rank):
        low = jnp.minimum(donor, last - donor)
        single = jnp.maximum(donor, last - donor) - low
        rest_rank = rank - single
        gap = low - rest_rank // 2
        side = 1 - 2 * lax.rem(jnp.maximum(rest_rank, 0), 2)
        paired = donor + side * gap
        lone = jnp.where(donor < last - donor, last - rank, rank)
        return jnp.where(rank == last, donor, jnp.where(rank < single, lone, paired))

    def add(out, *terms):
        def body(part, carry):
            at = pl.ds(pl.multiple_of(part * strip, strip), strip)
            value = terms[0][at, :].astype(jnp.float32)
            for term in terms[1:]:
                value = value + term[at, :].astype(jnp.float32)
            out[at, :] = value.astype(out.dtype)
            return carry

        lax.fori_loop(0, suffix // strip, body, 0)

    order = list(range(1, chips)) + [0]

    def own_half(slot):
        return part_ref.at[slot, pl.ds(pl.multiple_of(core * suffix, suffix), suffix)]

    def swap(slot):
        away = part_ref.at[slot, pl.ds(pl.multiple_of((1 - core) * suffix, suffix), suffix)]
        return send(away, c_in.at[slot], cc_send, cc_recv, slot, expert=beside)

    def cross(hop, to):
        return send(y_out.at[hop], y_in.at[hop], yy_send, yy_recv, hop, expert=to)

    def produce(step, rank):
        slot = step * donors + rank
        top = pl.multiple_of(lax.rem(row + step, chips) * group_rows, group_rows)
        left_at = pl.multiple_of(target(rank) * columns, columns)
        part_ref[slot] = jnp.dot(
            act_ref[pl.ds(top, group_rows), :],
            down_ref[:, pl.ds(left_at, columns)],
            preferred_element_type=jnp.float32,
        ).astype(part_ref.dtype)
        swap(slot).start()

    def pass_on(step, rank):
        slot = step * donors + rank
        hop = (step - 1) * donors + rank
        swap(slot).wait_recv()
        add(y_out.at[hop], own_half(slot), c_in.at[slot])
        cross(hop, lax.rem(row + step, chips) * 2 + core).start()

    for step in order:
        for side in range(2):
            mix(chips - 1, 2 * ((step + 1) % chips) + side)
        activate(lax.rem(row + step, chips))
        if step:

            def body(rank, carry):
                produce(step, rank)

                @pl.when(rank > 0)
                def _():
                    pass_on(step, rank - 1)

                return carry

            lax.fori_loop(0, donors, body, 0)
            pass_on(step, donors - 1)
        else:

            def body(rank, carry):
                produce(0, rank)
                return carry

            lax.fori_loop(0, donors, body, 0)

    def shift_right(goal):
        return send(zr_out.at[goal], zr_in.at[goal], zr_send, zr_recv, goal, donor=donor + 1)

    def shift_left(goal):
        return send(zl_out.at[goal], zl_in.at[goal], zl_send, zl_recv, goal, donor=donor - 1)

    def finish(rank, carry):
        goal = target(rank)
        swap(rank).wait_recv()
        terms = [own_half(rank), c_in.at[rank]]
        for step in range(1, chips):
            hop = (step - 1) * donors + rank
            cross(hop, mine).wait_recv()
            terms.append(y_in.at[hop])

        @pl.when((goal >= donor) & (donor > 0))
        def _():
            shift_right(goal).wait_recv()

        @pl.when((goal <= donor) & (donor < last))
        def _():
            shift_left(goal).wait_recv()

        @pl.when(goal > donor)
        def _():
            @pl.when(donor == 0)
            def _():
                add(zr_out.at[goal], *terms)

            @pl.when(donor > 0)
            def _():
                add(zr_out.at[goal], zr_in.at[goal], *terms)

            shift_right(goal).start()

        @pl.when(goal < donor)
        def _():
            @pl.when(donor == last)
            def _():
                add(zl_out.at[goal], *terms)

            @pl.when(donor < last)
            def _():
                add(zl_out.at[goal], zl_in.at[goal], *terms)

            shift_left(goal).start()

        @pl.when(goal == donor)
        def _():
            def close(ends):
                for part in range(columns // width):
                    wide = slice(part * width, (part + 1) * width)

                    def body(index, carry):
                        at = pl.ds(pl.multiple_of(index * strip, strip), strip)
                        down = pl.ds(pl.multiple_of(mine * suffix + index * strip, strip), strip)
                        value = full_ref[donor * (columns // width) + part, down, :].astype(jnp.float32)
                        total = terms[0][at, wide].astype(jnp.float32)
                        for term in terms[1:] + ends:
                            total = total + term[at, wide].astype(jnp.float32)
                        out_ref[at, wide] = (value + total).astype(out_ref.dtype)
                        return carry

                    lax.fori_loop(0, suffix // strip, body, 0)

            @pl.when(donor == 0)
            def _():
                close([zl_in.at[donor]])

            @pl.when(donor == last)
            def _():
                close([zr_in.at[donor]])

            @pl.when((donor > 0) & (donor < last))
            def _():
                close([zl_in.at[donor], zr_in.at[donor]])

        return carry

    lax.fori_loop(0, donors, finish, 0)

    for step in range(1, blocks):
        gates_to(step).wait_send()
    for index in range(seqs_each):

        @pl.when(partner(index) != mine)
        def _():
            hidden_to(index).wait_send()

    for step in range(1, chips):
        heads_y(step, mine, mine).wait_send()
    for step in range(chips):
        heads_c(step, mine).wait_send()

    def drain(chunk, carry):
        @pl.when(donor < last)
        def _():
            right(chunk).wait_send()

        @pl.when(donor > 0)
        def _():
            left(chunk).wait_send()

        for step in range(1, chips):
            across(step, chunk, row, mine).wait_send()
        for step in range(chips):
            over(step, chunk, row, core).wait_send()
        return carry

    lax.fori_loop(0, count, drain, 0)

    def drain_blocks(goal, carry):
        for step in range(chips):
            swap(step * donors + goal).wait_send()
        for step in range(1, chips):
            cross((step - 1) * donors + goal, mine).wait_send()

        @pl.when(goal > donor)
        def _():
            shift_right(goal).wait_send()

        @pl.when(goal < donor)
        def _():
            shift_left(goal).wait_send()

        return carry

    lax.fori_loop(0, donors, drain_blocks, 0)


def page_kernel(
    experts,
    donors,
    pool_ref,
    table_ref,
    length_ref,
    query_ref,
    fresh_ref,
    head_ref,
    out_buf,
    pages_in,
    sends,
    recvs,
):
    expert, donor = lax.axis_index("expert"), lax.axis_index("donor")
    seqs, kv_heads = out_buf.shape[0], out_buf.shape[1]
    suffix, columns = head_ref.shape
    head_dim = fresh_ref.shape[1] // 2
    order = [
        (step_e, step_z)
        for step_z in [*far_first(donors), 0]
        for step_e in range(experts)
        if step_e or step_z
    ]
    barrier = pltpu.get_barrier_semaphore()

    def ahead(step_e, step_z):
        return lax.rem(expert + step_e, experts), lax.rem(donor + step_z, donors)

    for step_e, step_z in order:
        to_e, to_z = ahead(step_e, step_z)
        pl.semaphore_signal(
            barrier, inc=1, device_id={"expert": to_e, "donor": to_z}, device_id_type=MESH
        )
    mine = expert * donors + donor
    pages, page_len = table_ref.shape[1], pages_in.shape[1]
    slots = seqs
    for seq in range(seqs):
        held = 0
        for index in range(pages):
            named = table_ref[seq, index]
            held = held + jnp.where(named // slots == mine, named % slots, 0)
        for group in range(kv_heads):
            out_buf[seq, group] = pool_ref[held, group]
    lane = lax.broadcasted_iota(jnp.int32, (1, pages * page_len), 1)
    holder = lane // page_len
    first = jnp.zeros_like(lane)
    for index in range(pages):
        first = jnp.where(holder == table_ref[expert, index] // slots, index * page_len, first)
    seen = first + lane % page_len < length_ref[expert]
    bias = jnp.where(seen, 0.0, -jnp.inf)
    pl.semaphore_wait(barrier, experts * donors - 1)

    def page(step_e, step_z):
        to_e, to_z = ahead(step_e, step_z)
        return send(
            out_buf.at[to_e, to_z * kv_heads // donors],
            pages_in.at[mine],
            sends,
            recvs,
            step_e * donors + step_z,
            expert=to_e,
            donor=to_z,
        )

    for step_e, step_z in order:
        page(step_e, step_z).start()
    pages_in[mine] = out_buf[expert, donor * kv_heads // donors]
    for step_e, step_z in order:
        from_e, from_z = ahead(experts - step_e, donors - step_z)
        send(
            out_buf.at[expert, donor * kv_heads // donors],
            pages_in.at[from_e * donors + from_z],
            sends,
            recvs,
            step_e * donors + step_z,
            expert=from_e,
            donor=from_z,
        ).wait_recv()
    keys_count = pages_in.shape[0] * pages_in.shape[1]
    causal = lax.broadcasted_iota(jnp.int32, (suffix, suffix), 0) >= lax.broadcasted_iota(
        jnp.int32, (suffix, suffix), 1
    )
    scale = head_dim ** (-0.5)
    both = (((1,), (1,)), ((), ()))
    for left in range(0, columns, head_dim):
        query = query_ref[:, left : left + head_dim]
        old_keys = pages_in[:, :, :head_dim].reshape(keys_count, head_dim)
        old = lax.dot_general(query, old_keys, both, preferred_element_type=jnp.float32)
        new = lax.dot_general(
            query, fresh_ref[:, :head_dim], both, preferred_element_type=jnp.float32
        )
        old = old * scale + bias
        new = jnp.where(causal, new * scale, -jnp.inf)
        top = jnp.maximum(
            jnp.max(old, axis=1, keepdims=True), jnp.max(new, axis=1, keepdims=True)
        )
        old = jnp.exp(old - top)
        new = jnp.exp(new - top)
        total = jnp.sum(old, axis=1, keepdims=True) + jnp.sum(new, axis=1, keepdims=True)
        old_vals = pages_in[:, :, head_dim:].reshape(keys_count, head_dim)
        mixed = jnp.dot(old.astype(query.dtype), old_vals, preferred_element_type=jnp.float32)
        mixed = mixed + jnp.dot(
            new.astype(query.dtype), fresh_ref[:, head_dim:], preferred_element_type=jnp.float32
        )
        head_ref[:, left : left + head_dim] = (mixed / total).astype(head_ref.dtype)
    for step_e, step_z in order:
        page(step_e, step_z).wait_send()


def page_heads(pool, table, lengths, queries, fresh, experts, donors):
    seqs, kv_heads, page_len, both = pool.shape
    dma = pltpu.SemaphoreType.DMA
    inside = pl.BlockSpec(memory_space=pltpu.VMEM)
    return pl.pallas_call(
        functools.partial(page_kernel, experts, donors),
        out_shape=jax.ShapeDtypeStruct(queries.shape, queries.dtype),
        in_specs=[inside] + [pl.BlockSpec(memory_space=pltpu.SMEM)] * 2 + [inside] * 2,
        out_specs=inside,
        scratch_shapes=[
            pltpu.VMEM((seqs, kv_heads, page_len, both), pool.dtype),
            pltpu.VMEM((experts * donors, page_len, both), pool.dtype),
            dma((experts * donors,)),
            dma((experts * donors,)),
        ],
        compiler_params=pltpu.CompilerParams(collective_id=4, has_side_effects=True),
        name="page_heads",
    )(pool, table, lengths, queries, fresh)


def mix_scratch(heads, out_weight, w_gate_up, chips, donors, piece):
    suffix, head_cols = heads.shape
    blocks = 2 * chips
    width = out_weight.shape[1]
    model_width, ff_local = w_gate_up.shape[1], w_gate_up.shape[3]
    tokens = blocks * suffix
    columns = model_width // donors
    count = tokens // piece
    kind = heads.dtype
    vmem = lambda *shape: pltpu.VMEM(shape, kind)
    wide = lambda *shape: pltpu.VMEM(shape, jnp.float32)
    held = lambda number: pltpu.VMEM((number, suffix, columns), kind)
    return [
        vmem(blocks // donors, suffix, width),
        wide(blocks, 8, suffix),
        wide(blocks, 8, suffix),
        wide(model_width // 128, 128),
        vmem(head_cols, width),
        vmem(3, model_width // 8, 2, ff_local),
        vmem(ff_local, model_width),
        vmem(tokens, head_cols),
        wide(tokens, width),
        vmem(count, piece, width),
        vmem(count, piece, width),
        vmem(count, piece, width),
        vmem(count, piece, width),
        vmem(blocks, tokens, width),
        vmem(model_width, 2 * ff_local),
        vmem(2 * suffix, width),
        wide(tokens, 2 * ff_local),
        wide(tokens, 128),
        vmem(tokens, ff_local),
        wide(2 * suffix, 1),
        vmem(chips * donors, 2 * suffix, columns),
        held(chips * donors),
        held((chips - 1) * donors),
        held((chips - 1) * donors),
        held(donors),
        held(donors),
        held(donors),
        held(donors),
    ]


def mix_blocks(
    heads, gain, probs, ids, hidden, out_weight, w_gate_up, w_down, chips, donors, piece, scratch
):
    suffix = heads.shape[0]
    columns = w_gate_up.shape[1] // donors
    count = 2 * chips * suffix // piece
    dma = pltpu.SemaphoreType.DMA
    pair = lambda number: [dma((number,)), dma((number,))]
    inside = pl.BlockSpec(memory_space=pltpu.VMEM)
    outside = pl.BlockSpec(memory_space=pl.ANY)
    return pl.pallas_call(
        functools.partial(mix_kernel, chips, donors, piece),
        out_shape=jax.ShapeDtypeStruct((suffix, columns), heads.dtype),
        in_specs=[inside] * 4 + [outside] * 4,
        out_specs=inside,
        scratch_shapes=scratch
        + [dma((3,)), dma((8,))]
        + pair(2 * chips - 1)
        + pair(2 * chips // donors)
        + pair(chips - 1)
        + pair(chips)
        + pair(count)
        + pair(count)
        + pair((chips - 1) * count)
        + pair(chips * count)
        + pair(chips * donors)
        + pair((chips - 1) * donors)
        + pair(donors)
        + pair(donors),
        compiler_params=pltpu.CompilerParams(
            collective_id=3, has_side_effects=True, vmem_limit_bytes=VMEM_BYTES
        ),
        name="mix_blocks",
    )(heads, gain, probs, ids, hidden, out_weight, w_gate_up, w_down)


def shards(
    hidden_in,
    queries,
    suffix_kv,
    kv_pool,
    page_table,
    prefix_len,
    out_weight,
    norm_gain,
    expert_ids,
    route_probs,
    w_gate_up,
    w_down,
):
    n_expert = lax.axis_size("expert")
    n_donor = lax.axis_size("donor")
    expert_index = lax.axis_index("expert")
    donor_index = lax.axis_index("donor")
    share_count = n_donor // 2
    seq_count, page_count = page_table.shape
    suffix_len = queries.shape[0]
    kv_heads = suffix_kv.shape[1]
    head_dim = suffix_kv.shape[2] // 2
    page_len = kv_pool.shape[2]
    model_width = hidden_in.shape[1]
    columns = model_width // n_donor
    experts_all = 2 * n_expert
    ff_local = w_gate_up.shape[3]
    my_group = donor_index * kv_heads // n_donor
    owner_index = expert_index * n_donor + donor_index
    owner_of = page_table // seq_count
    held_slot = jnp.sum(jnp.where(owner_of == owner_index, page_table % seq_count, 0), axis=1)
    chips = n_expert // 2
    my_pair = lax.dynamic_index_in_dim(suffix_kv, my_group, 1, keepdims=False)
    scratch = mix_scratch(queries, out_weight, w_gate_up, chips, n_donor, PIECE)
    held_bytes = sum(math.prod(item.shape) * item.dtype.itemsize for item in scratch)
    if held_bytes <= VMEM_BYTES - 4 * 1024 * 1024:
        head_out = page_heads(
            kv_pool, page_table, prefix_len, queries, my_pair, n_expert, n_donor
        )
        layer_out = mix_blocks(
            head_out,
            norm_gain.reshape(-1, 128),
            route_probs.T,
            expert_ids.T,
            hidden_in,
            out_weight,
            w_gate_up,
            w_down,
            chips,
            n_donor,
            PIECE,
            scratch,
        )
        return (layer_out, head_out)

    dest_group = jnp.arange(n_donor, dtype=jnp.int32) * kv_heads // n_donor
    wanted = (held_slot[:, None] * kv_heads + dest_group[None, :]).reshape(-1)
    outgoing = jnp.take(
        kv_pool.reshape(seq_count * kv_heads, page_len, 2 * head_dim), wanted, axis=0
    )
    arrived = lax.all_to_all(outgoing, ("expert", "donor"), split_axis=0, concat_axis=0, tiled=True)
    my_owners = lax.dynamic_index_in_dim(owner_of, expert_index, 0, keepdims=False)
    ordered = jnp.take(arrived, my_owners, axis=0).reshape(page_count * page_len, 2 * head_dim)
    prefix_keys = ordered[:, :head_dim]
    prefix_vals = ordered[:, head_dim:]
    score_scale = head_dim ** (-0.5)
    query_heads = queries.reshape(suffix_len, -1, head_dim)
    fresh_pair = lax.dynamic_index_in_dim(suffix_kv, my_group, 1, keepdims=False)
    causal = jnp.arange(suffix_len)[:, None] >= jnp.arange(suffix_len)[None, :]
    fresh_scores = (
        jnp.einsum(
            "thc,uc->thu", query_heads, fresh_pair[:, :head_dim], preferred_element_type=jnp.float32
        )
        * score_scale
    )
    fresh_scores = jnp.where(causal[:, None, :], fresh_scores, -jnp.inf)
    prefix_tokens = lax.dynamic_index_in_dim(prefix_len, expert_index, 0, keepdims=False)
    block_keys = min(1024, page_count * page_len)
    live_blocks = (prefix_tokens + block_keys - 1) // block_keys

    def block_scores(block_index):
        keys_block = lax.dynamic_slice_in_dim(prefix_keys, block_index * block_keys, block_keys, 0)
        raw_scores = (
            jnp.einsum("thc,kc->thk", query_heads, keys_block, preferred_element_type=jnp.float32)
            * score_scale
        )
        visible = block_index * block_keys + jnp.arange(block_keys) < prefix_tokens
        return jnp.where(visible[None, None, :], raw_scores, -jnp.inf)

    def raise_max(block_index, running):
        return jnp.maximum(running, jnp.max(block_scores(block_index), axis=2))

    row_max = lax.fori_loop(0, live_blocks, raise_max, jnp.max(fresh_scores, axis=2))

    def add_block(block_index, loop_state):
        row_total, weighted = loop_state
        exp_scores = jnp.exp(block_scores(block_index) - row_max[:, :, None])
        vals_block = lax.dynamic_slice_in_dim(prefix_vals, block_index * block_keys, block_keys, 0)
        weighted = weighted + jnp.einsum(
            "thk,kc->thc",
            exp_scores.astype(jnp.bfloat16),
            vals_block,
            preferred_element_type=jnp.float32,
        )
        return (row_total + jnp.sum(exp_scores, axis=2), weighted)

    fresh_exp = jnp.exp(fresh_scores - row_max[:, :, None])
    start_state = (
        jnp.sum(fresh_exp, axis=2),
        jnp.einsum(
            "thu,uc->thc",
            fresh_exp.astype(jnp.bfloat16),
            fresh_pair[:, head_dim:],
            preferred_element_type=jnp.float32,
        ),
    )
    row_total, weighted = lax.fori_loop(0, live_blocks, add_block, start_state)
    head_out = (weighted / row_total[:, :, None]).astype(jnp.bfloat16).reshape(suffix_len, -1)
    gate_weights = route_probs / jnp.sum(route_probs, axis=1, keepdims=True)
    chosen = expert_ids[:, :, None] == jnp.arange(experts_all, dtype=jnp.int32)
    gate_table = jnp.sum(jnp.where(chosen, gate_weights[:, :, None], 0.0), axis=1)
    gate_tables = [gate_table]
    for step in range(1, n_expert):
        pairs = [(source, (source + step) % n_expert) for source in range(n_expert)]
        gate_tables.append(lax.ppermute(gate_table, "expert", pairs))
    from_order = lax.rem(expert_index - jnp.arange(n_expert) + n_expert, n_expert)
    gate_all = jnp.stack(gate_tables)[from_order].reshape(n_expert * suffix_len, experts_all)
    my_expert = owner_index // share_count
    my_gates = lax.dynamic_slice_in_dim(gate_all, my_expert, 1, 1)

    seqs_each = n_expert // n_donor
    width = model_width // n_expert
    hidden_parts = []
    for shift in range(seqs_each):
        pairs = []
        for source in range(n_expert * n_donor):
            seq, part = source // n_donor, source % n_donor
            target = part * seqs_each + (seq + shift) % seqs_each
            pairs.append((source, target * n_donor + seq // seqs_each))
        target = donor_index * seqs_each + lax.rem(expert_index + shift, seqs_each)
        sent = lax.dynamic_slice_in_dim(hidden_in, target * width, width, 1)
        hidden_parts.append(lax.ppermute(sent, ("expert", "donor"), pairs))
    turned = lax.rem(expert_index - jnp.arange(seqs_each) + seqs_each * n_expert, seqs_each)
    hidden_block = jnp.stack(hidden_parts)[turned].reshape(seqs_each * suffix_len, width)

    heads_all = lax.all_gather(head_out, "expert", axis=0, tiled=True)
    w_in, heads_all = lax.optimization_barrier(
        (w_gate_up[0].reshape(model_width, 2 * ff_local), heads_all)
    )
    resid = gather_blocks(heads_all, out_weight, hidden_block, n_expert // 2, n_donor)
    resid_f = resid.astype(jnp.float32)
    inverse = lax.rsqrt(jnp.mean(resid_f * resid_f, axis=1, keepdims=True) + 1e-06)
    normed = (resid_f * inverse * norm_gain.astype(jnp.float32)).astype(jnp.bfloat16)
    gate_up = jnp.dot(
        normed,
        w_in,
        preferred_element_type=jnp.float32,
    )
    activated = (
        jax.nn.silu(gate_up[:, :ff_local]) * gate_up[:, ff_local:] * my_gates
    ).astype(jnp.bfloat16)
    expert_mix = reduce_blocks(activated, w_down[0], n_expert // 2, n_donor)
    resid_mine = lax.dynamic_slice(
        resid,
        (expert_index * suffix_len, donor_index * columns),
        (suffix_len, columns),
    )
    layer_out = (resid_mine.astype(jnp.float32) + expert_mix).astype(
        jnp.bfloat16
    )
    return (layer_out, head_out)


def solution(mesh):
    in_specs = (
        P(("groups", "expert"), None),
        P(("groups", "expert"), "donor"),
        P(("groups", "expert"), None, None),
        P(("groups", "expert", "donor"), None, None, None),
        P("groups", None),
        P("groups"),
        P("donor", "expert"),
        P(),
        P(("groups", "expert"), None),
        P(("groups", "expert"), None),
        P(("expert", "donor"), None, None, None),
        P(("expert", "donor"), None, None),
    )
    out_specs = (P(("groups", "expert"), "donor"), P(("groups", "expert"), "donor"))
    return jax.shard_map(shards, mesh=mesh, in_specs=in_specs, out_specs=out_specs, check_vma=False)
```

```python
import functools
import math

import jax
import jax.numpy as jnp
from jax import lax
from jax.experimental import pallas as pl
from jax.experimental.pallas import tpu as pltpu
from jax.sharding import PartitionSpec as P

MESH = pl.DeviceIdType.MESH
VMEM_BYTES = 60 * 1024 * 1024
PIECE = 32
HOP = 3
LAG = 3


def place():
    expert = lax.axis_index("expert")
    return expert // 2, lax.rem(expert, 2), lax.axis_index("donor")


def send(src, dst, sends, recvs, slot, **where):
    return pltpu.make_async_remote_copy(
        src_ref=src,
        dst_ref=dst,
        send_sem=sends.at[slot],
        recv_sem=recvs.at[slot],
        device_id=where,
        device_id_type=MESH,
    )


def greet(chips, donors):
    row, core, donor = place()
    barrier = pltpu.get_barrier_semaphore()
    pl.semaphore_signal(
        barrier, inc=1, device_id={"expert": row * 2 + 1 - core}, device_id_type=MESH
    )
    for step in range(1, chips):
        other = lax.rem(row + step, chips) * 2 + core
        pl.semaphore_signal(barrier, inc=1, device_id={"expert": other}, device_id_type=MESH)
    for step in range(1, donors):
        other = lax.rem(donor + step, donors)
        pl.semaphore_signal(barrier, inc=1, device_id={"donor": other}, device_id_type=MESH)
    pl.semaphore_wait(barrier, chips + donors - 1)


def far_first(donors):
    return sorted(range(1, donors), key=lambda k: (-min(k, donors - k), k))


def gather_kernel(
    chips,
    donors,
    heads_ref,
    out_ref,
    hidden_ref,
    full_ref,
    terms_ref,
    terms_in,
    block_ref,
    own_sem,
    t_send,
    t_recv,
    z_send,
    z_recv,
    y_send,
    y_recv,
    c_send,
    c_recv,
):
    row, core, donor = place()
    rows, cols = block_ref.shape
    greet(chips, donors)
    strip = 16

    def project(step_z, slot):
        top = pl.multiple_of(lax.rem(donor + step_z, donors) * rows, rows)
        terms_ref[slot] = jnp.dot(
            heads_ref[pl.ds(top, rows), :], out_ref[...], preferred_element_type=jnp.float32
        ).astype(terms_ref.dtype)

    term_copies = {}
    for step in far_first(donors):
        project(step, step)
        copy = send(
            terms_ref.at[step],
            terms_in.at[step - 1],
            t_send,
            t_recv,
            step - 1,
            donor=lax.rem(donor + step, donors),
        )
        copy.start()
        term_copies[step] = copy
    project(0, 0)
    for step in far_first(donors):
        term_copies[step].wait_recv()

    def add(index, carry):
        at = pl.ds(pl.multiple_of(index * strip, strip), strip)
        value = terms_ref[0, at, :].astype(jnp.float32)
        for step in range(1, donors):
            value = value + terms_in[step - 1, at, :].astype(jnp.float32)
        value = value + hidden_ref[at, :].astype(jnp.float32)
        block_ref[at, :] = value.astype(block_ref.dtype)
        return carry

    lax.fori_loop(0, rows // strip, add, 0)

    def slot_of(donor_from, row_from, core_from):
        top = pl.multiple_of(donor_from * rows, rows)
        left = pl.multiple_of((row_from * 2 + core_from) * cols, cols)
        return full_ref.at[pl.ds(top, rows), pl.ds(left, cols)]

    own = pltpu.make_async_copy(block_ref, slot_of(donor, row, core), own_sem)
    own.start()
    started = []

    def along_y(src, step_z, donor_from):
        for step in range(1, chips):
            copy = send(
                src,
                slot_of(donor_from, row, core),
                y_send,
                y_recv,
                step_z * (chips - 1) + step - 1,
                expert=lax.rem(row + step, chips) * 2 + core,
            )
            copy.start()
            started.append(copy)

    def beside(src, step_z, step_y, donor_from, row_from):
        copy = send(
            src,
            slot_of(donor_from, row_from, core),
            c_send,
            c_recv,
            step_z * chips + step_y,
            expert=row * 2 + 1 - core,
        )
        copy.start()
        started.append(copy)

    along_y(block_ref, 0, donor)
    z_copies = {}
    near_first = far_first(donors)[::-1]
    for step in near_first:
        copy = send(
            block_ref,
            slot_of(donor, row, core),
            z_send,
            z_recv,
            step - 1,
            donor=lax.rem(donor + step, donors),
        )
        copy.start()
        z_copies[step] = copy
    beside(block_ref, 0, 0, donor, row)

    def take_y(step_z, donor_from):
        for step in range(1, chips):
            row_from = lax.rem(row + chips - step, chips)
            there = slot_of(donor_from, row_from, core)
            send(
                there,
                there,
                y_send,
                y_recv,
                step_z * (chips - 1) + step - 1,
                expert=row_from * 2 + core,
            ).wait_recv()
            beside(there, step_z, step, donor_from, row_from)

    for step in near_first:
        donor_from = lax.rem(donor + donors - step, donors)
        there = slot_of(donor_from, row, core)
        send(there, there, z_send, z_recv, step - 1, donor=donor_from).wait_recv()
        along_y(there, step, donor_from)
        beside(there, step, 0, donor_from, row)
    for step in [0] + near_first:
        take_y(step, lax.rem(donor + donors - step, donors))
    for step_z in range(donors):
        donor_from = lax.rem(donor + donors - step_z, donors)
        for step_y in range(chips):
            row_from = lax.rem(row + chips - step_y, chips)
            there = slot_of(donor_from, row_from, 1 - core)
            send(
                there, there, c_send, c_recv, step_z * chips + step_y, expert=row * 2 + 1 - core
            ).wait_recv()
    own.wait()
    for copy in list(term_copies.values()) + list(z_copies.values()) + started:
        copy.wait_send()


def gather_blocks(heads, out_weight, block, chips, donors):
    rows, cols = block.shape
    dma = pltpu.SemaphoreType.DMA
    return pl.pallas_call(
        functools.partial(gather_kernel, chips, donors),
        out_shape=jax.ShapeDtypeStruct((rows * donors, cols * chips * 2), block.dtype),
        in_specs=[pl.BlockSpec(memory_space=pltpu.VMEM)] * 3,
        out_specs=pl.BlockSpec(memory_space=pltpu.VMEM),
        scratch_shapes=[
            pltpu.VMEM((donors, rows, cols), block.dtype),
            pltpu.VMEM((donors - 1, rows, cols), block.dtype),
            pltpu.VMEM((rows, cols), block.dtype),
            dma,
            dma((donors - 1,)),
            dma((donors - 1,)),
            dma((donors - 1,)),
            dma((donors - 1,)),
            dma((donors * (chips - 1),)),
            dma((donors * (chips - 1),)),
            dma((donors * chips,)),
            dma((donors * chips,)),
        ],
        compiler_params=pltpu.CompilerParams(collective_id=1, has_side_effects=True),
        name="gather_blocks",
    )(heads, out_weight, block)


def reduce_kernel(
    chips,
    donors,
    act_ref,
    down_ref,
    total_ref,
    part_ref,
    c_in,
    y_out,
    y_in,
    z_out,
    z_in,
    c_send,
    c_recv,
    y_send,
    y_recv,
    z_send,
    z_recv,
):
    row, core, donor = place()
    rows, cols = total_ref.shape
    greet(chips, donors)
    order = far_first(donors) + [0]
    strip = 16

    def tile(row_to, core_to, step_z):
        top = pl.multiple_of((row_to * 2 + core_to) * rows, rows)
        left = pl.multiple_of(lax.rem(donor + step_z, donors) * cols, cols)
        return part_ref.at[pl.ds(top, rows), pl.ds(left, cols)]

    def add(out, *terms):
        def body(index, carry):
            at = pl.ds(pl.multiple_of(index * strip, strip), strip)
            value = terms[0][at, :].astype(jnp.float32)
            for term in terms[1:]:
                value = value + term[at, :].astype(jnp.float32)
            out[at, :] = value.astype(out.dtype)
            return carry

        lax.fori_loop(0, rows // strip, body, 0)

    started = []
    arrivals = {}

    def multiply(step_z):
        left = pl.multiple_of(lax.rem(donor + step_z, donors) * cols, cols)

        def body(index, carry):
            at = pl.ds(pl.multiple_of(index * rows, rows), rows)
            part_ref[at, pl.ds(left, cols)] = jnp.dot(
                act_ref[at, :],
                down_ref[:, pl.ds(left, cols)],
                preferred_element_type=jnp.float32,
            ).astype(part_ref.dtype)
            return carry

        lax.fori_loop(0, chips * 2, body, 0)

    def beside(step_z):
        for step_y in range(chips - 1, -1, -1):
            slot = step_z * chips + step_y
            copy = send(
                tile(lax.rem(row + step_y, chips), 1 - core, step_z),
                c_in.at[slot],
                c_send,
                c_recv,
                slot,
                expert=row * 2 + 1 - core,
            )
            copy.start()
            started.append(copy)

    def along_y(step_z):
        for step_y in range(chips - 1, 0, -1):
            row_to = lax.rem(row + step_y, chips)
            slot = step_z * chips + step_y
            send(
                c_in.at[slot], c_in.at[slot], c_send, c_recv, slot, expert=row * 2 + 1 - core
            ).wait_recv()
            hop = step_z * (chips - 1) + step_y - 1
            add(y_out.at[hop], tile(row_to, core, step_z), c_in.at[slot])
            copy = send(
                y_out.at[hop], y_in.at[hop], y_send, y_recv, hop, expert=row_to * 2 + core
            )
            copy.start()
            arrivals[hop] = copy
            started.append(copy)

    for index, step_z in enumerate(order):
        multiply(step_z)
        beside(step_z)
        if index:
            along_y(order[index - 1])
    along_y(order[-1])
    for step_z in order:
        slot = step_z * chips
        send(
            c_in.at[slot], c_in.at[slot], c_send, c_recv, slot, expert=row * 2 + 1 - core
        ).wait_recv()
        terms = [tile(row, core, step_z), c_in.at[slot]]
        for step_y in range(1, chips):
            hop = step_z * (chips - 1) + step_y - 1
            arrivals[hop].wait_recv()
            terms.append(y_in.at[hop])
        if step_z:
            add(z_out.at[step_z - 1], *terms)
            copy = send(
                z_out.at[step_z - 1],
                z_in.at[step_z - 1],
                z_send,
                z_recv,
                step_z - 1,
                donor=lax.rem(donor + step_z, donors),
            )
            copy.start()
            arrivals["z", step_z] = copy
            started.append(copy)
        else:
            for step in order[:-1]:
                arrivals["z", step].wait_recv()
                terms.append(z_in.at[step - 1])
            add(total_ref, *terms)
    for copy in started:
        copy.wait_send()


def reduce_blocks(activated, down, chips, donors):
    rows, cols = activated.shape[0] // (chips * 2), down.shape[1] // donors
    dma = pltpu.SemaphoreType.DMA
    held = lambda count: pltpu.VMEM((count, rows, cols), activated.dtype)
    return pl.pallas_call(
        functools.partial(reduce_kernel, chips, donors),
        out_shape=jax.ShapeDtypeStruct((rows, cols), jnp.float32),
        in_specs=[pl.BlockSpec(memory_space=pltpu.VMEM)] * 2,
        out_specs=pl.BlockSpec(memory_space=pltpu.VMEM),
        scratch_shapes=[
            pltpu.VMEM((activated.shape[0], down.shape[1]), activated.dtype),
            held(donors * chips),
            held(donors * (chips - 1)),
            held(donors * (chips - 1)),
            held(donors - 1),
            held(donors - 1),
            dma((donors * chips,)),
            dma((donors * chips,)),
            dma((donors * (chips - 1),)),
            dma((donors * (chips - 1),)),
            dma((donors - 1,)),
            dma((donors - 1,)),
        ],
        compiler_params=pltpu.CompilerParams(collective_id=2, has_side_effects=True),
        name="reduce_blocks",
    )(activated, down)


def mix_kernel(
    chips,
    donors,
    piece,
    heads_in,
    gain_ref,
    probs_ref,
    ids_ref,
    hidden_hbm,
    outw_hbm,
    raw_hbm,
    down_hbm,
    out_ref,
    hidden_ref,
    gates_out,
    gates_in,
    gain_wide,
    outw_ref,
    raw_ref,
    down_ref,
    heads_ref,
    p_ref,
    r_out,
    r_in,
    l_out,
    l_in,
    full_ref,
    w_ref,
    x_ref,
    acc_ref,
    ssq_ref,
    act_ref,
    gates_ref,
    part_ref,
    c_in,
    y_out,
    y_in,
    zr_out,
    zr_in,
    zl_out,
    zl_in,
    local_sem,
    raw_sem,
    g_send,
    g_recv,
    h_send,
    h_recv,
    hy_send,
    hy_recv,
    hc_send,
    hc_recv,
    r_send,
    r_recv,
    l_send,
    l_recv,
    y_send,
    y_recv,
    c_send,
    c_recv,
    cc_send,
    cc_recv,
    yy_send,
    yy_recv,
    zr_send,
    zr_recv,
    zl_send,
    zl_recv,
):
    row, core, donor = place()
    mine = row * 2 + core
    beside = row * 2 + 1 - core
    suffix, head_cols = heads_in.shape
    blocks, tokens, width = full_ref.shape
    model_width, ff_both = w_ref.shape
    ff_local = ff_both // 2
    seqs_each = hidden_ref.shape[0]
    per_seq = suffix // piece
    count = blocks * per_seq
    half, half_count, per_half = suffix // 2, count // 2, per_seq // 2
    rows = blocks * half
    columns = out_ref.shape[1]
    last = donors - 1
    lag = LAG
    first_mix = half_count + lag
    raw_steps, raw_slots, raw_rows = raw_sem.shape[0], raw_ref.shape[0], raw_ref.shape[1]
    relay = min(128, raw_rows)
    strip = 16

    own_copies = [
        pltpu.make_async_copy(outw_hbm, outw_ref, local_sem.at[0]),
        pltpu.make_async_copy(heads_in, heads_ref.at[pl.ds(mine * suffix, suffix)], local_sem.at[1]),
        pltpu.make_async_copy(down_hbm.at[0], down_ref, local_sem.at[2]),
    ]
    own_copies[0].start()
    own_copies[1].start()

    def raw_copy(index):
        at = pl.ds(pl.multiple_of(index * raw_rows, raw_rows), raw_rows)
        return pltpu.make_async_copy(
            raw_hbm.at[0, at], raw_ref.at[lax.rem(index, raw_slots)], raw_sem.at[index]
        )

    for index in range(raw_slots):
        raw_copy(index).start()
    own_copies[2].start()

    barrier = pltpu.get_barrier_semaphore()
    for step in range(1, blocks):
        other = lax.rem(mine + step, blocks)
        pl.semaphore_signal(barrier, inc=1, device_id={"expert": other}, device_id_type=MESH)

    @pl.when(donor > 0)
    def _():
        pl.semaphore_signal(barrier, inc=1, device_id={"donor": donor - 1}, device_id_type=MESH)

    @pl.when(donor < last)
    def _():
        pl.semaphore_signal(barrier, inc=1, device_id={"donor": donor + 1}, device_id_type=MESH)

    gain_wide[...] = gain_ref[...].astype(jnp.float32)
    acc_ref[...] = jnp.zeros_like(acc_ref)
    ssq_ref[...] = jnp.zeros_like(ssq_ref)
    pl.semaphore_wait(barrier, blocks - 1 + jnp.minimum(donor, 1) + jnp.minimum(last - donor, 1))

    def heads_of(seq):
        return heads_ref.at[pl.ds(pl.multiple_of(seq * suffix, suffix), suffix)]

    def heads_y(step, seq, to):
        return send(heads_of(seq), heads_of(seq), hy_send, hy_recv, step - 1, expert=to)

    def heads_c(slot, seq):
        return send(heads_of(seq), heads_of(seq), hc_send, hc_recv, slot, expert=beside)

    def gates_to(step):
        return send(
            gates_out.at[step],
            gates_in.at[mine],
            g_send,
            g_recv,
            step - 1,
            expert=lax.rem(mine + step, blocks),
        )

    def partner(index):
        return lax.rem(donor - lax.rem(mine, donors) + donors, donors) + donors * index

    def hidden_to(index):
        at = pl.ds(pl.multiple_of(partner(index) * width, width), width)
        slot = mine // donors
        return pltpu.make_async_remote_copy(
            src_ref=hidden_hbm.at[:, at],
            dst_ref=hidden_ref.at[slot],
            send_sem=h_send.at[index],
            recv_sem=h_recv.at[slot],
            device_id={"expert": partner(index)},
            device_id_type=MESH,
        )

    def hidden_own(index):
        at = pl.ds(pl.multiple_of(mine * width, width), width)
        return pltpu.make_async_copy(hidden_hbm.at[:, at], hidden_ref.at[index], h_recv.at[index])

    own_copies[1].wait()
    heads_c(0, mine).start()
    for step in range(1, chips):
        heads_y(step, mine, lax.rem(row + step, chips) * 2 + core).start()
    for index in range(seqs_each):

        @pl.when(partner(index) != mine)
        def _():
            hidden_to(index).start()

        @pl.when(partner(index) == mine)
        def _():
            hidden_own(index).start()

    square = (suffix, suffix)
    eye = lax.broadcasted_iota(jnp.int32, square, 0) == lax.broadcasted_iota(jnp.int32, square, 1)
    parts_of = donors // 2
    share = probs_ref[...] / jnp.sum(probs_ref[...], axis=0, keepdims=True)
    for step in range(blocks):
        named = (lax.rem(mine + step, blocks) * donors + donor) // parts_of
        line = jnp.sum(jnp.where(ids_ref[...] == named, share, 0.0), axis=0, keepdims=True)
        if step:
            gates_out[step] = jnp.broadcast_to(line, gates_out.shape[1:])
            gates_to(step).start()
        else:
            gates_in[mine] = jnp.broadcast_to(line, gates_out.shape[1:])
    own_copies[0].wait()

    def seq_at(from_row, from_core, index):
        return lax.rem(from_row + index // 2, chips) * 2 + lax.rem(from_core + lax.rem(index, 2), 2)

    def spot(chunk):
        within = lax.rem(chunk, half_count)
        offset = chunk // half_count * half + lax.rem(within, per_half) * piece
        return within // per_half, offset

    def tile(from_row, from_core, chunk):
        index, offset = spot(chunk)
        seq = seq_at(from_row, from_core, index)
        top = pl.multiple_of(seq * suffix + offset, piece)
        return full_ref.at[from_row * 2 + from_core, pl.ds(top, piece)]

    def right(chunk):
        return send(r_out.at[chunk], r_in.at[chunk], r_send, r_recv, chunk, donor=donor + 1)

    def left(chunk):
        return send(l_out.at[chunk], l_in.at[chunk], l_send, l_recv, chunk, donor=donor - 1)

    def across(step, chunk, from_row, to):
        there = tile(from_row, core, chunk)
        return send(there, there, y_send, y_recv, (step - 1) * count + chunk, expert=to)

    def over(step, chunk, from_row, from_core):
        there = tile(from_row, from_core, chunk)
        return send(there, there, c_send, c_recv, step * count + chunk, expert=beside)

    reach = jnp.maximum(donor, last - donor) * HOP

    def partial(index):
        seq = seq_at(row, core, index)
        step = index // 2

        @pl.when((index > 0) & (lax.rem(index, 2) == 0))
        def _():
            back = lax.rem(chips - step, chips)
            copy = send(
                heads_of(seq), heads_of(seq), hy_send, hy_recv, back - 1, expert=beside
            )
            copy.wait_recv()
            heads_c(back, seq).start()

        @pl.when(lax.rem(index, 2) == 1)
        def _():
            heads_c(lax.rem(chips - step, chips), seq).wait_recv()

        at = pl.ds(pl.multiple_of(index * suffix, suffix), suffix)
        p_ref[at, :] = jnp.dot(
            heads_ref[pl.ds(pl.multiple_of(seq * suffix, suffix), suffix), :],
            outw_ref[...],
            preferred_element_type=jnp.float32,
        )

        for index in range(seqs_each):

            @pl.when(partner(index) == seq)
            def _():
                hidden_own(index).wait()
                p_ref[at, :] = p_ref[at, :] + hidden_ref[index].astype(jnp.float32)

    def p_rows(chunk):
        index, offset = spot(chunk)
        return p_ref[pl.ds(pl.multiple_of(index * suffix + offset, piece), piece), :]

    def relay_weights(index):
        raw_copy(index).wait()
        half = lax.broadcasted_iota(jnp.int32, (relay, 2 * relay), 0)
        whole = lax.broadcasted_iota(jnp.int32, (relay, 2 * relay), 1)

        def body(part, carry):
            at = pl.ds(pl.multiple_of(index * raw_rows + part * relay, relay), relay)
            from_at = pl.ds(pl.multiple_of(part * relay, relay), relay)
            both = raw_ref[lax.rem(index, raw_slots), from_at].reshape(2 * relay, ff_local)
            for side in range(2):
                pick = (whole == 2 * half + side).astype(raw_ref.dtype)
                w_ref[at, side * ff_local : (side + 1) * ff_local] = jnp.dot(
                    pick, both, preferred_element_type=jnp.float32
                ).astype(w_ref.dtype)
            return carry

        lax.fori_loop(0, raw_rows // relay, body, 0)

        @pl.when(index + raw_slots < raw_steps)
        def _():
            raw_copy(index + raw_slots).start()

    cut = ff_both // 3

    def mix(turn, index):
        from_row = lax.rem(row + index // 2, chips)
        from_core = lax.rem(core + lax.rem(index, 2), 2)
        back = lax.rem(chips - index // 2, chips)

        @pl.when(lax.rem(index, 2) == 1)
        def _():
            def body(chunk, carry):
                over(back, turn * half_count + chunk, from_row, from_core).wait_recv()
                return carry

            lax.fori_loop(0, half_count, body, 0)

        block = from_row * 2 + from_core
        top = pl.multiple_of(turn * rows, rows)
        left_at = pl.multiple_of(block * width, width)
        lanes = gain_wide.shape[1]
        tiles = width // lanes
        gain = gain_wide[pl.ds(pl.multiple_of(block * tiles, tiles), tiles), :]

        def scale(part, carry):
            here = pl.ds(pl.multiple_of(part * strip, strip), strip)
            at = pl.ds(pl.multiple_of(top + part * strip, strip), strip)
            seq, inside = part * strip // half, lax.rem(part * strip, half)
            source = pl.ds(
                pl.multiple_of(seq * suffix + turn * half + inside, strip), strip
            )
            total = ssq_ref[at, :]
            for part_at in range(tiles):
                wide = slice(part_at * lanes, (part_at + 1) * lanes)
                value = full_ref[block, source, wide].astype(jnp.float32)
                x_ref[here, wide] = (value * gain[part_at : part_at + 1, :]).astype(x_ref.dtype)
                total = total + value * value
            ssq_ref[at, :] = total
            return carry

        lax.fori_loop(0, rows // strip, scale, 0)
        at = pl.ds(top, rows)

        def multiply(part, carry):
            wide = pl.ds(pl.multiple_of(part * cut, cut), cut)
            acc_ref[at, wide] = acc_ref[at, wide] + jnp.dot(
                x_ref[...], w_ref[pl.ds(left_at, width), wide], preferred_element_type=jnp.float32
            )
            return carry

        lax.fori_loop(0, ff_both // cut, multiply, 0)

    def weigh():
        for step in range(1, blocks):
            back = lax.rem(mine + blocks - step, blocks)
            send(
                gates_out.at[step], gates_in.at[back], g_send, g_recv, step - 1, expert=back
            ).wait_recv()
        for seq in range(blocks):
            column = jnp.sum(jnp.where(eye, gates_in[seq][:1, :], 0.0), axis=1, keepdims=True)
            for turn in range(2):
                top = turn * rows + seq * half
                gates_ref[top : top + half, :] = column[turn * half : (turn + 1) * half, :]

    def activate(turn):
        def body(part, carry):
            at = pl.ds(pl.multiple_of(turn * rows + part * strip, strip), strip)
            mean = jnp.sum(ssq_ref[at, :], axis=1, keepdims=True) * (1.0 / model_width)
            inverse = lax.rsqrt(mean + 1e-06)
            gate = acc_ref[at, :ff_local] * inverse
            up = acc_ref[at, ff_local:] * inverse
            value = gate / (1.0 + jnp.exp(-gate)) * up * gates_ref[at, :]
            act_ref[at, :] = value.astype(act_ref.dtype)
            return carry

        lax.fori_loop(0, rows // strip, body, 0)

    def target(rank):
        low = jnp.minimum(donor, last - donor)
        single = jnp.maximum(donor, last - donor) - low
        rest_rank = rank - single
        gap = low - rest_rank // 2
        side = 1 - 2 * lax.rem(jnp.maximum(rest_rank, 0), 2)
        paired = donor + side * gap
        lone = jnp.where(donor < last - donor, last - rank, rank)
        return jnp.where(rank == last, donor, jnp.where(rank < single, lone, paired))

    def add(out, *terms):
        def body(part, carry):
            at = pl.ds(pl.multiple_of(part * strip, strip), strip)
            value = terms[0][at, :].astype(jnp.float32)
            for term in terms[1:]:
                value = value + term[at, :].astype(jnp.float32)
            out[at, :] = value.astype(out.dtype)
            return carry

        lax.fori_loop(0, half // strip, body, 0)

    order = list(range(1, chips)) + [0]

    def own_rows(slot, to_row):
        top = pl.multiple_of((to_row * 2 + core) * half, half)
        return part_ref.at[slot, pl.ds(top, half)]

    def swap(slot, to_row):
        top = pl.multiple_of((to_row * 2 + 1 - core) * half, half)
        place_in = slot * chips + to_row
        return send(
            part_ref.at[slot, pl.ds(top, half)],
            c_in.at[place_in],
            cc_send,
            cc_recv,
            place_in,
            expert=beside,
        )

    def cross(hop, to):
        return send(y_out.at[hop], y_in.at[hop], yy_send, yy_recv, hop, expert=to)

    def produce(slot):
        top = pl.multiple_of(slot // donors * rows, rows)
        left_at = pl.multiple_of(target(lax.rem(slot, donors)) * columns, columns)
        part_ref[slot] = jnp.dot(
            act_ref[pl.ds(top, rows), :],
            down_ref[:, pl.ds(left_at, columns)],
            preferred_element_type=jnp.float32,
        ).astype(part_ref.dtype)
        for step in order:
            swap(slot, lax.rem(row + step, chips)).start()

    def pass_on(slot):
        for step in range(1, chips):
            to_row = lax.rem(row + step, chips)
            hop = (step - 1) * 2 * donors + slot
            swap(slot, to_row).wait_recv()
            add(y_out.at[hop], own_rows(slot, to_row), c_in.at[slot * chips + to_row])
            cross(hop, to_row * 2 + core).start()

    stages = blocks + 1 + donors + 1

    def task(index):
        turn, stage = index // stages, lax.rem(index, stages)

        @pl.when(stage < blocks)
        def _():
            mix(turn, stage)

        @pl.when(stage == blocks)
        def _():
            @pl.when(turn == 0)
            def _():
                own_copies[2].wait()
                weigh()

            activate(turn)

        slot = turn * donors + stage - blocks - 1

        @pl.when((stage > blocks) & (stage < stages - 1))
        def _():
            produce(slot)

        @pl.when(stage > blocks + 1)
        def _():
            pass_on(slot - 1)

    def march(t, carry):
        @pl.when((t < half_count) & (lax.rem(t, per_half) == 0))
        def _():
            partial(t // per_half)

        here = t - donor * HOP

        @pl.when((here >= 0) & (here < count))
        def _():
            @pl.when(donor == 0)
            def _():
                r_out[here] = p_rows(here).astype(r_out.dtype)

            @pl.when(donor > 0)
            def _():
                right(here).wait_recv()

            @pl.when((donor > 0) & (donor < last))
            def _():
                r_out[here] = (p_rows(here) + r_in[here].astype(jnp.float32)).astype(r_out.dtype)

            @pl.when(donor < last)
            def _():
                right(here).start()

        there = t - (last - donor) * HOP

        @pl.when((there >= 0) & (there < count))
        def _():
            @pl.when(donor == last)
            def _():
                l_out[there] = p_rows(there).astype(l_out.dtype)

            @pl.when(donor < last)
            def _():
                left(there).wait_recv()

            @pl.when((donor > 0) & (donor < last))
            def _():
                l_out[there] = (p_rows(there) + l_in[there].astype(jnp.float32)).astype(l_out.dtype)

            @pl.when(donor > 0)
            def _():
                left(there).start()

        done = t - reach

        @pl.when((done >= 0) & (done < count))
        def _():
            goal = tile(row, core, done)

            @pl.when(donor == 0)
            def _():
                goal[...] = (p_rows(done) + l_in[done].astype(jnp.float32)).astype(goal.dtype)

            @pl.when(donor == last)
            def _():
                goal[...] = (p_rows(done) + r_in[done].astype(jnp.float32)).astype(goal.dtype)

            @pl.when((donor > 0) & (donor < last))
            def _():
                goal[...] = (
                    p_rows(done) + r_in[done].astype(jnp.float32) + l_in[done].astype(jnp.float32)
                ).astype(goal.dtype)

            for step in range(1, chips):
                across(step, done, row, lax.rem(row + step, chips) * 2 + core).start()
            over(0, done, row, core).start()

        came = t - reach - lag

        @pl.when((came >= 0) & (came < count))
        def _():
            for step in range(1, chips):
                from_row = lax.rem(row + chips - step, chips)
                across(step, came, from_row, from_row * 2 + core).wait_recv()
                over(step, came, from_row, core).start()

        @pl.when(t < raw_steps)
        def _():
            relay_weights(t)

        ready = t - reach - first_mix

        @pl.when((ready >= 0) & (ready < stages))
        def _():
            task(ready)

        return carry

    steps = count + last * HOP + lag
    lax.fori_loop(0, steps, march, 0)

    def rest(index, carry):
        task(index)
        return carry

    lax.fori_loop(jnp.minimum(steps - reach - first_mix, stages), 2 * stages, rest, 0)

    def shift_right(key):
        return send(zr_out.at[key], zr_in.at[key], zr_send, zr_recv, key, donor=donor + 1)

    def shift_left(key):
        return send(zl_out.at[key], zl_in.at[key], zl_send, zl_recv, key, donor=donor - 1)

    def finish(slot, carry):
        turn = slot // donors
        goal = target(lax.rem(slot, donors))
        key = turn * donors + goal
        swap(slot, row).wait_recv()
        terms = [own_rows(slot, row), c_in.at[slot * chips + row]]
        for step in range(1, chips):
            hop = (step - 1) * 2 * donors + slot
            cross(hop, mine).wait_recv()
            terms.append(y_in.at[hop])

        @pl.when((goal >= donor) & (donor > 0))
        def _():
            shift_right(key).wait_recv()

        @pl.when((goal <= donor) & (donor < last))
        def _():
            shift_left(key).wait_recv()

        @pl.when(goal > donor)
        def _():
            @pl.when(donor == 0)
            def _():
                add(zr_out.at[key], *terms)

            @pl.when(donor > 0)
            def _():
                add(zr_out.at[key], zr_in.at[key], *terms)

            shift_right(key).start()

        @pl.when(goal < donor)
        def _():
            @pl.when(donor == last)
            def _():
                add(zl_out.at[key], *terms)

            @pl.when(donor < last)
            def _():
                add(zl_out.at[key], zl_in.at[key], *terms)

            shift_left(key).start()

        @pl.when(goal == donor)
        def _():
            def close(ends):
                for part in range(columns // width):
                    wide = slice(part * width, (part + 1) * width)

                    def body(index, carry):
                        at = pl.ds(pl.multiple_of(index * strip, strip), strip)
                        to = pl.ds(pl.multiple_of(turn * half + index * strip, strip), strip)
                        down = pl.ds(
                            pl.multiple_of(mine * suffix + turn * half + index * strip, strip), strip
                        )
                        value = full_ref[donor * (columns // width) + part, down, :].astype(jnp.float32)
                        total = terms[0][at, wide].astype(jnp.float32)
                        for term in terms[1:] + ends:
                            total = total + term[at, wide].astype(jnp.float32)
                        out_ref[to, wide] = (value + total).astype(out_ref.dtype)
                        return carry

                    lax.fori_loop(0, half // strip, body, 0)

            @pl.when(donor == 0)
            def _():
                close([zl_in.at[key]])

            @pl.when(donor == last)
            def _():
                close([zr_in.at[key]])

            @pl.when((donor > 0) & (donor < last))
            def _():
                close([zl_in.at[key], zr_in.at[key]])

        return carry

    lax.fori_loop(0, 2 * donors, finish, 0)

    for step in range(1, blocks):
        gates_to(step).wait_send()
    for index in range(seqs_each):

        @pl.when(partner(index) != mine)
        def _():
            hidden_to(index).wait_send()

    for step in range(1, chips):
        heads_y(step, mine, mine).wait_send()
    for step in range(chips):
        heads_c(step, mine).wait_send()

    def drain(chunk, carry):
        @pl.when(donor < last)
        def _():
            right(chunk).wait_send()

        @pl.when(donor > 0)
        def _():
            left(chunk).wait_send()

        for step in range(1, chips):
            across(step, chunk, row, mine).wait_send()
        for step in range(chips):
            over(step, chunk, row, core).wait_send()
        return carry

    lax.fori_loop(0, count, drain, 0)

    def drain_blocks(slot, carry):
        goal = lax.rem(slot, donors)
        for step in range(chips):
            swap(slot, step).wait_send()
        for step in range(1, chips):
            cross((step - 1) * 2 * donors + slot, mine).wait_send()

        @pl.when(goal > donor)
        def _():
            shift_right(slot).wait_send()

        @pl.when(goal < donor)
        def _():
            shift_left(slot).wait_send()

        return carry

    lax.fori_loop(0, 2 * donors, drain_blocks, 0)


def page_kernel(
    experts,
    donors,
    pool_ref,
    table_ref,
    length_ref,
    query_ref,
    fresh_ref,
    head_ref,
    out_buf,
    pages_in,
    sends,
    recvs,
):
    expert, donor = lax.axis_index("expert"), lax.axis_index("donor")
    seqs, kv_heads = out_buf.shape[0], out_buf.shape[1]
    suffix, columns = head_ref.shape
    head_dim = fresh_ref.shape[1] // 2
    order = [
        (step_e, step_z)
        for step_z in [*far_first(donors), 0]
        for step_e in range(experts)
        if step_e or step_z
    ]
    barrier = pltpu.get_barrier_semaphore()

    def ahead(step_e, step_z):
        return lax.rem(expert + step_e, experts), lax.rem(donor + step_z, donors)

    for step_e, step_z in order:
        to_e, to_z = ahead(step_e, step_z)
        pl.semaphore_signal(
            barrier, inc=1, device_id={"expert": to_e, "donor": to_z}, device_id_type=MESH
        )
    mine = expert * donors + donor
    pages, page_len = table_ref.shape[1], pages_in.shape[1]
    slots = seqs
    for seq in range(seqs):
        held = 0
        for index in range(pages):
            named = table_ref[seq, index]
            held = held + jnp.where(named // slots == mine, named % slots, 0)
        for group in range(kv_heads):
            out_buf[seq, group] = pool_ref[held, group]
    lane = lax.broadcasted_iota(jnp.int32, (1, pages * page_len), 1)
    holder = lane // page_len
    first = jnp.zeros_like(lane)
    for index in range(pages):
        first = jnp.where(holder == table_ref[expert, index] // slots, index * page_len, first)
    seen = first + lane % page_len < length_ref[expert]
    bias = jnp.where(seen, 0.0, -jnp.inf)
    pl.semaphore_wait(barrier, experts * donors - 1)

    def page(step_e, step_z):
        to_e, to_z = ahead(step_e, step_z)
        return send(
            out_buf.at[to_e, to_z * kv_heads // donors],
            pages_in.at[mine],
            sends,
            recvs,
            step_e * donors + step_z,
            expert=to_e,
            donor=to_z,
        )

    for step_e, step_z in order:
        page(step_e, step_z).start()
    pages_in[mine] = out_buf[expert, donor * kv_heads // donors]
    for step_e, step_z in order:
        from_e, from_z = ahead(experts - step_e, donors - step_z)
        send(
            out_buf.at[expert, donor * kv_heads // donors],
            pages_in.at[from_e * donors + from_z],
            sends,
            recvs,
            step_e * donors + step_z,
            expert=from_e,
            donor=from_z,
        ).wait_recv()
    keys_count = pages_in.shape[0] * pages_in.shape[1]
    causal = lax.broadcasted_iota(jnp.int32, (suffix, suffix), 0) >= lax.broadcasted_iota(
        jnp.int32, (suffix, suffix), 1
    )
    scale = head_dim ** (-0.5)
    both = (((1,), (1,)), ((), ()))
    for left in range(0, columns, head_dim):
        query = query_ref[:, left : left + head_dim]
        old_keys = pages_in[:, :, :head_dim].reshape(keys_count, head_dim)
        old = lax.dot_general(query, old_keys, both, preferred_element_type=jnp.float32)
        new = lax.dot_general(
            query, fresh_ref[:, :head_dim], both, preferred_element_type=jnp.float32
        )
        old = old * scale + bias
        new = jnp.where(causal, new * scale, -jnp.inf)
        top = jnp.maximum(
            jnp.max(old, axis=1, keepdims=True), jnp.max(new, axis=1, keepdims=True)
        )
        old = jnp.exp(old - top)
        new = jnp.exp(new - top)
        total = jnp.sum(old, axis=1, keepdims=True) + jnp.sum(new, axis=1, keepdims=True)
        old_vals = pages_in[:, :, head_dim:].reshape(keys_count, head_dim)
        mixed = jnp.dot(old.astype(query.dtype), old_vals, preferred_element_type=jnp.float32)
        mixed = mixed + jnp.dot(
            new.astype(query.dtype), fresh_ref[:, head_dim:], preferred_element_type=jnp.float32
        )
        head_ref[:, left : left + head_dim] = (mixed / total).astype(head_ref.dtype)
    for step_e, step_z in order:
        page(step_e, step_z).wait_send()


def page_heads(pool, table, lengths, queries, fresh, experts, donors):
    seqs, kv_heads, page_len, both = pool.shape
    dma = pltpu.SemaphoreType.DMA
    inside = pl.BlockSpec(memory_space=pltpu.VMEM)
    return pl.pallas_call(
        functools.partial(page_kernel, experts, donors),
        out_shape=jax.ShapeDtypeStruct(queries.shape, queries.dtype),
        in_specs=[inside] + [pl.BlockSpec(memory_space=pltpu.SMEM)] * 2 + [inside] * 2,
        out_specs=inside,
        scratch_shapes=[
            pltpu.VMEM((seqs, kv_heads, page_len, both), pool.dtype),
            pltpu.VMEM((experts * donors, page_len, both), pool.dtype),
            dma((experts * donors,)),
            dma((experts * donors,)),
        ],
        compiler_params=pltpu.CompilerParams(collective_id=4, has_side_effects=True),
        name="page_heads",
    )(pool, table, lengths, queries, fresh)


def mix_scratch(heads, out_weight, w_gate_up, chips, donors, piece):
    suffix, head_cols = heads.shape
    blocks = 2 * chips
    width = out_weight.shape[1]
    model_width, ff_local = w_gate_up.shape[1], w_gate_up.shape[3]
    tokens = blocks * suffix
    columns = model_width // donors
    count = tokens // piece
    kind = heads.dtype
    vmem = lambda *shape: pltpu.VMEM(shape, kind)
    wide = lambda *shape: pltpu.VMEM(shape, jnp.float32)
    held = lambda number: pltpu.VMEM((2 * number, suffix // 2, columns), kind)
    return [
        vmem(blocks // donors, suffix, width),
        wide(blocks, 8, suffix),
        wide(blocks, 8, suffix),
        wide(model_width // 128, 128),
        vmem(head_cols, width),
        vmem(3, model_width // 8, 2, ff_local),
        vmem(ff_local, model_width),
        vmem(tokens, head_cols),
        wide(tokens, width),
        vmem(count, piece, width),
        vmem(count, piece, width),
        vmem(count, piece, width),
        vmem(count, piece, width),
        vmem(blocks, tokens, width),
        vmem(model_width, 2 * ff_local),
        vmem(tokens // 2, width),
        wide(tokens, 2 * ff_local),
        wide(tokens, 128),
        vmem(tokens, ff_local),
        wide(tokens, 1),
        vmem(2 * donors, tokens // 2, columns),
        held(chips * donors),
        held((chips - 1) * donors),
        held((chips - 1) * donors),
        held(donors),
        held(donors),
        held(donors),
        held(donors),
    ]


def mix_blocks(
    heads, gain, probs, ids, hidden, out_weight, w_gate_up, w_down, chips, donors, piece, scratch
):
    suffix = heads.shape[0]
    columns = w_gate_up.shape[1] // donors
    count = 2 * chips * suffix // piece
    dma = pltpu.SemaphoreType.DMA
    pair = lambda number: [dma((number,)), dma((number,))]
    inside = pl.BlockSpec(memory_space=pltpu.VMEM)
    outside = pl.BlockSpec(memory_space=pl.ANY)
    return pl.pallas_call(
        functools.partial(mix_kernel, chips, donors, piece),
        out_shape=jax.ShapeDtypeStruct((suffix, columns), heads.dtype),
        in_specs=[inside] * 4 + [outside] * 4,
        out_specs=inside,
        scratch_shapes=scratch
        + [dma((3,)), dma((8,))]
        + pair(2 * chips - 1)
        + pair(2 * chips // donors)
        + pair(chips - 1)
        + pair(chips)
        + pair(count)
        + pair(count)
        + pair((chips - 1) * count)
        + pair(chips * count)
        + pair(2 * chips * donors)
        + pair(2 * (chips - 1) * donors)
        + pair(2 * donors)
        + pair(2 * donors),
        compiler_params=pltpu.CompilerParams(
            collective_id=3, has_side_effects=True, vmem_limit_bytes=VMEM_BYTES
        ),
        name="mix_blocks",
    )(heads, gain, probs, ids, hidden, out_weight, w_gate_up, w_down)


def shards(
    hidden_in,
    queries,
    suffix_kv,
    kv_pool,
    page_table,
    prefix_len,
    out_weight,
    norm_gain,
    expert_ids,
    route_probs,
    w_gate_up,
    w_down,
):
    n_expert = lax.axis_size("expert")
    n_donor = lax.axis_size("donor")
    expert_index = lax.axis_index("expert")
    donor_index = lax.axis_index("donor")
    share_count = n_donor // 2
    seq_count, page_count = page_table.shape
    suffix_len = queries.shape[0]
    kv_heads = suffix_kv.shape[1]
    head_dim = suffix_kv.shape[2] // 2
    page_len = kv_pool.shape[2]
    model_width = hidden_in.shape[1]
    columns = model_width // n_donor
    experts_all = 2 * n_expert
    ff_local = w_gate_up.shape[3]
    my_group = donor_index * kv_heads // n_donor
    owner_index = expert_index * n_donor + donor_index
    owner_of = page_table // seq_count
    held_slot = jnp.sum(jnp.where(owner_of == owner_index, page_table % seq_count, 0), axis=1)
    chips = n_expert // 2
    my_pair = lax.dynamic_index_in_dim(suffix_kv, my_group, 1, keepdims=False)
    scratch = mix_scratch(queries, out_weight, w_gate_up, chips, n_donor, PIECE)
    held_bytes = sum(math.prod(item.shape) * item.dtype.itemsize for item in scratch)
    if held_bytes <= VMEM_BYTES - 4 * 1024 * 1024:
        head_out = page_heads(
            kv_pool, page_table, prefix_len, queries, my_pair, n_expert, n_donor
        )
        layer_out = mix_blocks(
            head_out,
            norm_gain.reshape(-1, 128),
            route_probs.T,
            expert_ids.T,
            hidden_in,
            out_weight,
            w_gate_up,
            w_down,
            chips,
            n_donor,
            PIECE,
            scratch,
        )
        return (layer_out, head_out)

    dest_group = jnp.arange(n_donor, dtype=jnp.int32) * kv_heads // n_donor
    wanted = (held_slot[:, None] * kv_heads + dest_group[None, :]).reshape(-1)
    outgoing = jnp.take(
        kv_pool.reshape(seq_count * kv_heads, page_len, 2 * head_dim), wanted, axis=0
    )
    arrived = lax.all_to_all(outgoing, ("expert", "donor"), split_axis=0, concat_axis=0, tiled=True)
    my_owners = lax.dynamic_index_in_dim(owner_of, expert_index, 0, keepdims=False)
    ordered = jnp.take(arrived, my_owners, axis=0).reshape(page_count * page_len, 2 * head_dim)
    prefix_keys = ordered[:, :head_dim]
    prefix_vals = ordered[:, head_dim:]
    score_scale = head_dim ** (-0.5)
    query_heads = queries.reshape(suffix_len, -1, head_dim)
    fresh_pair = lax.dynamic_index_in_dim(suffix_kv, my_group, 1, keepdims=False)
    causal = jnp.arange(suffix_len)[:, None] >= jnp.arange(suffix_len)[None, :]
    fresh_scores = (
        jnp.einsum(
            "thc,uc->thu", query_heads, fresh_pair[:, :head_dim], preferred_element_type=jnp.float32
        )
        * score_scale
    )
    fresh_scores = jnp.where(causal[:, None, :], fresh_scores, -jnp.inf)
    prefix_tokens = lax.dynamic_index_in_dim(prefix_len, expert_index, 0, keepdims=False)
    block_keys = min(1024, page_count * page_len)
    live_blocks = (prefix_tokens + block_keys - 1) // block_keys

    def block_scores(block_index):
        keys_block = lax.dynamic_slice_in_dim(prefix_keys, block_index * block_keys, block_keys, 0)
        raw_scores = (
            jnp.einsum("thc,kc->thk", query_heads, keys_block, preferred_element_type=jnp.float32)
            * score_scale
        )
        visible = block_index * block_keys + jnp.arange(block_keys) < prefix_tokens
        return jnp.where(visible[None, None, :], raw_scores, -jnp.inf)

    def raise_max(block_index, running):
        return jnp.maximum(running, jnp.max(block_scores(block_index), axis=2))

    row_max = lax.fori_loop(0, live_blocks, raise_max, jnp.max(fresh_scores, axis=2))

    def add_block(block_index, loop_state):
        row_total, weighted = loop_state
        exp_scores = jnp.exp(block_scores(block_index) - row_max[:, :, None])
        vals_block = lax.dynamic_slice_in_dim(prefix_vals, block_index * block_keys, block_keys, 0)
        weighted = weighted + jnp.einsum(
            "thk,kc->thc",
            exp_scores.astype(jnp.bfloat16),
            vals_block,
            preferred_element_type=jnp.float32,
        )
        return (row_total + jnp.sum(exp_scores, axis=2), weighted)

    fresh_exp = jnp.exp(fresh_scores - row_max[:, :, None])
    start_state = (
        jnp.sum(fresh_exp, axis=2),
        jnp.einsum(
            "thu,uc->thc",
            fresh_exp.astype(jnp.bfloat16),
            fresh_pair[:, head_dim:],
            preferred_element_type=jnp.float32,
        ),
    )
    row_total, weighted = lax.fori_loop(0, live_blocks, add_block, start_state)
    head_out = (weighted / row_total[:, :, None]).astype(jnp.bfloat16).reshape(suffix_len, -1)
    gate_weights = route_probs / jnp.sum(route_probs, axis=1, keepdims=True)
    chosen = expert_ids[:, :, None] == jnp.arange(experts_all, dtype=jnp.int32)
    gate_table = jnp.sum(jnp.where(chosen, gate_weights[:, :, None], 0.0), axis=1)
    gate_tables = [gate_table]
    for step in range(1, n_expert):
        pairs = [(source, (source + step) % n_expert) for source in range(n_expert)]
        gate_tables.append(lax.ppermute(gate_table, "expert", pairs))
    from_order = lax.rem(expert_index - jnp.arange(n_expert) + n_expert, n_expert)
    gate_all = jnp.stack(gate_tables)[from_order].reshape(n_expert * suffix_len, experts_all)
    my_expert = owner_index // share_count
    my_gates = lax.dynamic_slice_in_dim(gate_all, my_expert, 1, 1)

    seqs_each = n_expert // n_donor
    width = model_width // n_expert
    hidden_parts = []
    for shift in range(seqs_each):
        pairs = []
        for source in range(n_expert * n_donor):
            seq, part = source // n_donor, source % n_donor
            target = part * seqs_each + (seq + shift) % seqs_each
            pairs.append((source, target * n_donor + seq // seqs_each))
        target = donor_index * seqs_each + lax.rem(expert_index + shift, seqs_each)
        sent = lax.dynamic_slice_in_dim(hidden_in, target * width, width, 1)
        hidden_parts.append(lax.ppermute(sent, ("expert", "donor"), pairs))
    turned = lax.rem(expert_index - jnp.arange(seqs_each) + seqs_each * n_expert, seqs_each)
    hidden_block = jnp.stack(hidden_parts)[turned].reshape(seqs_each * suffix_len, width)

    heads_all = lax.all_gather(head_out, "expert", axis=0, tiled=True)
    w_in, heads_all = lax.optimization_barrier(
        (w_gate_up[0].reshape(model_width, 2 * ff_local), heads_all)
    )
    resid = gather_blocks(heads_all, out_weight, hidden_block, n_expert // 2, n_donor)
    resid_f = resid.astype(jnp.float32)
    inverse = lax.rsqrt(jnp.mean(resid_f * resid_f, axis=1, keepdims=True) + 1e-06)
    normed = (resid_f * inverse * norm_gain.astype(jnp.float32)).astype(jnp.bfloat16)
    gate_up = jnp.dot(
        normed,
        w_in,
        preferred_element_type=jnp.float32,
    )
    activated = (
        jax.nn.silu(gate_up[:, :ff_local]) * gate_up[:, ff_local:] * my_gates
    ).astype(jnp.bfloat16)
    expert_mix = reduce_blocks(activated, w_down[0], n_expert // 2, n_donor)
    resid_mine = lax.dynamic_slice(
        resid,
        (expert_index * suffix_len, donor_index * columns),
        (suffix_len, columns),
    )
    layer_out = (resid_mine.astype(jnp.float32) + expert_mix).astype(
        jnp.bfloat16
    )
    return (layer_out, head_out)


def solution(mesh):
    in_specs = (
        P(("groups", "expert"), None),
        P(("groups", "expert"), "donor"),
        P(("groups", "expert"), None, None),
        P(("groups", "expert", "donor"), None, None, None),
        P("groups", None),
        P("groups"),
        P("donor", "expert"),
        P(),
        P(("groups", "expert"), None),
        P(("groups", "expert"), None),
        P(("expert", "donor"), None, None, None),
        P(("expert", "donor"), None, None),
    )
    out_specs = (P(("groups", "expert"), "donor"), P(("groups", "expert"), "donor"))
    return jax.shard_map(shards, mesh=mesh, in_specs=in_specs, out_specs=out_specs, check_vma=False)
```

```python
import functools
import math

import jax
import jax.numpy as jnp
from jax import lax
from jax.experimental import pallas as pl
from jax.experimental.pallas import tpu as pltpu
from jax.sharding import PartitionSpec as P

MESH = pl.DeviceIdType.MESH
VMEM_BYTES = 60 * 1024 * 1024
PIECE = 32
HOP = 3
LAG = 3


def place():
    expert = lax.axis_index("expert")
    return expert // 2, lax.rem(expert, 2), lax.axis_index("donor")


def send(src, dst, sends, recvs, slot, **where):
    return pltpu.make_async_remote_copy(
        src_ref=src,
        dst_ref=dst,
        send_sem=sends.at[slot],
        recv_sem=recvs.at[slot],
        device_id=where,
        device_id_type=MESH,
    )


def greet(chips, donors):
    row, core, donor = place()
    barrier = pltpu.get_barrier_semaphore()
    pl.semaphore_signal(
        barrier, inc=1, device_id={"expert": row * 2 + 1 - core}, device_id_type=MESH
    )
    for step in range(1, chips):
        other = lax.rem(row + step, chips) * 2 + core
        pl.semaphore_signal(barrier, inc=1, device_id={"expert": other}, device_id_type=MESH)
    for step in range(1, donors):
        other = lax.rem(donor + step, donors)
        pl.semaphore_signal(barrier, inc=1, device_id={"donor": other}, device_id_type=MESH)
    pl.semaphore_wait(barrier, chips + donors - 1)


def far_first(donors):
    return sorted(range(1, donors), key=lambda k: (-min(k, donors - k), k))


def gather_kernel(
    chips,
    donors,
    heads_ref,
    out_ref,
    hidden_ref,
    full_ref,
    terms_ref,
    terms_in,
    block_ref,
    own_sem,
    t_send,
    t_recv,
    z_send,
    z_recv,
    y_send,
    y_recv,
    c_send,
    c_recv,
):
    row, core, donor = place()
    rows, cols = block_ref.shape
    greet(chips, donors)
    strip = 16

    def project(step_z, slot):
        top = pl.multiple_of(lax.rem(donor + step_z, donors) * rows, rows)
        terms_ref[slot] = jnp.dot(
            heads_ref[pl.ds(top, rows), :], out_ref[...], preferred_element_type=jnp.float32
        ).astype(terms_ref.dtype)

    term_copies = {}
    for step in far_first(donors):
        project(step, step)
        copy = send(
            terms_ref.at[step],
            terms_in.at[step - 1],
            t_send,
            t_recv,
            step - 1,
            donor=lax.rem(donor + step, donors),
        )
        copy.start()
        term_copies[step] = copy
    project(0, 0)
    for step in far_first(donors):
        term_copies[step].wait_recv()

    def add(index, carry):
        at = pl.ds(pl.multiple_of(index * strip, strip), strip)
        value = terms_ref[0, at, :].astype(jnp.float32)
        for step in range(1, donors):
            value = value + terms_in[step - 1, at, :].astype(jnp.float32)
        value = value + hidden_ref[at, :].astype(jnp.float32)
        block_ref[at, :] = value.astype(block_ref.dtype)
        return carry

    lax.fori_loop(0, rows // strip, add, 0)

    def slot_of(donor_from, row_from, core_from):
        top = pl.multiple_of(donor_from * rows, rows)
        left = pl.multiple_of((row_from * 2 + core_from) * cols, cols)
        return full_ref.at[pl.ds(top, rows), pl.ds(left, cols)]

    own = pltpu.make_async_copy(block_ref, slot_of(donor, row, core), own_sem)
    own.start()
    started = []

    def along_y(src, step_z, donor_from):
        for step in range(1, chips):
            copy = send(
                src,
                slot_of(donor_from, row, core),
                y_send,
                y_recv,
                step_z * (chips - 1) + step - 1,
                expert=lax.rem(row + step, chips) * 2 + core,
            )
            copy.start()
            started.append(copy)

    def beside(src, step_z, step_y, donor_from, row_from):
        copy = send(
            src,
            slot_of(donor_from, row_from, core),
            c_send,
            c_recv,
            step_z * chips + step_y,
            expert=row * 2 + 1 - core,
        )
        copy.start()
        started.append(copy)

    along_y(block_ref, 0, donor)
    z_copies = {}
    near_first = far_first(donors)[::-1]
    for step in near_first:
        copy = send(
            block_ref,
            slot_of(donor, row, core),
            z_send,
            z_recv,
            step - 1,
            donor=lax.rem(donor + step, donors),
        )
        copy.start()
        z_copies[step] = copy
    beside(block_ref, 0, 0, donor, row)

    def take_y(step_z, donor_from):
        for step in range(1, chips):
            row_from = lax.rem(row + chips - step, chips)
            there = slot_of(donor_from, row_from, core)
            send(
                there,
                there,
                y_send,
                y_recv,
                step_z * (chips - 1) + step - 1,
                expert=row_from * 2 + core,
            ).wait_recv()
            beside(there, step_z, step, donor_from, row_from)

    for step in near_first:
        donor_from = lax.rem(donor + donors - step, donors)
        there = slot_of(donor_from, row, core)
        send(there, there, z_send, z_recv, step - 1, donor=donor_from).wait_recv()
        along_y(there, step, donor_from)
        beside(there, step, 0, donor_from, row)
    for step in [0] + near_first:
        take_y(step, lax.rem(donor + donors - step, donors))
    for step_z in range(donors):
        donor_from = lax.rem(donor + donors - step_z, donors)
        for step_y in range(chips):
            row_from = lax.rem(row + chips - step_y, chips)
            there = slot_of(donor_from, row_from, 1 - core)
            send(
                there, there, c_send, c_recv, step_z * chips + step_y, expert=row * 2 + 1 - core
            ).wait_recv()
    own.wait()
    for copy in list(term_copies.values()) + list(z_copies.values()) + started:
        copy.wait_send()


def gather_blocks(heads, out_weight, block, chips, donors):
    rows, cols = block.shape
    dma = pltpu.SemaphoreType.DMA
    return pl.pallas_call(
        functools.partial(gather_kernel, chips, donors),
        out_shape=jax.ShapeDtypeStruct((rows * donors, cols * chips * 2), block.dtype),
        in_specs=[pl.BlockSpec(memory_space=pltpu.VMEM)] * 3,
        out_specs=pl.BlockSpec(memory_space=pltpu.VMEM),
        scratch_shapes=[
            pltpu.VMEM((donors, rows, cols), block.dtype),
            pltpu.VMEM((donors - 1, rows, cols), block.dtype),
            pltpu.VMEM((rows, cols), block.dtype),
            dma,
            dma((donors - 1,)),
            dma((donors - 1,)),
            dma((donors - 1,)),
            dma((donors - 1,)),
            dma((donors * (chips - 1),)),
            dma((donors * (chips - 1),)),
            dma((donors * chips,)),
            dma((donors * chips,)),
        ],
        compiler_params=pltpu.CompilerParams(collective_id=1, has_side_effects=True),
        name="gather_blocks",
    )(heads, out_weight, block)


def reduce_kernel(
    chips,
    donors,
    act_ref,
    down_ref,
    total_ref,
    part_ref,
    c_in,
    y_out,
    y_in,
    z_out,
    z_in,
    c_send,
    c_recv,
    y_send,
    y_recv,
    z_send,
    z_recv,
):
    row, core, donor = place()
    rows, cols = total_ref.shape
    greet(chips, donors)
    order = far_first(donors) + [0]
    strip = 16

    def tile(row_to, core_to, step_z):
        top = pl.multiple_of((row_to * 2 + core_to) * rows, rows)
        left = pl.multiple_of(lax.rem(donor + step_z, donors) * cols, cols)
        return part_ref.at[pl.ds(top, rows), pl.ds(left, cols)]

    def add(out, *terms):
        def body(index, carry):
            at = pl.ds(pl.multiple_of(index * strip, strip), strip)
            value = terms[0][at, :].astype(jnp.float32)
            for term in terms[1:]:
                value = value + term[at, :].astype(jnp.float32)
            out[at, :] = value.astype(out.dtype)
            return carry

        lax.fori_loop(0, rows // strip, body, 0)

    started = []
    arrivals = {}

    def multiply(step_z):
        left = pl.multiple_of(lax.rem(donor + step_z, donors) * cols, cols)

        def body(index, carry):
            at = pl.ds(pl.multiple_of(index * rows, rows), rows)
            part_ref[at, pl.ds(left, cols)] = jnp.dot(
                act_ref[at, :],
                down_ref[:, pl.ds(left, cols)],
                preferred_element_type=jnp.float32,
            ).astype(part_ref.dtype)
            return carry

        lax.fori_loop(0, chips * 2, body, 0)

    def beside(step_z):
        for step_y in range(chips - 1, -1, -1):
            slot = step_z * chips + step_y
            copy = send(
                tile(lax.rem(row + step_y, chips), 1 - core, step_z),
                c_in.at[slot],
                c_send,
                c_recv,
                slot,
                expert=row * 2 + 1 - core,
            )
            copy.start()
            started.append(copy)

    def along_y(step_z):
        for step_y in range(chips - 1, 0, -1):
            row_to = lax.rem(row + step_y, chips)
            slot = step_z * chips + step_y
            send(
                c_in.at[slot], c_in.at[slot], c_send, c_recv, slot, expert=row * 2 + 1 - core
            ).wait_recv()
            hop = step_z * (chips - 1) + step_y - 1
            add(y_out.at[hop], tile(row_to, core, step_z), c_in.at[slot])
            copy = send(
                y_out.at[hop], y_in.at[hop], y_send, y_recv, hop, expert=row_to * 2 + core
            )
            copy.start()
            arrivals[hop] = copy
            started.append(copy)

    for index, step_z in enumerate(order):
        multiply(step_z)
        beside(step_z)
        if index:
            along_y(order[index - 1])
    along_y(order[-1])
    for step_z in order:
        slot = step_z * chips
        send(
            c_in.at[slot], c_in.at[slot], c_send, c_recv, slot, expert=row * 2 + 1 - core
        ).wait_recv()
        terms = [tile(row, core, step_z), c_in.at[slot]]
        for step_y in range(1, chips):
            hop = step_z * (chips - 1) + step_y - 1
            arrivals[hop].wait_recv()
            terms.append(y_in.at[hop])
        if step_z:
            add(z_out.at[step_z - 1], *terms)
            copy = send(
                z_out.at[step_z - 1],
                z_in.at[step_z - 1],
                z_send,
                z_recv,
                step_z - 1,
                donor=lax.rem(donor + step_z, donors),
            )
            copy.start()
            arrivals["z", step_z] = copy
            started.append(copy)
        else:
            for step in order[:-1]:
                arrivals["z", step].wait_recv()
                terms.append(z_in.at[step - 1])
            add(total_ref, *terms)
    for copy in started:
        copy.wait_send()


def reduce_blocks(activated, down, chips, donors):
    rows, cols = activated.shape[0] // (chips * 2), down.shape[1] // donors
    dma = pltpu.SemaphoreType.DMA
    held = lambda count: pltpu.VMEM((count, rows, cols), activated.dtype)
    return pl.pallas_call(
        functools.partial(reduce_kernel, chips, donors),
        out_shape=jax.ShapeDtypeStruct((rows, cols), jnp.float32),
        in_specs=[pl.BlockSpec(memory_space=pltpu.VMEM)] * 2,
        out_specs=pl.BlockSpec(memory_space=pltpu.VMEM),
        scratch_shapes=[
            pltpu.VMEM((activated.shape[0], down.shape[1]), activated.dtype),
            held(donors * chips),
            held(donors * (chips - 1)),
            held(donors * (chips - 1)),
            held(donors - 1),
            held(donors - 1),
            dma((donors * chips,)),
            dma((donors * chips,)),
            dma((donors * (chips - 1),)),
            dma((donors * (chips - 1),)),
            dma((donors - 1,)),
            dma((donors - 1,)),
        ],
        compiler_params=pltpu.CompilerParams(collective_id=2, has_side_effects=True),
        name="reduce_blocks",
    )(activated, down)


def mix_kernel(
    chips,
    donors,
    piece,
    heads_in,
    gain_ref,
    probs_ref,
    ids_ref,
    hidden_hbm,
    outw_hbm,
    raw_hbm,
    down_hbm,
    out_ref,
    hidden_ref,
    gates_out,
    gates_in,
    gain_wide,
    outw_ref,
    raw_ref,
    down_ref,
    heads_ref,
    p_ref,
    r_out,
    r_in,
    l_out,
    l_in,
    full_ref,
    w_ref,
    x_ref,
    acc_ref,
    ssq_ref,
    act_ref,
    gates_ref,
    part_ref,
    c_in,
    y_out,
    y_in,
    zr_out,
    zr_in,
    zl_out,
    zl_in,
    local_sem,
    raw_sem,
    g_send,
    g_recv,
    h_send,
    h_recv,
    hy_send,
    hy_recv,
    hc_send,
    hc_recv,
    r_send,
    r_recv,
    l_send,
    l_recv,
    y_send,
    y_recv,
    c_send,
    c_recv,
    cc_send,
    cc_recv,
    yy_send,
    yy_recv,
    zr_send,
    zr_recv,
    zl_send,
    zl_recv,
):
    row, core, donor = place()
    mine = row * 2 + core
    beside = row * 2 + 1 - core
    suffix, head_cols = heads_in.shape
    blocks, tokens, width = full_ref.shape
    model_width, ff_both = w_ref.shape
    ff_local = ff_both // 2
    seqs_each = hidden_ref.shape[0]
    per_seq = suffix // piece
    count = blocks * per_seq
    per_group = count // chips
    group_rows = 2 * suffix
    columns = out_ref.shape[1]
    last = donors - 1
    lag = LAG
    first_mix = per_group + lag
    raw_steps, raw_slots, raw_rows = raw_sem.shape[0], raw_ref.shape[0], raw_ref.shape[1]
    relay = min(128, raw_rows)
    strip = 16

    own_copies = [
        pltpu.make_async_copy(outw_hbm, outw_ref, local_sem.at[0]),
        pltpu.make_async_copy(heads_in, heads_ref.at[pl.ds(mine * suffix, suffix)], local_sem.at[1]),
        pltpu.make_async_copy(down_hbm.at[0], down_ref, local_sem.at[2]),
    ]
    own_copies[0].start()
    own_copies[1].start()

    def raw_copy(index):
        at = pl.ds(pl.multiple_of(index * raw_rows, raw_rows), raw_rows)
        return pltpu.make_async_copy(
            raw_hbm.at[0, at], raw_ref.at[lax.rem(index, raw_slots)], raw_sem.at[index]
        )

    for index in range(raw_slots):
        raw_copy(index).start()
    own_copies[2].start()

    barrier = pltpu.get_barrier_semaphore()
    for step in range(1, blocks):
        other = lax.rem(mine + step, blocks)
        pl.semaphore_signal(barrier, inc=1, device_id={"expert": other}, device_id_type=MESH)

    @pl.when(donor > 0)
    def _():
        pl.semaphore_signal(barrier, inc=1, device_id={"donor": donor - 1}, device_id_type=MESH)

    @pl.when(donor < last)
    def _():
        pl.semaphore_signal(barrier, inc=1, device_id={"donor": donor + 1}, device_id_type=MESH)

    gain_wide[...] = gain_ref[...].astype(jnp.float32)
    acc_ref[...] = jnp.zeros_like(acc_ref)
    ssq_ref[...] = jnp.zeros_like(ssq_ref)
    pl.semaphore_wait(barrier, blocks - 1 + jnp.minimum(donor, 1) + jnp.minimum(last - donor, 1))

    def heads_of(seq):
        return heads_ref.at[pl.ds(pl.multiple_of(seq * suffix, suffix), suffix)]

    def heads_y(step, seq, to):
        return send(heads_of(seq), heads_of(seq), hy_send, hy_recv, step - 1, expert=to)

    def heads_c(slot, seq):
        return send(heads_of(seq), heads_of(seq), hc_send, hc_recv, slot, expert=beside)

    def gates_to(step):
        return send(
            gates_out.at[step],
            gates_in.at[mine],
            g_send,
            g_recv,
            step - 1,
            expert=lax.rem(mine + step, blocks),
        )

    def partner(index):
        return lax.rem(donor - lax.rem(mine, donors) + donors, donors) + donors * index

    def hidden_to(index):
        at = pl.ds(pl.multiple_of(partner(index) * width, width), width)
        slot = mine // donors
        return pltpu.make_async_remote_copy(
            src_ref=hidden_hbm.at[:, at],
            dst_ref=hidden_ref.at[slot],
            send_sem=h_send.at[index],
            recv_sem=h_recv.at[slot],
            device_id={"expert": partner(index)},
            device_id_type=MESH,
        )

    def hidden_own(index):
        at = pl.ds(pl.multiple_of(mine * width, width), width)
        return pltpu.make_async_copy(hidden_hbm.at[:, at], hidden_ref.at[index], h_recv.at[index])

    own_copies[1].wait()
    heads_c(0, mine).start()
    for step in range(1, chips):
        heads_y(step, mine, lax.rem(row + step, chips) * 2 + core).start()
    for index in range(seqs_each):

        @pl.when(partner(index) != mine)
        def _():
            hidden_to(index).start()

        @pl.when(partner(index) == mine)
        def _():
            hidden_own(index).start()

    square = (suffix, suffix)
    eye = lax.broadcasted_iota(jnp.int32, square, 0) == lax.broadcasted_iota(jnp.int32, square, 1)
    parts_of = donors // 2
    share = probs_ref[...] / jnp.sum(probs_ref[...], axis=0, keepdims=True)
    for step in range(blocks):
        named = (lax.rem(mine + step, blocks) * donors + donor) // parts_of
        line = jnp.sum(jnp.where(ids_ref[...] == named, share, 0.0), axis=0, keepdims=True)
        if step:
            gates_out[step] = jnp.broadcast_to(line, gates_out.shape[1:])
            gates_to(step).start()
        else:
            gates_in[mine] = jnp.broadcast_to(line, gates_out.shape[1:])
    own_copies[0].wait()

    def seq_at(from_row, from_core, index):
        return lax.rem(from_row + index // 2, chips) * 2 + lax.rem(from_core + lax.rem(index, 2), 2)

    def tile(from_row, from_core, chunk):
        seq = seq_at(from_row, from_core, chunk // per_seq)
        top = pl.multiple_of(seq * suffix + lax.rem(chunk, per_seq) * piece, piece)
        return full_ref.at[from_row * 2 + from_core, pl.ds(top, piece)]

    def right(chunk):
        return send(r_out.at[chunk], r_in.at[chunk], r_send, r_recv, chunk, donor=donor + 1)

    def left(chunk):
        return send(l_out.at[chunk], l_in.at[chunk], l_send, l_recv, chunk, donor=donor - 1)

    def across(step, chunk, from_row, to):
        there = tile(from_row, core, chunk)
        return send(there, there, y_send, y_recv, (step - 1) * count + chunk, expert=to)

    def over(step, chunk, from_row, from_core):
        there = tile(from_row, from_core, chunk)
        return send(there, there, c_send, c_recv, step * count + chunk, expert=beside)

    reach = jnp.maximum(donor, last - donor) * HOP

    def partial(index):
        seq = seq_at(row, core, index)
        step = index // 2

        @pl.when((index > 0) & (lax.rem(index, 2) == 0))
        def _():
            back = lax.rem(chips - step, chips)
            copy = send(
                heads_of(seq), heads_of(seq), hy_send, hy_recv, back - 1, expert=beside
            )
            copy.wait_recv()
            heads_c(back, seq).start()

        @pl.when(lax.rem(index, 2) == 1)
        def _():
            heads_c(lax.rem(chips - step, chips), seq).wait_recv()

        at = pl.ds(pl.multiple_of(index * suffix, suffix), suffix)
        p_ref[at, :] = jnp.dot(
            heads_ref[pl.ds(pl.multiple_of(seq * suffix, suffix), suffix), :],
            outw_ref[...],
            preferred_element_type=jnp.float32,
        )

        for index in range(seqs_each):

            @pl.when(partner(index) == seq)
            def _():
                hidden_own(index).wait()
                p_ref[at, :] = p_ref[at, :] + hidden_ref[index].astype(jnp.float32)

    def p_rows(chunk):
        return p_ref[pl.ds(pl.multiple_of(chunk * piece, piece), piece), :]

    def relay_weights(index):
        raw_copy(index).wait()
        half = lax.broadcasted_iota(jnp.int32, (relay, 2 * relay), 0)
        whole = lax.broadcasted_iota(jnp.int32, (relay, 2 * relay), 1)

        def body(part, carry):
            at = pl.ds(pl.multiple_of(index * raw_rows + part * relay, relay), relay)
            from_at = pl.ds(pl.multiple_of(part * relay, relay), relay)
            both = raw_ref[lax.rem(index, raw_slots), from_at].reshape(2 * relay, ff_local)
            for side in range(2):
                pick = (whole == 2 * half + side).astype(raw_ref.dtype)
                w_ref[at, side * ff_local : (side + 1) * ff_local] = jnp.dot(
                    pick, both, preferred_element_type=jnp.float32
                ).astype(w_ref.dtype)
            return carry

        lax.fori_loop(0, raw_rows // relay, body, 0)

        @pl.when(index + raw_slots < raw_steps)
        def _():
            raw_copy(index + raw_slots).start()

    cut = ff_both // 3

    def mix(turn, index):
        from_row = lax.rem(row + index // 2, chips)
        from_core = lax.rem(core + lax.rem(index, 2), 2)
        back = lax.rem(chips - index // 2, chips)

        @pl.when(lax.rem(index, 2) == 1)
        def _():
            def body(chunk, carry):
                over(back, turn * per_group + chunk, from_row, from_core).wait_recv()
                return carry

            lax.fori_loop(0, per_group, body, 0)

        block = from_row * 2 + from_core
        group = lax.rem(from_row + turn, chips)
        top = pl.multiple_of(group * group_rows, group_rows)
        left_at = pl.multiple_of(block * width, width)
        lanes = gain_wide.shape[1]
        tiles = width // lanes
        gain = gain_wide[pl.ds(pl.multiple_of(block * tiles, tiles), tiles), :]

        def scale(part, carry):
            here = pl.ds(pl.multiple_of(part * strip, strip), strip)
            at = pl.ds(pl.multiple_of(top + part * strip, strip), strip)
            total = ssq_ref[at, :]
            for part_at in range(tiles):
                wide = slice(part_at * lanes, (part_at + 1) * lanes)
                value = full_ref[block, at, wide].astype(jnp.float32)
                x_ref[here, wide] = (value * gain[part_at : part_at + 1, :]).astype(x_ref.dtype)
                total = total + value * value
            ssq_ref[at, :] = total
            return carry

        lax.fori_loop(0, group_rows // strip, scale, 0)
        at = pl.ds(top, group_rows)

        def multiply(part, carry):
            wide = pl.ds(pl.multiple_of(part * cut, cut), cut)
            acc_ref[at, wide] = acc_ref[at, wide] + jnp.dot(
                x_ref[...], w_ref[pl.ds(left_at, width), wide], preferred_element_type=jnp.float32
            )
            return carry

        lax.fori_loop(0, ff_both // cut, multiply, 0)

    early = blocks * (chips - 1)

    def march(t, carry):
        @pl.when((t < count) & (lax.rem(t, per_seq) == 0))
        def _():
            partial(t // per_seq)

        here = t - donor * HOP

        @pl.when((here >= 0) & (here < count))
        def _():
            @pl.when(donor == 0)
            def _():
                r_out[here] = p_rows(here).astype(r_out.dtype)

            @pl.when(donor > 0)
            def _():
                right(here).wait_recv()

            @pl.when((donor > 0) & (donor < last))
            def _():
                r_out[here] = (p_rows(here) + r_in[here].astype(jnp.float32)).astype(r_out.dtype)

            @pl.when(donor < last)
            def _():
                right(here).start()

        there = t - (last - donor) * HOP

        @pl.when((there >= 0) & (there < count))
        def _():
            @pl.when(donor == last)
            def _():
                l_out[there] = p_rows(there).astype(l_out.dtype)

            @pl.when(donor < last)
            def _():
                left(there).wait_recv()

            @pl.when((donor > 0) & (donor < last))
            def _():
                l_out[there] = (p_rows(there) + l_in[there].astype(jnp.float32)).astype(l_out.dtype)

            @pl.when(donor > 0)
            def _():
                left(there).start()

        done = t - reach

        @pl.when((done >= 0) & (done < count))
        def _():
            goal = tile(row, core, done)

            @pl.when(donor == 0)
            def _():
                goal[...] = (p_rows(done) + l_in[done].astype(jnp.float32)).astype(goal.dtype)

            @pl.when(donor == last)
            def _():
                goal[...] = (p_rows(done) + r_in[done].astype(jnp.float32)).astype(goal.dtype)

            @pl.when((donor > 0) & (donor < last))
            def _():
                goal[...] = (
                    p_rows(done) + r_in[done].astype(jnp.float32) + l_in[done].astype(jnp.float32)
                ).astype(goal.dtype)

            for step in range(1, chips):
                across(step, done, row, lax.rem(row + step, chips) * 2 + core).start()
            over(0, done, row, core).start()

        came = t - reach - lag

        @pl.when((came >= 0) & (came < count))
        def _():
            for step in range(1, chips):
                from_row = lax.rem(row + chips - step, chips)
                across(step, came, from_row, from_row * 2 + core).wait_recv()
                over(step, came, from_row, core).start()

        @pl.when(t < raw_steps)
        def _():
            relay_weights(t)

        ready = t - reach - first_mix

        @pl.when((ready >= 0) & (ready < early))
        def _():
            mix(ready // blocks, lax.rem(ready, blocks))

        return carry

    steps = count + last * HOP + lag
    lax.fori_loop(0, steps, march, 0)

    def rest(index, carry):
        mix(index // blocks, lax.rem(index, blocks))
        return carry

    lax.fori_loop(jnp.minimum(steps - reach - first_mix, early), early, rest, 0)
    own_copies[2].wait()

    for step in range(1, blocks):
        back = lax.rem(mine + blocks - step, blocks)
        send(
            gates_out.at[step], gates_in.at[back], g_send, g_recv, step - 1, expert=back
        ).wait_recv()

    def activate(group):
        for side in range(2):
            seq = group * 2 + side
            gates_ref[side * suffix : (side + 1) * suffix, :] = jnp.sum(
                jnp.where(eye, gates_in[seq][:1, :], 0.0), axis=1, keepdims=True
            )

        def body(part, carry):
            at = pl.ds(pl.multiple_of(group * group_rows + part * strip, strip), strip)
            here = pl.ds(pl.multiple_of(part * strip, strip), strip)
            mean = jnp.sum(ssq_ref[at, :], axis=1, keepdims=True) * (1.0 / model_width)
            inverse = lax.rsqrt(mean + 1e-06)
            gate = acc_ref[at, :ff_local] * inverse
            up = acc_ref[at, ff_local:] * inverse
            value = gate / (1.0 + jnp.exp(-gate)) * up * gates_ref[here, :]
            act_ref[at, :] = value.astype(act_ref.dtype)
            return carry

        lax.fori_loop(0, group_rows // strip, body, 0)

    def target(rank):
        low = jnp.minimum(donor, last - donor)
        single = jnp.maximum(donor, last - donor) - low
        rest_rank = rank - single
        gap = low - rest_rank // 2
        side = 1 - 2 * lax.rem(jnp.maximum(rest_rank, 0), 2)
        paired = donor + side * gap
        lone = jnp.where(donor < last - donor, last - rank, rank)
        return jnp.where(rank == last, donor, jnp.where(rank < single, lone, paired))

    def add(out, *terms):
        def body(part, carry):
            at = pl.ds(pl.multiple_of(part * strip, strip), strip)
            value = terms[0][at, :].astype(jnp.float32)
            for term in terms[1:]:
                value = value + term[at, :].astype(jnp.float32)
            out[at, :] = value.astype(out.dtype)
            return carry

        lax.fori_loop(0, suffix // strip, body, 0)

    order = list(range(1, chips)) + [0]

    def own_half(slot):
        return part_ref.at[slot, pl.ds(pl.multiple_of(core * suffix, suffix), suffix)]

    def swap(slot):
        away = part_ref.at[slot, pl.ds(pl.multiple_of((1 - core) * suffix, suffix), suffix)]
        return send(away, c_in.at[slot], cc_send, cc_recv, slot, expert=beside)

    def cross(hop, to):
        return send(y_out.at[hop], y_in.at[hop], yy_send, yy_recv, hop, expert=to)

    def produce(step, rank):
        slot = step * donors + rank
        top = pl.multiple_of(lax.rem(row + step, chips) * group_rows, group_rows)
        left_at = pl.multiple_of(target(rank) * columns, columns)
        part_ref[slot] = jnp.dot(
            act_ref[pl.ds(top, group_rows), :],
            down_ref[:, pl.ds(left_at, columns)],
            preferred_element_type=jnp.float32,
        ).astype(part_ref.dtype)
        swap(slot).start()

    def pass_on(step, rank):
        slot = step * donors + rank
        hop = (step - 1) * donors + rank
        swap(slot).wait_recv()
        add(y_out.at[hop], own_half(slot), c_in.at[slot])
        cross(hop, lax.rem(row + step, chips) * 2 + core).start()

    for step in order:
        for side in range(2):
            mix(chips - 1, 2 * ((step + 1) % chips) + side)
        activate(lax.rem(row + step, chips))
        if step:

            def body(rank, carry):
                produce(step, rank)

                @pl.when(rank > 0)
                def _():
                    pass_on(step, rank - 1)

                return carry

            lax.fori_loop(0, donors, body, 0)
            pass_on(step, donors - 1)
        else:

            def body(rank, carry):
                produce(0, rank)
                return carry

            lax.fori_loop(0, donors, body, 0)

    def shift_right(goal):
        return send(zr_out.at[goal], zr_in.at[goal], zr_send, zr_recv, goal, donor=donor + 1)

    def shift_left(goal):
        return send(zl_out.at[goal], zl_in.at[goal], zl_send, zl_recv, goal, donor=donor - 1)

    def finish(rank, carry):
        goal = target(rank)
        swap(rank).wait_recv()
        terms = [own_half(rank), c_in.at[rank]]
        for step in range(1, chips):
            hop = (step - 1) * donors + rank
            cross(hop, mine).wait_recv()
            terms.append(y_in.at[hop])

        @pl.when((goal >= donor) & (donor > 0))
        def _():
            shift_right(goal).wait_recv()

        @pl.when((goal <= donor) & (donor < last))
        def _():
            shift_left(goal).wait_recv()

        @pl.when(goal > donor)
        def _():
            @pl.when(donor == 0)
            def _():
                add(zr_out.at[goal], *terms)

            @pl.when(donor > 0)
            def _():
                add(zr_out.at[goal], zr_in.at[goal], *terms)

            shift_right(goal).start()

        @pl.when(goal < donor)
        def _():
            @pl.when(donor == last)
            def _():
                add(zl_out.at[goal], *terms)

            @pl.when(donor < last)
            def _():
                add(zl_out.at[goal], zl_in.at[goal], *terms)

            shift_left(goal).start()

        @pl.when(goal == donor)
        def _():
            def close(ends):
                for part in range(columns // width):
                    wide = slice(part * width, (part + 1) * width)

                    def body(index, carry):
                        at = pl.ds(pl.multiple_of(index * strip, strip), strip)
                        down = pl.ds(pl.multiple_of(mine * suffix + index * strip, strip), strip)
                        value = full_ref[donor * (columns // width) + part, down, :].astype(jnp.float32)
                        total = terms[0][at, wide].astype(jnp.float32)
                        for term in terms[1:] + ends:
                            total = total + term[at, wide].astype(jnp.float32)
                        out_ref[at, wide] = (value + total).astype(out_ref.dtype)
                        return carry

                    lax.fori_loop(0, suffix // strip, body, 0)

            @pl.when(donor == 0)
            def _():
                close([zl_in.at[donor]])

            @pl.when(donor == last)
            def _():
                close([zr_in.at[donor]])

            @pl.when((donor > 0) & (donor < last))
            def _():
                close([zl_in.at[donor], zr_in.at[donor]])

        return carry

    lax.fori_loop(0, donors, finish, 0)

    for step in range(1, blocks):
        gates_to(step).wait_send()
    for index in range(seqs_each):

        @pl.when(partner(index) != mine)
        def _():
            hidden_to(index).wait_send()

    for step in range(1, chips):
        heads_y(step, mine, mine).wait_send()
    for step in range(chips):
        heads_c(step, mine).wait_send()

    def drain(chunk, carry):
        @pl.when(donor < last)
        def _():
            right(chunk).wait_send()

        @pl.when(donor > 0)
        def _():
            left(chunk).wait_send()

        for step in range(1, chips):
            across(step, chunk, row, mine).wait_send()
        for step in range(chips):
            over(step, chunk, row, core).wait_send()
        return carry

    lax.fori_loop(0, count, drain, 0)

    def drain_blocks(goal, carry):
        for step in range(chips):
            swap(step * donors + goal).wait_send()
        for step in range(1, chips):
            cross((step - 1) * donors + goal, mine).wait_send()

        @pl.when(goal > donor)
        def _():
            shift_right(goal).wait_send()

        @pl.when(goal < donor)
        def _():
            shift_left(goal).wait_send()

        return carry

    lax.fori_loop(0, donors, drain_blocks, 0)


def page_kernel(
    experts,
    donors,
    pool_ref,
    table_ref,
    length_ref,
    query_ref,
    fresh_ref,
    head_ref,
    out_buf,
    pages_in,
    sends,
    recvs,
):
    expert, donor = lax.axis_index("expert"), lax.axis_index("donor")
    seqs, kv_heads = out_buf.shape[0], out_buf.shape[1]
    suffix, columns = head_ref.shape
    head_dim = fresh_ref.shape[1] // 2
    order = [
        (step_e, step_z)
        for step_z in [*far_first(donors), 0]
        for step_e in range(experts)
        if step_e or step_z
    ]
    barrier = pltpu.get_barrier_semaphore()

    def ahead(step_e, step_z):
        return lax.rem(expert + step_e, experts), lax.rem(donor + step_z, donors)

    for step_e, step_z in order:
        to_e, to_z = ahead(step_e, step_z)
        pl.semaphore_signal(
            barrier, inc=1, device_id={"expert": to_e, "donor": to_z}, device_id_type=MESH
        )
    mine = expert * donors + donor
    pages, page_len = table_ref.shape[1], pages_in.shape[1]
    slots = seqs
    for seq in range(seqs):
        held = 0
        for index in range(pages):
            named = table_ref[seq, index]
            held = held + jnp.where(named // slots == mine, named % slots, 0)
        for group in range(kv_heads):
            out_buf[seq, group] = pool_ref[held, group]
    lane = lax.broadcasted_iota(jnp.int32, (1, pages * page_len), 1)
    holder = lane // page_len
    first = jnp.zeros_like(lane)
    for index in range(pages):
        first = jnp.where(holder == table_ref[expert, index] // slots, index * page_len, first)
    seen = first + lane % page_len < length_ref[expert]
    bias = jnp.where(seen, 0.0, -jnp.inf)
    pl.semaphore_wait(barrier, experts * donors - 1)

    def page(step_e, step_z):
        to_e, to_z = ahead(step_e, step_z)
        return send(
            out_buf.at[to_e, to_z * kv_heads // donors],
            pages_in.at[mine],
            sends,
            recvs,
            step_e * donors + step_z,
            expert=to_e,
            donor=to_z,
        )

    for step_e, step_z in order:
        page(step_e, step_z).start()
    pages_in[mine] = out_buf[expert, donor * kv_heads // donors]
    for step_e, step_z in order:
        from_e, from_z = ahead(experts - step_e, donors - step_z)
        send(
            out_buf.at[expert, donor * kv_heads // donors],
            pages_in.at[from_e * donors + from_z],
            sends,
            recvs,
            step_e * donors + step_z,
            expert=from_e,
            donor=from_z,
        ).wait_recv()
    keys_count = pages_in.shape[0] * pages_in.shape[1]
    causal = lax.broadcasted_iota(jnp.int32, (suffix, suffix), 0) >= lax.broadcasted_iota(
        jnp.int32, (suffix, suffix), 1
    )
    scale = head_dim ** (-0.5)
    both = (((1,), (1,)), ((), ()))
    for left in range(0, columns, head_dim):
        query = query_ref[:, left : left + head_dim]
        old_keys = pages_in[:, :, :head_dim].reshape(keys_count, head_dim)
        old = lax.dot_general(query, old_keys, both, preferred_element_type=jnp.float32)
        new = lax.dot_general(
            query, fresh_ref[:, :head_dim], both, preferred_element_type=jnp.float32
        )
        old = old * scale + bias
        new = jnp.where(causal, new * scale, -jnp.inf)
        top = jnp.maximum(
            jnp.max(old, axis=1, keepdims=True), jnp.max(new, axis=1, keepdims=True)
        )
        old = jnp.exp(old - top)
        new = jnp.exp(new - top)
        total = jnp.sum(old, axis=1, keepdims=True) + jnp.sum(new, axis=1, keepdims=True)
        old_vals = pages_in[:, :, head_dim:].reshape(keys_count, head_dim)
        mixed = jnp.dot(old.astype(query.dtype), old_vals, preferred_element_type=jnp.float32)
        mixed = mixed + jnp.dot(
            new.astype(query.dtype), fresh_ref[:, head_dim:], preferred_element_type=jnp.float32
        )
        head_ref[:, left : left + head_dim] = (mixed / total).astype(head_ref.dtype)
    for step_e, step_z in order:
        page(step_e, step_z).wait_send()


def page_heads(pool, table, lengths, queries, fresh, experts, donors):
    seqs, kv_heads, page_len, both = pool.shape
    dma = pltpu.SemaphoreType.DMA
    inside = pl.BlockSpec(memory_space=pltpu.VMEM)
    return pl.pallas_call(
        functools.partial(page_kernel, experts, donors),
        out_shape=jax.ShapeDtypeStruct(queries.shape, queries.dtype),
        in_specs=[inside] + [pl.BlockSpec(memory_space=pltpu.SMEM)] * 2 + [inside] * 2,
        out_specs=inside,
        scratch_shapes=[
            pltpu.VMEM((seqs, kv_heads, page_len, both), pool.dtype),
            pltpu.VMEM((experts * donors, page_len, both), pool.dtype),
            dma((experts * donors,)),
            dma((experts * donors,)),
        ],
        compiler_params=pltpu.CompilerParams(collective_id=4, has_side_effects=True),
        name="page_heads",
    )(pool, table, lengths, queries, fresh)


def relay_steps(suffix, chips, donors, piece):
    before_mix = 2 * suffix // piece + LAG + HOP * (donors // 2)
    return min(16, 1 << (before_mix.bit_length() - 1))


def mix_scratch(heads, out_weight, w_gate_up, chips, donors, piece):
    suffix, head_cols = heads.shape
    blocks = 2 * chips
    width = out_weight.shape[1]
    model_width, ff_local = w_gate_up.shape[1], w_gate_up.shape[3]
    tokens = blocks * suffix
    columns = model_width // donors
    count = tokens // piece
    kind = heads.dtype
    vmem = lambda *shape: pltpu.VMEM(shape, kind)
    wide = lambda *shape: pltpu.VMEM(shape, jnp.float32)
    held = lambda number: pltpu.VMEM((number, suffix, columns), kind)
    return [
        vmem(blocks // donors, suffix, width),
        wide(blocks, 8, suffix),
        wide(blocks, 8, suffix),
        wide(model_width // 128, 128),
        vmem(head_cols, width),
        vmem(3, model_width // relay_steps(suffix, chips, donors, piece), 2, ff_local),
        vmem(ff_local, model_width),
        vmem(tokens, head_cols),
        wide(tokens, width),
        vmem(count, piece, width),
        vmem(count, piece, width),
        vmem(count, piece, width),
        vmem(count, piece, width),
        vmem(blocks, tokens, width),
        vmem(model_width, 2 * ff_local),
        vmem(2 * suffix, width),
        wide(tokens, 2 * ff_local),
        wide(tokens, 128),
        vmem(tokens, ff_local),
        wide(2 * suffix, 1),
        vmem(chips * donors, 2 * suffix, columns),
        held(chips * donors),
        held((chips - 1) * donors),
        held((chips - 1) * donors),
        held(donors),
        held(donors),
        held(donors),
        held(donors),
    ]


def mix_blocks(
    heads, gain, probs, ids, hidden, out_weight, w_gate_up, w_down, chips, donors, piece, scratch
):
    suffix = heads.shape[0]
    columns = w_gate_up.shape[1] // donors
    count = 2 * chips * suffix // piece
    dma = pltpu.SemaphoreType.DMA
    pair = lambda number: [dma((number,)), dma((number,))]
    inside = pl.BlockSpec(memory_space=pltpu.VMEM)
    outside = pl.BlockSpec(memory_space=pl.ANY)
    return pl.pallas_call(
        functools.partial(mix_kernel, chips, donors, piece),
        out_shape=jax.ShapeDtypeStruct((suffix, columns), heads.dtype),
        in_specs=[inside] * 4 + [outside] * 4,
        out_specs=inside,
        scratch_shapes=scratch
        + [dma((3,)), dma((relay_steps(suffix, chips, donors, piece),))]
        + pair(2 * chips - 1)
        + pair(2 * chips // donors)
        + pair(chips - 1)
        + pair(chips)
        + pair(count)
        + pair(count)
        + pair((chips - 1) * count)
        + pair(chips * count)
        + pair(chips * donors)
        + pair((chips - 1) * donors)
        + pair(donors)
        + pair(donors),
        compiler_params=pltpu.CompilerParams(
            collective_id=3, has_side_effects=True, vmem_limit_bytes=VMEM_BYTES
        ),
        name="mix_blocks",
    )(heads, gain, probs, ids, hidden, out_weight, w_gate_up, w_down)


def shards(
    hidden_in,
    queries,
    suffix_kv,
    kv_pool,
    page_table,
    prefix_len,
    out_weight,
    norm_gain,
    expert_ids,
    route_probs,
    w_gate_up,
    w_down,
):
    n_expert = lax.axis_size("expert")
    n_donor = lax.axis_size("donor")
    expert_index = lax.axis_index("expert")
    donor_index = lax.axis_index("donor")
    share_count = n_donor // 2
    seq_count, page_count = page_table.shape
    suffix_len = queries.shape[0]
    kv_heads = suffix_kv.shape[1]
    head_dim = suffix_kv.shape[2] // 2
    page_len = kv_pool.shape[2]
    model_width = hidden_in.shape[1]
    columns = model_width // n_donor
    experts_all = 2 * n_expert
    ff_local = w_gate_up.shape[3]
    my_group = donor_index * kv_heads // n_donor
    owner_index = expert_index * n_donor + donor_index
    owner_of = page_table // seq_count
    held_slot = jnp.sum(jnp.where(owner_of == owner_index, page_table % seq_count, 0), axis=1)
    chips = n_expert // 2
    my_pair = lax.dynamic_index_in_dim(suffix_kv, my_group, 1, keepdims=False)
    scratch = mix_scratch(queries, out_weight, w_gate_up, chips, n_donor, PIECE)
    held_bytes = sum(math.prod(item.shape) * item.dtype.itemsize for item in scratch)
    if held_bytes <= VMEM_BYTES - 4 * 1024 * 1024:
        head_out = page_heads(
            kv_pool, page_table, prefix_len, queries, my_pair, n_expert, n_donor
        )
        layer_out = mix_blocks(
            head_out,
            norm_gain.reshape(-1, 128),
            route_probs.T,
            expert_ids.T,
            hidden_in,
            out_weight,
            w_gate_up,
            w_down,
            chips,
            n_donor,
            PIECE,
            scratch,
        )
        return (layer_out, head_out)

    dest_group = jnp.arange(n_donor, dtype=jnp.int32) * kv_heads // n_donor
    wanted = (held_slot[:, None] * kv_heads + dest_group[None, :]).reshape(-1)
    outgoing = jnp.take(
        kv_pool.reshape(seq_count * kv_heads, page_len, 2 * head_dim), wanted, axis=0
    )
    arrived = lax.all_to_all(outgoing, ("expert", "donor"), split_axis=0, concat_axis=0, tiled=True)
    my_owners = lax.dynamic_index_in_dim(owner_of, expert_index, 0, keepdims=False)
    ordered = jnp.take(arrived, my_owners, axis=0).reshape(page_count * page_len, 2 * head_dim)
    prefix_keys = ordered[:, :head_dim]
    prefix_vals = ordered[:, head_dim:]
    score_scale = head_dim ** (-0.5)
    query_heads = queries.reshape(suffix_len, -1, head_dim)
    fresh_pair = lax.dynamic_index_in_dim(suffix_kv, my_group, 1, keepdims=False)
    causal = jnp.arange(suffix_len)[:, None] >= jnp.arange(suffix_len)[None, :]
    fresh_scores = (
        jnp.einsum(
            "thc,uc->thu", query_heads, fresh_pair[:, :head_dim], preferred_element_type=jnp.float32
        )
        * score_scale
    )
    fresh_scores = jnp.where(causal[:, None, :], fresh_scores, -jnp.inf)
    prefix_tokens = lax.dynamic_index_in_dim(prefix_len, expert_index, 0, keepdims=False)
    block_keys = min(1024, page_count * page_len)
    live_blocks = (prefix_tokens + block_keys - 1) // block_keys

    def block_scores(block_index):
        keys_block = lax.dynamic_slice_in_dim(prefix_keys, block_index * block_keys, block_keys, 0)
        raw_scores = (
            jnp.einsum("thc,kc->thk", query_heads, keys_block, preferred_element_type=jnp.float32)
            * score_scale
        )
        visible = block_index * block_keys + jnp.arange(block_keys) < prefix_tokens
        return jnp.where(visible[None, None, :], raw_scores, -jnp.inf)

    def raise_max(block_index, running):
        return jnp.maximum(running, jnp.max(block_scores(block_index), axis=2))

    row_max = lax.fori_loop(0, live_blocks, raise_max, jnp.max(fresh_scores, axis=2))

    def add_block(block_index, loop_state):
        row_total, weighted = loop_state
        exp_scores = jnp.exp(block_scores(block_index) - row_max[:, :, None])
        vals_block = lax.dynamic_slice_in_dim(prefix_vals, block_index * block_keys, block_keys, 0)
        weighted = weighted + jnp.einsum(
            "thk,kc->thc",
            exp_scores.astype(jnp.bfloat16),
            vals_block,
            preferred_element_type=jnp.float32,
        )
        return (row_total + jnp.sum(exp_scores, axis=2), weighted)

    fresh_exp = jnp.exp(fresh_scores - row_max[:, :, None])
    start_state = (
        jnp.sum(fresh_exp, axis=2),
        jnp.einsum(
            "thu,uc->thc",
            fresh_exp.astype(jnp.bfloat16),
            fresh_pair[:, head_dim:],
            preferred_element_type=jnp.float32,
        ),
    )
    row_total, weighted = lax.fori_loop(0, live_blocks, add_block, start_state)
    head_out = (weighted / row_total[:, :, None]).astype(jnp.bfloat16).reshape(suffix_len, -1)
    gate_weights = route_probs / jnp.sum(route_probs, axis=1, keepdims=True)
    chosen = expert_ids[:, :, None] == jnp.arange(experts_all, dtype=jnp.int32)
    gate_table = jnp.sum(jnp.where(chosen, gate_weights[:, :, None], 0.0), axis=1)
    gate_tables = [gate_table]
    for step in range(1, n_expert):
        pairs = [(source, (source + step) % n_expert) for source in range(n_expert)]
        gate_tables.append(lax.ppermute(gate_table, "expert", pairs))
    from_order = lax.rem(expert_index - jnp.arange(n_expert) + n_expert, n_expert)
    gate_all = jnp.stack(gate_tables)[from_order].reshape(n_expert * suffix_len, experts_all)
    my_expert = owner_index // share_count
    my_gates = lax.dynamic_slice_in_dim(gate_all, my_expert, 1, 1)

    seqs_each = n_expert // n_donor
    width = model_width // n_expert
    hidden_parts = []
    for shift in range(seqs_each):
        pairs = []
        for source in range(n_expert * n_donor):
            seq, part = source // n_donor, source % n_donor
            target = part * seqs_each + (seq + shift) % seqs_each
            pairs.append((source, target * n_donor + seq // seqs_each))
        target = donor_index * seqs_each + lax.rem(expert_index + shift, seqs_each)
        sent = lax.dynamic_slice_in_dim(hidden_in, target * width, width, 1)
        hidden_parts.append(lax.ppermute(sent, ("expert", "donor"), pairs))
    turned = lax.rem(expert_index - jnp.arange(seqs_each) + seqs_each * n_expert, seqs_each)
    hidden_block = jnp.stack(hidden_parts)[turned].reshape(seqs_each * suffix_len, width)

    heads_all = lax.all_gather(head_out, "expert", axis=0, tiled=True)
    w_in, heads_all = lax.optimization_barrier(
        (w_gate_up[0].reshape(model_width, 2 * ff_local), heads_all)
    )
    resid = gather_blocks(heads_all, out_weight, hidden_block, n_expert // 2, n_donor)
    resid_f = resid.astype(jnp.float32)
    inverse = lax.rsqrt(jnp.mean(resid_f * resid_f, axis=1, keepdims=True) + 1e-06)
    normed = (resid_f * inverse * norm_gain.astype(jnp.float32)).astype(jnp.bfloat16)
    gate_up = jnp.dot(
        normed,
        w_in,
        preferred_element_type=jnp.float32,
    )
    activated = (
        jax.nn.silu(gate_up[:, :ff_local]) * gate_up[:, ff_local:] * my_gates
    ).astype(jnp.bfloat16)
    expert_mix = reduce_blocks(activated, w_down[0], n_expert // 2, n_donor)
    resid_mine = lax.dynamic_slice(
        resid,
        (expert_index * suffix_len, donor_index * columns),
        (suffix_len, columns),
    )
    layer_out = (resid_mine.astype(jnp.float32) + expert_mix).astype(
        jnp.bfloat16
    )
    return (layer_out, head_out)


def solution(mesh):
    in_specs = (
        P(("groups", "expert"), None),
        P(("groups", "expert"), "donor"),
        P(("groups", "expert"), None, None),
        P(("groups", "expert", "donor"), None, None, None),
        P("groups", None),
        P("groups"),
        P("donor", "expert"),
        P(),
        P(("groups", "expert"), None),
        P(("groups", "expert"), None),
        P(("expert", "donor"), None, None, None),
        P(("expert", "donor"), None, None),
    )
    out_specs = (P(("groups", "expert"), "donor"), P(("groups", "expert"), "donor"))
    return jax.shard_map(shards, mesh=mesh, in_specs=in_specs, out_specs=out_specs, check_vma=False)
```

```python
import functools
import math

import jax
import jax.numpy as jnp
from jax import lax
from jax.experimental import pallas as pl
from jax.experimental.pallas import tpu as pltpu
from jax.sharding import PartitionSpec as P

MESH = pl.DeviceIdType.MESH
VMEM_BYTES = 60 * 1024 * 1024
PIECE = 32
HOP = 3
LAG = 3


def place():
    expert = lax.axis_index("expert")
    return expert // 2, lax.rem(expert, 2), lax.axis_index("donor")


def send(src, dst, sends, recvs, slot, **where):
    return pltpu.make_async_remote_copy(
        src_ref=src,
        dst_ref=dst,
        send_sem=sends.at[slot],
        recv_sem=recvs.at[slot],
        device_id=where,
        device_id_type=MESH,
    )


def greet(chips, donors):
    row, core, donor = place()
    barrier = pltpu.get_barrier_semaphore()
    pl.semaphore_signal(
        barrier, inc=1, device_id={"expert": row * 2 + 1 - core}, device_id_type=MESH
    )
    for step in range(1, chips):
        other = lax.rem(row + step, chips) * 2 + core
        pl.semaphore_signal(barrier, inc=1, device_id={"expert": other}, device_id_type=MESH)
    for step in range(1, donors):
        other = lax.rem(donor + step, donors)
        pl.semaphore_signal(barrier, inc=1, device_id={"donor": other}, device_id_type=MESH)
    pl.semaphore_wait(barrier, chips + donors - 1)


def far_first(donors):
    return sorted(range(1, donors), key=lambda k: (-min(k, donors - k), k))


def gather_kernel(
    chips,
    donors,
    heads_ref,
    out_ref,
    hidden_ref,
    full_ref,
    terms_ref,
    terms_in,
    block_ref,
    own_sem,
    t_send,
    t_recv,
    z_send,
    z_recv,
    y_send,
    y_recv,
    c_send,
    c_recv,
):
    row, core, donor = place()
    rows, cols = block_ref.shape
    greet(chips, donors)
    strip = 16

    def project(step_z, slot):
        top = pl.multiple_of(lax.rem(donor + step_z, donors) * rows, rows)
        terms_ref[slot] = jnp.dot(
            heads_ref[pl.ds(top, rows), :], out_ref[...], preferred_element_type=jnp.float32
        ).astype(terms_ref.dtype)

    term_copies = {}
    for step in far_first(donors):
        project(step, step)
        copy = send(
            terms_ref.at[step],
            terms_in.at[step - 1],
            t_send,
            t_recv,
            step - 1,
            donor=lax.rem(donor + step, donors),
        )
        copy.start()
        term_copies[step] = copy
    project(0, 0)
    for step in far_first(donors):
        term_copies[step].wait_recv()

    def add(index, carry):
        at = pl.ds(pl.multiple_of(index * strip, strip), strip)
        value = terms_ref[0, at, :].astype(jnp.float32)
        for step in range(1, donors):
            value = value + terms_in[step - 1, at, :].astype(jnp.float32)
        value = value + hidden_ref[at, :].astype(jnp.float32)
        block_ref[at, :] = value.astype(block_ref.dtype)
        return carry

    lax.fori_loop(0, rows // strip, add, 0)

    def slot_of(donor_from, row_from, core_from):
        top = pl.multiple_of(donor_from * rows, rows)
        left = pl.multiple_of((row_from * 2 + core_from) * cols, cols)
        return full_ref.at[pl.ds(top, rows), pl.ds(left, cols)]

    own = pltpu.make_async_copy(block_ref, slot_of(donor, row, core), own_sem)
    own.start()
    started = []

    def along_y(src, step_z, donor_from):
        for step in range(1, chips):
            copy = send(
                src,
                slot_of(donor_from, row, core),
                y_send,
                y_recv,
                step_z * (chips - 1) + step - 1,
                expert=lax.rem(row + step, chips) * 2 + core,
            )
            copy.start()
            started.append(copy)

    def beside(src, step_z, step_y, donor_from, row_from):
        copy = send(
            src,
            slot_of(donor_from, row_from, core),
            c_send,
            c_recv,
            step_z * chips + step_y,
            expert=row * 2 + 1 - core,
        )
        copy.start()
        started.append(copy)

    along_y(block_ref, 0, donor)
    z_copies = {}
    near_first = far_first(donors)[::-1]
    for step in near_first:
        copy = send(
            block_ref,
            slot_of(donor, row, core),
            z_send,
            z_recv,
            step - 1,
            donor=lax.rem(donor + step, donors),
        )
        copy.start()
        z_copies[step] = copy
    beside(block_ref, 0, 0, donor, row)

    def take_y(step_z, donor_from):
        for step in range(1, chips):
            row_from = lax.rem(row + chips - step, chips)
            there = slot_of(donor_from, row_from, core)
            send(
                there,
                there,
                y_send,
                y_recv,
                step_z * (chips - 1) + step - 1,
                expert=row_from * 2 + core,
            ).wait_recv()
            beside(there, step_z, step, donor_from, row_from)

    for step in near_first:
        donor_from = lax.rem(donor + donors - step, donors)
        there = slot_of(donor_from, row, core)
        send(there, there, z_send, z_recv, step - 1, donor=donor_from).wait_recv()
        along_y(there, step, donor_from)
        beside(there, step, 0, donor_from, row)
    for step in [0] + near_first:
        take_y(step, lax.rem(donor + donors - step, donors))
    for step_z in range(donors):
        donor_from = lax.rem(donor + donors - step_z, donors)
        for step_y in range(chips):
            row_from = lax.rem(row + chips - step_y, chips)
            there = slot_of(donor_from, row_from, 1 - core)
            send(
                there, there, c_send, c_recv, step_z * chips + step_y, expert=row * 2 + 1 - core
            ).wait_recv()
    own.wait()
    for copy in list(term_copies.values()) + list(z_copies.values()) + started:
        copy.wait_send()


def gather_blocks(heads, out_weight, block, chips, donors):
    rows, cols = block.shape
    dma = pltpu.SemaphoreType.DMA
    return pl.pallas_call(
        functools.partial(gather_kernel, chips, donors),
        out_shape=jax.ShapeDtypeStruct((rows * donors, cols * chips * 2), block.dtype),
        in_specs=[pl.BlockSpec(memory_space=pltpu.VMEM)] * 3,
        out_specs=pl.BlockSpec(memory_space=pltpu.VMEM),
        scratch_shapes=[
            pltpu.VMEM((donors, rows, cols), block.dtype),
            pltpu.VMEM((donors - 1, rows, cols), block.dtype),
            pltpu.VMEM((rows, cols), block.dtype),
            dma,
            dma((donors - 1,)),
            dma((donors - 1,)),
            dma((donors - 1,)),
            dma((donors - 1,)),
            dma((donors * (chips - 1),)),
            dma((donors * (chips - 1),)),
            dma((donors * chips,)),
            dma((donors * chips,)),
        ],
        compiler_params=pltpu.CompilerParams(collective_id=1, has_side_effects=True),
        name="gather_blocks",
    )(heads, out_weight, block)


def reduce_kernel(
    chips,
    donors,
    act_ref,
    down_ref,
    total_ref,
    part_ref,
    c_in,
    y_out,
    y_in,
    z_out,
    z_in,
    c_send,
    c_recv,
    y_send,
    y_recv,
    z_send,
    z_recv,
):
    row, core, donor = place()
    rows, cols = total_ref.shape
    greet(chips, donors)
    order = far_first(donors) + [0]
    strip = 16

    def tile(row_to, core_to, step_z):
        top = pl.multiple_of((row_to * 2 + core_to) * rows, rows)
        left = pl.multiple_of(lax.rem(donor + step_z, donors) * cols, cols)
        return part_ref.at[pl.ds(top, rows), pl.ds(left, cols)]

    def add(out, *terms):
        def body(index, carry):
            at = pl.ds(pl.multiple_of(index * strip, strip), strip)
            value = terms[0][at, :].astype(jnp.float32)
            for term in terms[1:]:
                value = value + term[at, :].astype(jnp.float32)
            out[at, :] = value.astype(out.dtype)
            return carry

        lax.fori_loop(0, rows // strip, body, 0)

    started = []
    arrivals = {}

    def multiply(step_z):
        left = pl.multiple_of(lax.rem(donor + step_z, donors) * cols, cols)

        def body(index, carry):
            at = pl.ds(pl.multiple_of(index * rows, rows), rows)
            part_ref[at, pl.ds(left, cols)] = jnp.dot(
                act_ref[at, :],
                down_ref[:, pl.ds(left, cols)],
                preferred_element_type=jnp.float32,
            ).astype(part_ref.dtype)
            return carry

        lax.fori_loop(0, chips * 2, body, 0)

    def beside(step_z):
        for step_y in range(chips - 1, -1, -1):
            slot = step_z * chips + step_y
            copy = send(
                tile(lax.rem(row + step_y, chips), 1 - core, step_z),
                c_in.at[slot],
                c_send,
                c_recv,
                slot,
                expert=row * 2 + 1 - core,
            )
            copy.start()
            started.append(copy)

    def along_y(step_z):
        for step_y in range(chips - 1, 0, -1):
            row_to = lax.rem(row + step_y, chips)
            slot = step_z * chips + step_y
            send(
                c_in.at[slot], c_in.at[slot], c_send, c_recv, slot, expert=row * 2 + 1 - core
            ).wait_recv()
            hop = step_z * (chips - 1) + step_y - 1
            add(y_out.at[hop], tile(row_to, core, step_z), c_in.at[slot])
            copy = send(
                y_out.at[hop], y_in.at[hop], y_send, y_recv, hop, expert=row_to * 2 + core
            )
            copy.start()
            arrivals[hop] = copy
            started.append(copy)

    for index, step_z in enumerate(order):
        multiply(step_z)
        beside(step_z)
        if index:
            along_y(order[index - 1])
    along_y(order[-1])
    for step_z in order:
        slot = step_z * chips
        send(
            c_in.at[slot], c_in.at[slot], c_send, c_recv, slot, expert=row * 2 + 1 - core
        ).wait_recv()
        terms = [tile(row, core, step_z), c_in.at[slot]]
        for step_y in range(1, chips):
            hop = step_z * (chips - 1) + step_y - 1
            arrivals[hop].wait_recv()
            terms.append(y_in.at[hop])
        if step_z:
            add(z_out.at[step_z - 1], *terms)
            copy = send(
                z_out.at[step_z - 1],
                z_in.at[step_z - 1],
                z_send,
                z_recv,
                step_z - 1,
                donor=lax.rem(donor + step_z, donors),
            )
            copy.start()
            arrivals["z", step_z] = copy
            started.append(copy)
        else:
            for step in order[:-1]:
                arrivals["z", step].wait_recv()
                terms.append(z_in.at[step - 1])
            add(total_ref, *terms)
    for copy in started:
        copy.wait_send()


def reduce_blocks(activated, down, chips, donors):
    rows, cols = activated.shape[0] // (chips * 2), down.shape[1] // donors
    dma = pltpu.SemaphoreType.DMA
    held = lambda count: pltpu.VMEM((count, rows, cols), activated.dtype)
    return pl.pallas_call(
        functools.partial(reduce_kernel, chips, donors),
        out_shape=jax.ShapeDtypeStruct((rows, cols), jnp.float32),
        in_specs=[pl.BlockSpec(memory_space=pltpu.VMEM)] * 2,
        out_specs=pl.BlockSpec(memory_space=pltpu.VMEM),
        scratch_shapes=[
            pltpu.VMEM((activated.shape[0], down.shape[1]), activated.dtype),
            held(donors * chips),
            held(donors * (chips - 1)),
            held(donors * (chips - 1)),
            held(donors - 1),
            held(donors - 1),
            dma((donors * chips,)),
            dma((donors * chips,)),
            dma((donors * (chips - 1),)),
            dma((donors * (chips - 1),)),
            dma((donors - 1,)),
            dma((donors - 1,)),
        ],
        compiler_params=pltpu.CompilerParams(collective_id=2, has_side_effects=True),
        name="reduce_blocks",
    )(activated, down)


def mix_kernel(
    chips,
    donors,
    piece,
    heads_in,
    gain_ref,
    probs_ref,
    ids_ref,
    hidden_hbm,
    outw_hbm,
    raw_hbm,
    down_hbm,
    out_ref,
    hidden_ref,
    gates_out,
    gates_in,
    gain_wide,
    outw_ref,
    raw_ref,
    down_ref,
    heads_ref,
    p_ref,
    r_out,
    r_in,
    l_out,
    l_in,
    full_ref,
    w_ref,
    x_ref,
    acc_ref,
    ssq_ref,
    act_ref,
    gates_ref,
    part_ref,
    c_in,
    y_out,
    y_in,
    zr_out,
    zr_in,
    zl_out,
    zl_in,
    local_sem,
    raw_sem,
    g_send,
    g_recv,
    h_send,
    h_recv,
    hy_send,
    hy_recv,
    hc_send,
    hc_recv,
    r_send,
    r_recv,
    l_send,
    l_recv,
    y_send,
    y_recv,
    c_send,
    c_recv,
    cc_send,
    cc_recv,
    yy_send,
    yy_recv,
    zr_send,
    zr_recv,
    zl_send,
    zl_recv,
):
    row, core, donor = place()
    mine = row * 2 + core
    beside = row * 2 + 1 - core
    suffix, head_cols = heads_in.shape
    blocks, tokens, width = full_ref.shape
    model_width, ff_both = w_ref.shape
    ff_local = ff_both // 2
    seqs_each = hidden_ref.shape[0]
    per_seq = suffix // piece
    count = blocks * per_seq
    per_group = count // chips
    group_rows = 2 * suffix
    columns = out_ref.shape[1]
    last = donors - 1
    lag = LAG
    first_mix = per_group + lag
    raw_steps, raw_slots, raw_rows = raw_sem.shape[0], raw_ref.shape[0], raw_ref.shape[1]
    relay = min(128, raw_rows)
    strip = 16

    own_copies = [
        pltpu.make_async_copy(outw_hbm, outw_ref, local_sem.at[0]),
        pltpu.make_async_copy(heads_in, heads_ref.at[pl.ds(mine * suffix, suffix)], local_sem.at[1]),
        pltpu.make_async_copy(down_hbm.at[0], down_ref, local_sem.at[2]),
    ]
    own_copies[0].start()
    own_copies[1].start()

    def raw_copy(index):
        at = pl.ds(pl.multiple_of(index * raw_rows, raw_rows), raw_rows)
        return pltpu.make_async_copy(
            raw_hbm.at[0, at], raw_ref.at[lax.rem(index, raw_slots)], raw_sem.at[index]
        )

    for index in range(raw_slots):
        raw_copy(index).start()
    own_copies[2].start()

    barrier = pltpu.get_barrier_semaphore()
    for step in range(1, blocks):
        other = lax.rem(mine + step, blocks)
        pl.semaphore_signal(barrier, inc=1, device_id={"expert": other}, device_id_type=MESH)

    @pl.when(donor > 0)
    def _():
        pl.semaphore_signal(barrier, inc=1, device_id={"donor": donor - 1}, device_id_type=MESH)

    @pl.when(donor < last)
    def _():
        pl.semaphore_signal(barrier, inc=1, device_id={"donor": donor + 1}, device_id_type=MESH)

    gain_wide[...] = gain_ref[...].astype(jnp.float32)
    acc_ref[...] = jnp.zeros_like(acc_ref)
    ssq_ref[...] = jnp.zeros_like(ssq_ref)
    pl.semaphore_wait(barrier, blocks - 1 + jnp.minimum(donor, 1) + jnp.minimum(last - donor, 1))

    def heads_of(seq):
        return heads_ref.at[pl.ds(pl.multiple_of(seq * suffix, suffix), suffix)]

    def heads_y(step, seq, to):
        return send(heads_of(seq), heads_of(seq), hy_send, hy_recv, step - 1, expert=to)

    def heads_c(slot, seq):
        return send(heads_of(seq), heads_of(seq), hc_send, hc_recv, slot, expert=beside)

    def gates_to(step):
        return send(
            gates_out.at[step],
            gates_in.at[mine],
            g_send,
            g_recv,
            step - 1,
            expert=lax.rem(mine + step, blocks),
        )

    def partner(index):
        return lax.rem(donor - lax.rem(mine, donors) + donors, donors) + donors * index

    def hidden_to(index):
        at = pl.ds(pl.multiple_of(partner(index) * width, width), width)
        slot = mine // donors
        return pltpu.make_async_remote_copy(
            src_ref=hidden_hbm.at[:, at],
            dst_ref=hidden_ref.at[slot],
            send_sem=h_send.at[index],
            recv_sem=h_recv.at[slot],
            device_id={"expert": partner(index)},
            device_id_type=MESH,
        )

    def hidden_own(index):
        at = pl.ds(pl.multiple_of(mine * width, width), width)
        return pltpu.make_async_copy(hidden_hbm.at[:, at], hidden_ref.at[index], h_recv.at[index])

    own_copies[1].wait()
    heads_c(0, mine).start()
    for step in range(1, chips):
        heads_y(step, mine, lax.rem(row + step, chips) * 2 + core).start()
    for index in range(seqs_each):

        @pl.when(partner(index) != mine)
        def _():
            hidden_to(index).start()

        @pl.when(partner(index) == mine)
        def _():
            hidden_own(index).start()

    square = (suffix, suffix)
    eye = lax.broadcasted_iota(jnp.int32, square, 0) == lax.broadcasted_iota(jnp.int32, square, 1)
    parts_of = donors // 2
    share = probs_ref[...] / jnp.sum(probs_ref[...], axis=0, keepdims=True)
    for step in range(blocks):
        named = (lax.rem(mine + step, blocks) * donors + donor) // parts_of
        line = jnp.sum(jnp.where(ids_ref[...] == named, share, 0.0), axis=0, keepdims=True)
        if step:
            gates_out[step] = jnp.broadcast_to(line, gates_out.shape[1:])
            gates_to(step).start()
        else:
            gates_in[mine] = jnp.broadcast_to(line, gates_out.shape[1:])
    own_copies[0].wait()

    def seq_at(from_row, from_core, index):
        return lax.rem(from_row + index // 2, chips) * 2 + lax.rem(from_core + lax.rem(index, 2), 2)

    def tile(from_row, from_core, chunk):
        seq = seq_at(from_row, from_core, chunk // per_seq)
        top = pl.multiple_of(seq * suffix + lax.rem(chunk, per_seq) * piece, piece)
        return full_ref.at[from_row * 2 + from_core, pl.ds(top, piece)]

    def right(chunk):
        return send(r_out.at[chunk], r_in.at[chunk], r_send, r_recv, chunk, donor=donor + 1)

    def left(chunk):
        return send(l_out.at[chunk], l_in.at[chunk], l_send, l_recv, chunk, donor=donor - 1)

    def across(step, chunk, from_row, to):
        there = tile(from_row, core, chunk)
        return send(there, there, y_send, y_recv, (step - 1) * count + chunk, expert=to)

    def over(step, chunk, from_row, from_core):
        there = tile(from_row, from_core, chunk)
        return send(there, there, c_send, c_recv, step * count + chunk, expert=beside)

    reach = jnp.maximum(donor, last - donor) * HOP

    def partial(index):
        seq = seq_at(row, core, index)
        step = index // 2

        @pl.when((index > 0) & (lax.rem(index, 2) == 0))
        def _():
            back = lax.rem(chips - step, chips)
            copy = send(
                heads_of(seq), heads_of(seq), hy_send, hy_recv, back - 1, expert=beside
            )
            copy.wait_recv()
            heads_c(back, seq).start()

        @pl.when(lax.rem(index, 2) == 1)
        def _():
            heads_c(lax.rem(chips - step, chips), seq).wait_recv()

        at = pl.ds(pl.multiple_of(index * suffix, suffix), suffix)
        p_ref[at, :] = jnp.dot(
            heads_ref[pl.ds(pl.multiple_of(seq * suffix, suffix), suffix), :],
            outw_ref[...],
            preferred_element_type=jnp.float32,
        )

        for index in range(seqs_each):

            @pl.when(partner(index) == seq)
            def _():
                hidden_own(index).wait()
                p_ref[at, :] = p_ref[at, :] + hidden_ref[index].astype(jnp.float32)

    def p_rows(chunk):
        return p_ref[pl.ds(pl.multiple_of(chunk * piece, piece), piece), :]

    def relay_weights(index):
        raw_copy(index).wait()
        half = lax.broadcasted_iota(jnp.int32, (relay, 2 * relay), 0)
        whole = lax.broadcasted_iota(jnp.int32, (relay, 2 * relay), 1)

        def body(part, carry):
            at = pl.ds(pl.multiple_of(index * raw_rows + part * relay, relay), relay)
            from_at = pl.ds(pl.multiple_of(part * relay, relay), relay)
            both = raw_ref[lax.rem(index, raw_slots), from_at].reshape(2 * relay, ff_local)
            for side in range(2):
                pick = (whole == 2 * half + side).astype(raw_ref.dtype)
                w_ref[at, side * ff_local : (side + 1) * ff_local] = jnp.dot(
                    pick, both, preferred_element_type=jnp.float32
                ).astype(w_ref.dtype)
            return carry

        lax.fori_loop(0, raw_rows // relay, body, 0)

        @pl.when(index + raw_slots < raw_steps)
        def _():
            raw_copy(index + raw_slots).start()

    cut = ff_both // 3

    def mix(turn, index):
        from_row = lax.rem(row + index // 2, chips)
        from_core = lax.rem(core + lax.rem(index, 2), 2)
        back = lax.rem(chips - index // 2, chips)

        @pl.when(lax.rem(index, 2) == 1)
        def _():
            def body(chunk, carry):
                over(back, turn * per_group + chunk, from_row, from_core).wait_recv()
                return carry

            lax.fori_loop(0, per_group, body, 0)

        block = from_row * 2 + from_core
        group = lax.rem(from_row + turn, chips)
        top = pl.multiple_of(group * group_rows, group_rows)
        left_at = pl.multiple_of(block * width, width)
        lanes = gain_wide.shape[1]
        tiles = width // lanes
        gain = gain_wide[pl.ds(pl.multiple_of(block * tiles, tiles), tiles), :]

        def scale(part, carry):
            here = pl.ds(pl.multiple_of(part * strip, strip), strip)
            at = pl.ds(pl.multiple_of(top + part * strip, strip), strip)
            total = ssq_ref[at, :]
            for part_at in range(tiles):
                wide = slice(part_at * lanes, (part_at + 1) * lanes)
                value = full_ref[block, at, wide].astype(jnp.float32)
                x_ref[here, wide] = (value * gain[part_at : part_at + 1, :]).astype(x_ref.dtype)
                total = total + value * value
            ssq_ref[at, :] = total
            return carry

        lax.fori_loop(0, group_rows // strip, scale, 0)
        at = pl.ds(top, group_rows)

        def multiply(part, carry):
            wide = pl.ds(pl.multiple_of(part * cut, cut), cut)
            acc_ref[at, wide] = acc_ref[at, wide] + jnp.dot(
                x_ref[...], w_ref[pl.ds(left_at, width), wide], preferred_element_type=jnp.float32
            )
            return carry

        lax.fori_loop(0, ff_both // cut, multiply, 0)

    early = blocks * (chips - 1)

    def march(t, carry):
        @pl.when((t < count) & (lax.rem(t, per_seq) == 0))
        def _():
            partial(t // per_seq)

        here = t - donor * HOP

        @pl.when((here >= 0) & (here < count))
        def _():
            @pl.when(donor == 0)
            def _():
                r_out[here] = p_rows(here).astype(r_out.dtype)

            @pl.when(donor > 0)
            def _():
                right(here).wait_recv()

            @pl.when((donor > 0) & (donor < last))
            def _():
                r_out[here] = (p_rows(here) + r_in[here].astype(jnp.float32)).astype(r_out.dtype)

            @pl.when(donor < last)
            def _():
                right(here).start()

        there = t - (last - donor) * HOP

        @pl.when((there >= 0) & (there < count))
        def _():
            @pl.when(donor == last)
            def _():
                l_out[there] = p_rows(there).astype(l_out.dtype)

            @pl.when(donor < last)
            def _():
                left(there).wait_recv()

            @pl.when((donor > 0) & (donor < last))
            def _():
                l_out[there] = (p_rows(there) + l_in[there].astype(jnp.float32)).astype(l_out.dtype)

            @pl.when(donor > 0)
            def _():
                left(there).start()

        done = t - reach

        @pl.when((done >= 0) & (done < count))
        def _():
            goal = tile(row, core, done)

            @pl.when(donor == 0)
            def _():
                goal[...] = (p_rows(done) + l_in[done].astype(jnp.float32)).astype(goal.dtype)

            @pl.when(donor == last)
            def _():
                goal[...] = (p_rows(done) + r_in[done].astype(jnp.float32)).astype(goal.dtype)

            @pl.when((donor > 0) & (donor < last))
            def _():
                goal[...] = (
                    p_rows(done) + r_in[done].astype(jnp.float32) + l_in[done].astype(jnp.float32)
                ).astype(goal.dtype)

            for step in range(1, chips):
                across(step, done, row, lax.rem(row + step, chips) * 2 + core).start()
            over(0, done, row, core).start()

        came = t - reach - lag

        @pl.when((came >= 0) & (came < count))
        def _():
            for step in range(1, chips):
                from_row = lax.rem(row + chips - step, chips)
                across(step, came, from_row, from_row * 2 + core).wait_recv()
                over(step, came, from_row, core).start()

        @pl.when(t < raw_steps)
        def _():
            relay_weights(t)

        ready = t - reach - first_mix

        @pl.when((ready >= 0) & (ready < early))
        def _():
            mix(ready // blocks, lax.rem(ready, blocks))

        return carry

    steps = count + last * HOP + lag
    lax.fori_loop(0, steps, march, 0)

    def rest(index, carry):
        mix(index // blocks, lax.rem(index, blocks))
        return carry

    lax.fori_loop(jnp.minimum(steps - reach - first_mix, early), early, rest, 0)
    own_copies[2].wait()

    for step in range(1, blocks):
        back = lax.rem(mine + blocks - step, blocks)
        send(
            gates_out.at[step], gates_in.at[back], g_send, g_recv, step - 1, expert=back
        ).wait_recv()

    def activate(group):
        for side in range(2):
            seq = group * 2 + side
            gates_ref[side * suffix : (side + 1) * suffix, :] = jnp.sum(
                jnp.where(eye, gates_in[seq][:1, :], 0.0), axis=1, keepdims=True
            )

        def body(part, carry):
            at = pl.ds(pl.multiple_of(group * group_rows + part * strip, strip), strip)
            here = pl.ds(pl.multiple_of(part * strip, strip), strip)
            mean = jnp.sum(ssq_ref[at, :], axis=1, keepdims=True) * (1.0 / model_width)
            inverse = lax.rsqrt(mean + 1e-06)
            gate = acc_ref[at, :ff_local] * inverse
            up = acc_ref[at, ff_local:] * inverse
            value = gate / (1.0 + jnp.exp(-gate)) * up * gates_ref[here, :]
            act_ref[at, :] = value.astype(act_ref.dtype)
            return carry

        lax.fori_loop(0, group_rows // strip, body, 0)

    def target(rank):
        low = jnp.minimum(donor, last - donor)
        single = jnp.maximum(donor, last - donor) - low
        rest_rank = rank - single
        gap = low - rest_rank // 2
        side = 1 - 2 * lax.rem(jnp.maximum(rest_rank, 0), 2)
        paired = donor + side * gap
        lone = jnp.where(donor < last - donor, last - rank, rank)
        return jnp.where(rank == last, donor, jnp.where(rank < single, lone, paired))

    def add(out, *terms):
        def body(part, carry):
            at = pl.ds(pl.multiple_of(part * strip, strip), strip)
            value = terms[0][at, :].astype(jnp.float32)
            for term in terms[1:]:
                value = value + term[at, :].astype(jnp.float32)
            out[at, :] = value.astype(out.dtype)
            return carry

        lax.fori_loop(0, suffix // strip, body, 0)

    order = list(range(1, chips)) + [0]

    def own_half(slot):
        return part_ref.at[slot, pl.ds(pl.multiple_of(core * suffix, suffix), suffix)]

    def swap(slot):
        away = part_ref.at[slot, pl.ds(pl.multiple_of((1 - core) * suffix, suffix), suffix)]
        return send(away, c_in.at[slot], cc_send, cc_recv, slot, expert=beside)

    def cross(hop, to):
        return send(y_out.at[hop], y_in.at[hop], yy_send, yy_recv, hop, expert=to)

    def produce(step, rank):
        slot = step * donors + rank
        top = pl.multiple_of(lax.rem(row + step, chips) * group_rows, group_rows)
        left_at = pl.multiple_of(target(rank) * columns, columns)
        part_ref[slot] = jnp.dot(
            act_ref[pl.ds(top, group_rows), :],
            down_ref[:, pl.ds(left_at, columns)],
            preferred_element_type=jnp.float32,
        ).astype(part_ref.dtype)
        swap(slot).start()

    def pass_on(step, rank):
        slot = step * donors + rank
        hop = (step - 1) * donors + rank
        swap(slot).wait_recv()
        add(y_out.at[hop], own_half(slot), c_in.at[slot])
        cross(hop, lax.rem(row + step, chips) * 2 + core).start()

    for step in order:
        for side in range(2):
            mix(chips - 1, 2 * ((step + 1) % chips) + side)
        activate(lax.rem(row + step, chips))
        if step:

            def body(rank, carry):
                produce(step, rank)

                @pl.when(rank > 0)
                def _():
                    pass_on(step, rank - 1)

                return carry

            lax.fori_loop(0, donors, body, 0)
            pass_on(step, donors - 1)
        else:

            def body(rank, carry):
                produce(0, rank)
                return carry

            lax.fori_loop(0, donors, body, 0)

    def shift_right(goal):
        return send(zr_out.at[goal], zr_in.at[goal], zr_send, zr_recv, goal, donor=donor + 1)

    def shift_left(goal):
        return send(zl_out.at[goal], zl_in.at[goal], zl_send, zl_recv, goal, donor=donor - 1)

    def finish(rank, carry):
        goal = target(rank)
        swap(rank).wait_recv()
        terms = [own_half(rank), c_in.at[rank]]
        for step in range(1, chips):
            hop = (step - 1) * donors + rank
            cross(hop, mine).wait_recv()
            terms.append(y_in.at[hop])

        @pl.when((goal >= donor) & (donor > 0))
        def _():
            shift_right(goal).wait_recv()

        @pl.when((goal <= donor) & (donor < last))
        def _():
            shift_left(goal).wait_recv()

        @pl.when(goal > donor)
        def _():
            @pl.when(donor == 0)
            def _():
                add(zr_out.at[goal], *terms)

            @pl.when(donor > 0)
            def _():
                add(zr_out.at[goal], zr_in.at[goal], *terms)

            shift_right(goal).start()

        @pl.when(goal < donor)
        def _():
            @pl.when(donor == last)
            def _():
                add(zl_out.at[goal], *terms)

            @pl.when(donor < last)
            def _():
                add(zl_out.at[goal], zl_in.at[goal], *terms)

            shift_left(goal).start()

        @pl.when(goal == donor)
        def _():
            def close(ends):
                for part in range(columns // width):
                    wide = slice(part * width, (part + 1) * width)

                    def body(index, carry):
                        at = pl.ds(pl.multiple_of(index * strip, strip), strip)
                        down = pl.ds(pl.multiple_of(mine * suffix + index * strip, strip), strip)
                        value = full_ref[donor * (columns // width) + part, down, :].astype(jnp.float32)
                        total = terms[0][at, wide].astype(jnp.float32)
                        for term in terms[1:] + ends:
                            total = total + term[at, wide].astype(jnp.float32)
                        out_ref[at, wide] = (value + total).astype(out_ref.dtype)
                        return carry

                    lax.fori_loop(0, suffix // strip, body, 0)

            @pl.when(donor == 0)
            def _():
                close([zl_in.at[donor]])

            @pl.when(donor == last)
            def _():
                close([zr_in.at[donor]])

            @pl.when((donor > 0) & (donor < last))
            def _():
                close([zl_in.at[donor], zr_in.at[donor]])

        return carry

    lax.fori_loop(0, donors, finish, 0)

    for step in range(1, blocks):
        gates_to(step).wait_send()
    for index in range(seqs_each):

        @pl.when(partner(index) != mine)
        def _():
            hidden_to(index).wait_send()

    for step in range(1, chips):
        heads_y(step, mine, mine).wait_send()
    for step in range(chips):
        heads_c(step, mine).wait_send()

    def drain(chunk, carry):
        @pl.when(donor < last)
        def _():
            right(chunk).wait_send()

        @pl.when(donor > 0)
        def _():
            left(chunk).wait_send()

        for step in range(1, chips):
            across(step, chunk, row, mine).wait_send()
        for step in range(chips):
            over(step, chunk, row, core).wait_send()
        return carry

    lax.fori_loop(0, count, drain, 0)

    def drain_blocks(goal, carry):
        for step in range(chips):
            swap(step * donors + goal).wait_send()
        for step in range(1, chips):
            cross((step - 1) * donors + goal, mine).wait_send()

        @pl.when(goal > donor)
        def _():
            shift_right(goal).wait_send()

        @pl.when(goal < donor)
        def _():
            shift_left(goal).wait_send()

        return carry

    lax.fori_loop(0, donors, drain_blocks, 0)


def page_kernel(
    experts,
    donors,
    pool_ref,
    table_ref,
    length_ref,
    query_ref,
    suffix_ref,
    head_ref,
    fresh_ref,
    out_buf,
    pages_in,
    sends,
    recvs,
):
    expert, donor = lax.axis_index("expert"), lax.axis_index("donor")
    seqs, kv_heads = out_buf.shape[0], out_buf.shape[1]
    suffix, columns = head_ref.shape
    head_dim = fresh_ref.shape[1] // 2
    order = [
        (step_e, step_z)
        for step_z in [*far_first(donors), 0]
        for step_e in range(experts)
        if step_e or step_z
    ]
    barrier = pltpu.get_barrier_semaphore()

    def ahead(step_e, step_z):
        return lax.rem(expert + step_e, experts), lax.rem(donor + step_z, donors)

    for step_e, step_z in order:
        to_e, to_z = ahead(step_e, step_z)
        pl.semaphore_signal(
            barrier, inc=1, device_id={"expert": to_e, "donor": to_z}, device_id_type=MESH
        )
    mine = expert * donors + donor
    pages, page_len = table_ref.shape[1], pages_in.shape[1]
    slots = seqs
    for seq in range(seqs):
        held = 0
        for index in range(pages):
            named = table_ref[seq, index]
            held = held + jnp.where(named // slots == mine, named % slots, 0)
        for group in range(kv_heads):
            out_buf[seq, group] = pool_ref[held, group]
    lane = lax.broadcasted_iota(jnp.int32, (1, pages * page_len), 1)
    holder = lane // page_len
    first = jnp.zeros_like(lane)
    for index in range(pages):
        first = jnp.where(holder == table_ref[expert, index] // slots, index * page_len, first)
    seen = first + lane % page_len < length_ref[expert]
    bias = jnp.where(seen, 0.0, -jnp.inf)
    pl.semaphore_wait(barrier, experts * donors - 1)

    def page(step_e, step_z):
        to_e, to_z = ahead(step_e, step_z)
        return send(
            out_buf.at[to_e, to_z * kv_heads // donors],
            pages_in.at[mine],
            sends,
            recvs,
            step_e * donors + step_z,
            expert=to_e,
            donor=to_z,
        )

    for step_e, step_z in order:
        page(step_e, step_z).start()
    pages_in[mine] = out_buf[expert, donor * kv_heads // donors]
    for group in range(kv_heads):

        @pl.when(donor * kv_heads // donors == group)
        def _():
            fresh_ref[...] = suffix_ref[:, group, :]

    for step_e, step_z in order:
        from_e, from_z = ahead(experts - step_e, donors - step_z)
        send(
            out_buf.at[expert, donor * kv_heads // donors],
            pages_in.at[from_e * donors + from_z],
            sends,
            recvs,
            step_e * donors + step_z,
            expert=from_e,
            donor=from_z,
        ).wait_recv()
    keys_count = pages_in.shape[0] * pages_in.shape[1]
    causal = lax.broadcasted_iota(jnp.int32, (suffix, suffix), 0) >= lax.broadcasted_iota(
        jnp.int32, (suffix, suffix), 1
    )
    scale = head_dim ** (-0.5)
    both = (((1,), (1,)), ((), ()))
    for left in range(0, columns, head_dim):
        query = query_ref[:, left : left + head_dim]
        old_keys = pages_in[:, :, :head_dim].reshape(keys_count, head_dim)
        old = lax.dot_general(query, old_keys, both, preferred_element_type=jnp.float32)
        new = lax.dot_general(
            query, fresh_ref[:, :head_dim], both, preferred_element_type=jnp.float32
        )
        old = old * scale + bias
        new = jnp.where(causal, new * scale, -jnp.inf)
        top = jnp.maximum(
            jnp.max(old, axis=1, keepdims=True), jnp.max(new, axis=1, keepdims=True)
        )
        old = jnp.exp(old - top)
        new = jnp.exp(new - top)
        total = jnp.sum(old, axis=1, keepdims=True) + jnp.sum(new, axis=1, keepdims=True)
        old_vals = pages_in[:, :, head_dim:].reshape(keys_count, head_dim)
        mixed = jnp.dot(old.astype(query.dtype), old_vals, preferred_element_type=jnp.float32)
        mixed = mixed + jnp.dot(
            new.astype(query.dtype), fresh_ref[:, head_dim:], preferred_element_type=jnp.float32
        )
        head_ref[:, left : left + head_dim] = (mixed / total).astype(head_ref.dtype)
    for step_e, step_z in order:
        page(step_e, step_z).wait_send()


def page_heads(pool, table, lengths, queries, suffix_kv, experts, donors):
    seqs, kv_heads, page_len, both = pool.shape
    dma = pltpu.SemaphoreType.DMA
    inside = pl.BlockSpec(memory_space=pltpu.VMEM)
    return pl.pallas_call(
        functools.partial(page_kernel, experts, donors),
        out_shape=jax.ShapeDtypeStruct(queries.shape, queries.dtype),
        in_specs=[inside] + [pl.BlockSpec(memory_space=pltpu.SMEM)] * 2 + [inside] * 2,
        out_specs=inside,
        scratch_shapes=[
            pltpu.VMEM((queries.shape[0], both), pool.dtype),
            pltpu.VMEM((seqs, kv_heads, page_len, both), pool.dtype),
            pltpu.VMEM((experts * donors, page_len, both), pool.dtype),
            dma((experts * donors,)),
            dma((experts * donors,)),
        ],
        compiler_params=pltpu.CompilerParams(collective_id=4, has_side_effects=True),
        name="page_heads",
    )(pool, table, lengths, queries, suffix_kv)


def relay_steps(suffix, chips, donors, piece):
    before_mix = 2 * suffix // piece + LAG + HOP * (donors // 2)
    return min(16, 1 << (before_mix.bit_length() - 1))


def mix_scratch(heads, out_weight, w_gate_up, chips, donors, piece):
    suffix, head_cols = heads.shape
    blocks = 2 * chips
    width = out_weight.shape[1]
    model_width, ff_local = w_gate_up.shape[1], w_gate_up.shape[3]
    tokens = blocks * suffix
    columns = model_width // donors
    count = tokens // piece
    kind = heads.dtype
    vmem = lambda *shape: pltpu.VMEM(shape, kind)
    wide = lambda *shape: pltpu.VMEM(shape, jnp.float32)
    held = lambda number: pltpu.VMEM((number, suffix, columns), kind)
    return [
        vmem(blocks // donors, suffix, width),
        wide(blocks, 8, suffix),
        wide(blocks, 8, suffix),
        wide(model_width // 128, 128),
        vmem(head_cols, width),
        vmem(3, model_width // relay_steps(suffix, chips, donors, piece), 2, ff_local),
        vmem(ff_local, model_width),
        vmem(tokens, head_cols),
        wide(tokens, width),
        vmem(count, piece, width),
        vmem(count, piece, width),
        vmem(count, piece, width),
        vmem(count, piece, width),
        vmem(blocks, tokens, width),
        vmem(model_width, 2 * ff_local),
        vmem(2 * suffix, width),
        wide(tokens, 2 * ff_local),
        wide(tokens, 128),
        vmem(tokens, ff_local),
        wide(2 * suffix, 1),
        vmem(chips * donors, 2 * suffix, columns),
        held(chips * donors),
        held((chips - 1) * donors),
        held((chips - 1) * donors),
        held(donors),
        held(donors),
        held(donors),
        held(donors),
    ]


def mix_blocks(
    heads, gain, probs, ids, hidden, out_weight, w_gate_up, w_down, chips, donors, piece, scratch
):
    suffix = heads.shape[0]
    columns = w_gate_up.shape[1] // donors
    count = 2 * chips * suffix // piece
    dma = pltpu.SemaphoreType.DMA
    pair = lambda number: [dma((number,)), dma((number,))]
    inside = pl.BlockSpec(memory_space=pltpu.VMEM)
    outside = pl.BlockSpec(memory_space=pl.ANY)
    return pl.pallas_call(
        functools.partial(mix_kernel, chips, donors, piece),
        out_shape=jax.ShapeDtypeStruct((suffix, columns), heads.dtype),
        in_specs=[inside] * 4 + [outside] * 4,
        out_specs=inside,
        scratch_shapes=scratch
        + [dma((3,)), dma((relay_steps(suffix, chips, donors, piece),))]
        + pair(2 * chips - 1)
        + pair(2 * chips // donors)
        + pair(chips - 1)
        + pair(chips)
        + pair(count)
        + pair(count)
        + pair((chips - 1) * count)
        + pair(chips * count)
        + pair(chips * donors)
        + pair((chips - 1) * donors)
        + pair(donors)
        + pair(donors),
        compiler_params=pltpu.CompilerParams(
            collective_id=3, has_side_effects=True, vmem_limit_bytes=VMEM_BYTES
        ),
        name="mix_blocks",
    )(heads, gain, probs, ids, hidden, out_weight, w_gate_up, w_down)


def shards(
    hidden_in,
    queries,
    suffix_kv,
    kv_pool,
    page_table,
    prefix_len,
    out_weight,
    norm_gain,
    expert_ids,
    route_probs,
    w_gate_up,
    w_down,
):
    n_expert = lax.axis_size("expert")
    n_donor = lax.axis_size("donor")
    expert_index = lax.axis_index("expert")
    donor_index = lax.axis_index("donor")
    share_count = n_donor // 2
    seq_count, page_count = page_table.shape
    suffix_len = queries.shape[0]
    kv_heads = suffix_kv.shape[1]
    head_dim = suffix_kv.shape[2] // 2
    page_len = kv_pool.shape[2]
    model_width = hidden_in.shape[1]
    columns = model_width // n_donor
    experts_all = 2 * n_expert
    ff_local = w_gate_up.shape[3]
    my_group = donor_index * kv_heads // n_donor
    owner_index = expert_index * n_donor + donor_index
    owner_of = page_table // seq_count
    held_slot = jnp.sum(jnp.where(owner_of == owner_index, page_table % seq_count, 0), axis=1)
    chips = n_expert // 2
    scratch = mix_scratch(queries, out_weight, w_gate_up, chips, n_donor, PIECE)
    held_bytes = sum(math.prod(item.shape) * item.dtype.itemsize for item in scratch)
    if held_bytes <= VMEM_BYTES - 4 * 1024 * 1024:
        head_out = page_heads(
            kv_pool, page_table, prefix_len, queries, suffix_kv, n_expert, n_donor
        )
        layer_out = mix_blocks(
            head_out,
            norm_gain.reshape(-1, 128),
            route_probs.T,
            expert_ids.T,
            hidden_in,
            out_weight,
            w_gate_up,
            w_down,
            chips,
            n_donor,
            PIECE,
            scratch,
        )
        return (layer_out, head_out)

    dest_group = jnp.arange(n_donor, dtype=jnp.int32) * kv_heads // n_donor
    wanted = (held_slot[:, None] * kv_heads + dest_group[None, :]).reshape(-1)
    outgoing = jnp.take(
        kv_pool.reshape(seq_count * kv_heads, page_len, 2 * head_dim), wanted, axis=0
    )
    arrived = lax.all_to_all(outgoing, ("expert", "donor"), split_axis=0, concat_axis=0, tiled=True)
    my_owners = lax.dynamic_index_in_dim(owner_of, expert_index, 0, keepdims=False)
    ordered = jnp.take(arrived, my_owners, axis=0).reshape(page_count * page_len, 2 * head_dim)
    prefix_keys = ordered[:, :head_dim]
    prefix_vals = ordered[:, head_dim:]
    score_scale = head_dim ** (-0.5)
    query_heads = queries.reshape(suffix_len, -1, head_dim)
    fresh_pair = lax.dynamic_index_in_dim(suffix_kv, my_group, 1, keepdims=False)
    causal = jnp.arange(suffix_len)[:, None] >= jnp.arange(suffix_len)[None, :]
    fresh_scores = (
        jnp.einsum(
            "thc,uc->thu", query_heads, fresh_pair[:, :head_dim], preferred_element_type=jnp.float32
        )
        * score_scale
    )
    fresh_scores = jnp.where(causal[:, None, :], fresh_scores, -jnp.inf)
    prefix_tokens = lax.dynamic_index_in_dim(prefix_len, expert_index, 0, keepdims=False)
    block_keys = min(1024, page_count * page_len)
    live_blocks = (prefix_tokens + block_keys - 1) // block_keys

    def block_scores(block_index):
        keys_block = lax.dynamic_slice_in_dim(prefix_keys, block_index * block_keys, block_keys, 0)
        raw_scores = (
            jnp.einsum("thc,kc->thk", query_heads, keys_block, preferred_element_type=jnp.float32)
            * score_scale
        )
        visible = block_index * block_keys + jnp.arange(block_keys) < prefix_tokens
        return jnp.where(visible[None, None, :], raw_scores, -jnp.inf)

    def raise_max(block_index, running):
        return jnp.maximum(running, jnp.max(block_scores(block_index), axis=2))

    row_max = lax.fori_loop(0, live_blocks, raise_max, jnp.max(fresh_scores, axis=2))

    def add_block(block_index, loop_state):
        row_total, weighted = loop_state
        exp_scores = jnp.exp(block_scores(block_index) - row_max[:, :, None])
        vals_block = lax.dynamic_slice_in_dim(prefix_vals, block_index * block_keys, block_keys, 0)
        weighted = weighted + jnp.einsum(
            "thk,kc->thc",
            exp_scores.astype(jnp.bfloat16),
            vals_block,
            preferred_element_type=jnp.float32,
        )
        return (row_total + jnp.sum(exp_scores, axis=2), weighted)

    fresh_exp = jnp.exp(fresh_scores - row_max[:, :, None])
    start_state = (
        jnp.sum(fresh_exp, axis=2),
        jnp.einsum(
            "thu,uc->thc",
            fresh_exp.astype(jnp.bfloat16),
            fresh_pair[:, head_dim:],
            preferred_element_type=jnp.float32,
        ),
    )
    row_total, weighted = lax.fori_loop(0, live_blocks, add_block, start_state)
    head_out = (weighted / row_total[:, :, None]).astype(jnp.bfloat16).reshape(suffix_len, -1)
    gate_weights = route_probs / jnp.sum(route_probs, axis=1, keepdims=True)
    chosen = expert_ids[:, :, None] == jnp.arange(experts_all, dtype=jnp.int32)
    gate_table = jnp.sum(jnp.where(chosen, gate_weights[:, :, None], 0.0), axis=1)
    gate_tables = [gate_table]
    for step in range(1, n_expert):
        pairs = [(source, (source + step) % n_expert) for source in range(n_expert)]
        gate_tables.append(lax.ppermute(gate_table, "expert", pairs))
    from_order = lax.rem(expert_index - jnp.arange(n_expert) + n_expert, n_expert)
    gate_all = jnp.stack(gate_tables)[from_order].reshape(n_expert * suffix_len, experts_all)
    my_expert = owner_index // share_count
    my_gates = lax.dynamic_slice_in_dim(gate_all, my_expert, 1, 1)

    seqs_each = n_expert // n_donor
    width = model_width // n_expert
    hidden_parts = []
    for shift in range(seqs_each):
        pairs = []
        for source in range(n_expert * n_donor):
            seq, part = source // n_donor, source % n_donor
            target = part * seqs_each + (seq + shift) % seqs_each
            pairs.append((source, target * n_donor + seq // seqs_each))
        target = donor_index * seqs_each + lax.rem(expert_index + shift, seqs_each)
        sent = lax.dynamic_slice_in_dim(hidden_in, target * width, width, 1)
        hidden_parts.append(lax.ppermute(sent, ("expert", "donor"), pairs))
    turned = lax.rem(expert_index - jnp.arange(seqs_each) + seqs_each * n_expert, seqs_each)
    hidden_block = jnp.stack(hidden_parts)[turned].reshape(seqs_each * suffix_len, width)

    heads_all = lax.all_gather(head_out, "expert", axis=0, tiled=True)
    w_in, heads_all = lax.optimization_barrier(
        (w_gate_up[0].reshape(model_width, 2 * ff_local), heads_all)
    )
    resid = gather_blocks(heads_all, out_weight, hidden_block, n_expert // 2, n_donor)
    resid_f = resid.astype(jnp.float32)
    inverse = lax.rsqrt(jnp.mean(resid_f * resid_f, axis=1, keepdims=True) + 1e-06)
    normed = (resid_f * inverse * norm_gain.astype(jnp.float32)).astype(jnp.bfloat16)
    gate_up = jnp.dot(
        normed,
        w_in,
        preferred_element_type=jnp.float32,
    )
    activated = (
        jax.nn.silu(gate_up[:, :ff_local]) * gate_up[:, ff_local:] * my_gates
    ).astype(jnp.bfloat16)
    expert_mix = reduce_blocks(activated, w_down[0], n_expert // 2, n_donor)
    resid_mine = lax.dynamic_slice(
        resid,
        (expert_index * suffix_len, donor_index * columns),
        (suffix_len, columns),
    )
    layer_out = (resid_mine.astype(jnp.float32) + expert_mix).astype(
        jnp.bfloat16
    )
    return (layer_out, head_out)


def solution(mesh):
    in_specs = (
        P(("groups", "expert"), None),
        P(("groups", "expert"), "donor"),
        P(("groups", "expert"), None, None),
        P(("groups", "expert", "donor"), None, None, None),
        P("groups", None),
        P("groups"),
        P("donor", "expert"),
        P(),
        P(("groups", "expert"), None),
        P(("groups", "expert"), None),
        P(("expert", "donor"), None, None, None),
        P(("expert", "donor"), None, None),
    )
    out_specs = (P(("groups", "expert"), "donor"), P(("groups", "expert"), "donor"))
    return jax.shard_map(shards, mesh=mesh, in_specs=in_specs, out_specs=out_specs, check_vma=False)
```
